32 devices in a mesh: groups: 2 (over y), rows: 8 (over z, x), sub: 2 (over core).
Axes of the slice: x: 2, y: 2, z: 4, core: 2. Of those that a mesh axis runs over, the one named last changes fastest.
Arguments:
- coupling: bfloat16 [131072, 128], P(('groups', 'rows', 'sub')), parts along dimension 0, may hold values from 0.009 to 110
- tile_vals: bfloat16 [1024, 6, 128, 128], P(('groups', 'rows', 'sub')), parts along dimension 0, may hold values from -0.02734375 to 0.02734375
- tile_cols: int32 [1024, 6], P(('groups', 'rows', 'sub')), parts along dimension 0, may hold values from 0 to 511, as said below
- cluster_graph: int32 [256, 128], P('groups'), parts along dimension 0, may hold values from 0 to 3
- cluster_mass: float32 [256], P('groups'), parts along dimension 0, may hold values from 0.25 to 4
Outputs:
- log_coupling: float32 [131072, 128], P(('groups', 'rows', 'sub')), parts along dimension 0
The draws below stay inside these ranges and needn't reach their ends.
There are 2 independent parts, one for each index of `groups`. The reference program is written for one: setup_inputs(seed, part) draws one part's arguments, and reference() takes and returns one part's arrays. A program takes and returns all parts, laid end to end along the dimension named above; each array names one. Nothing has to cross between parts.
Inputs may be any that keep to these rules, and one draw needn't show every extreme that they name: `tile_cols`: within each device's rows of 32 block rows, a slot below 4 names a column block held by the same device or by the device just before or after it along rows+sub. Over the slots from 4 on, the block rows of one device name column blocks held by any one device at most 4 times, and some device exactly 4 times.
All inputs are finite; a program needn't handle non-finite values.
Results may differ from the reference program's by a relative error of at most 0.0003.
Values may be sent and summed in bfloat16 or wider, within the bound.
No kernel may reach another device: no remote copies, remote signals or barrier semaphores. Data moves between devices by JAX's collectives and lax.ppermute only.
A program may use at most 128 MiB of HBM per device.

```python
import math
import jax
import jax.numpy as jnp
from jax import lax

K = 128
BLK = 128
SLOTS = 6
NEAR = 4
FAR = 2
NB = 32
SHARDS = 16
NBLK = 512
NODES = 65536


def draw_tile_cols(key, part):
    key_near = jax.random.fold_in(key, 11)
    key_owner = jax.random.fold_in(key, 12)
    key_order = jax.random.fold_in(key, 13)
    key_local = jax.random.fold_in(key, 14)
    block_ids = jnp.arange(NBLK, dtype=jnp.int32)
    home_block = block_ids // NB * NB
    near_cols = home_block[:, None] - NB + jax.random.randint(key_near, (NBLK, NEAR), 0, 3 * NB)
    near_cols = jnp.clip(near_cols, 0, NBLK - 1)
    far_count = NB * FAR
    owners = jax.random.permutation(key_owner, SHARDS).astype(jnp.int32)
    listed = owners[jnp.arange(far_count, dtype=jnp.int32) % SHARDS]
    order_keys = jax.random.split(key_order, SHARDS)
    orders = jax.vmap(lambda one_key: jax.random.permutation(one_key, far_count))(order_keys)
    far_owner = listed[orders]
    far_cols = far_owner * NB + jax.random.randint(key_local, (SHARDS, far_count), 0, NB)
    far_cols = far_cols.reshape(NBLK, FAR)
    return jnp.concatenate([near_cols, far_cols], axis=1).astype(jnp.int32)


def draw_coupling(key, part):
    key_rough = jax.random.fold_in(key, 21)
    key_slope = jax.random.fold_in(key, 22)
    rough = jnp.clip(0.8 * jax.random.normal(key_rough, (NODES, K), jnp.float32), -2.4, 2.4)
    slope = jax.random.uniform(key_slope, (K,), jnp.float32, -2.2, 2.2)
    place = jnp.arange(NODES, dtype=jnp.float32) / NODES - 0.5
    return jnp.exp(rough + 2.0 * place[:, None] * slope[None, :]).astype(jnp.bfloat16)


def with_ends(drawn, key, least, high):
    dims = drawn.shape
    spot = [jax.random.randint(jax.random.fold_in(key, axis), (), 0, dims[axis]) for axis in range(len(dims))]
    drawn = drawn.at[tuple(spot)].set(least)
    longest = dims.index(max(dims))
    spot[longest] = (spot[longest] + 1) % dims[longest]
    return drawn.at[tuple(spot)].set(high)


def shard_levels(own_key, shape, cuts, least, top_value):
    loudness, own = 1.0, jax.random.fold_in(own_key, 6)
    for dim, blocks in cuts:
        heights = jnp.exp(jax.random.uniform(jax.random.fold_in(own, dim), (blocks,), jnp.float32, least / len(cuts), top_value / len(cuts)))
        loudness = loudness * jnp.repeat(heights, shape[dim] // blocks).reshape([-1 if axis == dim else 1 for axis in range(len(shape))])
    return loudness


def gaussian(rng, extent, width, limit, shards=(), held_as=jnp.bfloat16):
    values = width * jax.random.normal(rng, extent, jnp.float32)
    if shards:
        values = values * shard_levels(rng, extent, shards, -0.22, 0.18)
    return jnp.clip(values, -limit, limit).astype(held_as)


def setup_inputs(seed: int = 0, part: int = 0) -> dict:
    splits = jax.random.split(jax.random.key(seed), 6)
    own_keys = jax.random.split(jax.random.fold_in(splits[5], part), 6)
    coupling = draw_coupling(jax.random.fold_in(jax.random.fold_in(splits[5], part), 71), part)
    tile_vals = gaussian(own_keys[1], (NBLK, SLOTS, BLK, BLK), (64 * BLK * SLOTS) ** -0.5, 0.02734375, ((0, 16),))
    tile_cols = draw_tile_cols(jax.random.fold_in(jax.random.fold_in(splits[5], part), 71), part)
    cluster_graph = with_ends(jax.random.randint(own_keys[3], (K, K), 0, 4), jax.random.fold_in(own_keys[3], 1), 0, 3).astype(jnp.int32)
    cluster_mass = jnp.clip(jnp.exp(jax.random.uniform(own_keys[4], (K,), jnp.float32, math.log(0.25), math.log(4.0))), 0.25, 4.0)
    return {"coupling": coupling, "tile_vals": tile_vals, "tile_cols": tile_cols, "cluster_graph": cluster_graph, "cluster_mass": cluster_mass}


eta_step = 2.0
relax_power = 0.5


def reference(coupling, tile_vals, tile_cols, cluster_graph, cluster_mass):
    blocks = coupling.reshape(NBLK, BLK, K).astype(jnp.float32)
    spread = jnp.zeros((NBLK, BLK, K), jnp.float32)
    for slot_id in range(SLOTS):
        picked = jnp.take(blocks, tile_cols[:, slot_id].astype(jnp.int32), axis=0)
        spread = spread + jnp.einsum("nij,njk->nik", tile_vals[:, slot_id].astype(jnp.float32), picked, precision=lax.Precision.HIGHEST)
    spread = spread.reshape(NODES, K)
    graph = cluster_graph.astype(jnp.float32)
    affinity = jnp.dot(spread, graph.T / K, precision=lax.Precision.HIGHEST)
    whole = coupling.astype(jnp.float32)
    colmass = jnp.sum(whole, axis=0) / NODES
    pull = jnp.dot(graph * graph, colmass, precision=lax.Precision.HIGHEST) / K
    logits = jnp.log(whole) - eta_step * (pull[None, :] - 2.0 * affinity)
    newmass = jnp.sum(jnp.exp(logits), axis=0) / NODES
    shifted = logits + relax_power * (jnp.log(cluster_mass) - jnp.log(newmass))[None, :]
    return shifted - jnp.log(jnp.sum(jnp.exp(shifted), axis=1, keepdims=True))
```

```python
import functools

import jax
import jax.numpy as jnp
from jax import lax
from jax.experimental import pallas as pl
from jax.experimental.pallas import tpu as pltpu
from jax.sharding import PartitionSpec as P

NEAR = 4
NODES = ("rows", "sub")

eta_step = 2.0
relax_power = 0.5

ANY = pl.BlockSpec(memory_space=pl.ANY)
VMEM = pl.BlockSpec(memory_space=pltpu.VMEM)
SMEM = pl.BlockSpec(memory_space=pltpu.SMEM)


def requests_kernel(cap, nodes_total, cols_ref, coupling_ref, out_ref):
    blocks_dev, slots = cols_ref.shape
    shards = out_ref.shape[0]
    clusters = coupling_ref.shape[1]
    owner = lax.broadcasted_iota(jnp.int32, (blocks_dev, shards), 1)
    place = lax.broadcasted_iota(jnp.int32, (blocks_dev, clusters), 1).astype(jnp.float32)
    before = (
        lax.broadcasted_iota(jnp.int32, (blocks_dev, blocks_dev), 1)
        < lax.broadcasted_iota(jnp.int32, (blocks_dev, blocks_dev), 0)
    ).astype(jnp.float32)
    count = jnp.zeros((1, shards), jnp.float32)
    table = jnp.zeros((shards, clusters), jnp.float32)
    for slot_id in range(NEAR, slots):
        local = cols_ref[:, slot_id : slot_id + 1] - owner * blocks_dev
        hit = (local >= 0) & (local < blocks_dev)
        hits = hit.astype(jnp.float32)
        earlier = jnp.dot(before, hits, preferred_element_type=jnp.float32) + count
        rank = jnp.sum(earlier * hits, axis=1, keepdims=True)
        count = count + jnp.sum(hits, axis=0, keepdims=True)
        wanted = jnp.where(hit, local, 0).astype(jnp.float32)
        table = table + lax.dot_general(
            wanted,
            (rank == place).astype(jnp.float32),
            (((0,), (0,)), ((), ())),
            precision=lax.Precision.HIGHEST,
            preferred_element_type=jnp.float32,
        )
    rows = coupling_ref.shape[0]
    step = rows // 8

    def add(i, total):
        part = coupling_ref[pl.ds(pl.multiple_of(i * step, step), step), :].astype(jnp.float32)
        return total + jnp.sum(part.reshape(step // 8, 8, clusters), axis=0)

    total = lax.fori_loop(0, 8, add, jnp.zeros((8, clusters), jnp.float32))
    mass = jnp.sum(total, axis=0, keepdims=True) / nodes_total
    out_ref[:, :clusters] = jnp.broadcast_to(mass, (shards, clusters))
    out_ref[:, clusters:] = table


def gather_kernel(wanted_ref, blocks_ref, out_ref, sem):
    count = out_ref.shape[0]

    @pl.loop(0, count)
    def _(n):
        pltpu.make_async_copy(blocks_ref.at[wanted_ref[n]], out_ref.at[n], sem).start()

    pltpu.make_async_copy(out_ref, out_ref, sem).wait()


def split(x):
    high = x.astype(jnp.bfloat16)
    return jnp.concatenate([high, (x - high.astype(jnp.float32)).astype(jnp.bfloat16)], axis=1)


def near_kernel(
    group, cap, cols_ref, base_ref, left_ref, own_ref, right_ref, tiles_ref, rows_ref, graph_ref, mass_ref,
    part_ref, graph2_ref, where_ref, window, pull_ref, count_ref, sems,
):
    step = pl.program_id(0)
    blocks_dev, tile, clusters = own_ref.shape
    slots = cols_ref.shape[0] // blocks_dev

    @pl.when(step == 0)
    def _():
        copies = [
            pltpu.make_async_copy(src, window.at[pl.ds(i * blocks_dev, blocks_dev)], sems.at[i])
            for i, src in enumerate((left_ref, own_ref, right_ref))
        ]
        for copy in copies:
            copy.start()
        graph = graph_ref[...].astype(jnp.float32)
        colmass = jnp.sum(mass_ref[:, :clusters], axis=0, keepdims=True)
        pull_ref[...] = (
            lax.dot_general(
                jnp.broadcast_to(colmass, (8, clusters)),
                graph * graph,
                (((1,), (1,)), ((), ())),
                precision=lax.Precision.HIGHEST,
                preferred_element_type=jnp.float32,
            )
            / clusters
        )
        turned = graph.T.astype(jnp.bfloat16)
        graph2_ref[:clusters, :] = turned
        graph2_ref[clusters:, :] = turned

        shards = mass_ref.shape[0]

        @pl.loop(0, shards)
        def _(o):
            count_ref[o] = 0

        @pl.loop(0, blocks_dev)
        def _(b):
            pass

        for slot_id in range(NEAR, slots):

            @pl.loop(0, blocks_dev)
            def _(b):
                owner = cols_ref[b * slots + slot_id] // blocks_dev
                rank = count_ref[owner]
                count_ref[owner] = rank + 1
                where_ref[b * (slots - NEAR) + slot_id - NEAR] = owner * cap + rank

        for copy in copies:
            copy.wait()

    scale = 2.0 * eta_step / clusters
    for i in range(group):
        b = step * group + i
        picked = [window[cols_ref[b * slots + s] - base_ref[0]] for s in range(NEAR)]
        tiles = jnp.concatenate([tiles_ref[i, s] for s in range(NEAR)], axis=1)
        spread = jnp.dot(tiles, jnp.concatenate(picked, axis=0), preferred_element_type=jnp.float32)
        affinity = jnp.dot(split(spread), graph2_ref[...], preferred_element_type=jnp.float32)
        here = pl.ds(i * tile, tile)
        part_ref[here, :] = (
            jnp.log(rows_ref[here, :].astype(jnp.float32)) - eta_step * pull_ref[0:1, :] + scale * affinity
        )


def far_kernel(group, nodes_total, where_ref, blocks_ref, tiles_ref, part_ref, graph2_ref, logits_ref, mass_ref, total):
    step = pl.program_id(0)
    far_slots, tile, clusters = tiles_ref.shape[1:]

    @pl.when(step == 0)
    def _():
        total[...] = jnp.zeros_like(total)

    scale = 2.0 * eta_step / clusters
    for i in range(group):
        n = (step * group + i) * far_slots
        picked = [blocks_ref[where_ref[n + s]] for s in range(far_slots)]
        tiles = jnp.concatenate([tiles_ref[i, s] for s in range(far_slots)], axis=1)
        spread = jnp.dot(tiles, jnp.concatenate(picked, axis=0), preferred_element_type=jnp.float32)
        affinity = jnp.dot(split(spread), graph2_ref[...], preferred_element_type=jnp.float32)
        here = pl.ds(i * tile, tile)
        logits = part_ref[here, :] + scale * affinity
        logits_ref[here, :] = logits
        total[...] += jnp.sum(jnp.exp(logits).reshape(tile // 8, 8, clusters), axis=0)

    @pl.when(step == pl.num_programs(0) - 1)
    def _():
        mass_ref[...] = jnp.sum(total[...], axis=0, keepdims=True) / nodes_total


def last_kernel(logits_ref, newmass_ref, target_ref, out_ref):
    shift = relax_power * (jnp.log(target_ref[...]) - jnp.log(newmass_ref[...]))
    shifted = logits_ref[...] + shift
    out_ref[...] = shifted - jnp.log(jnp.sum(jnp.exp(shifted), axis=1, keepdims=True))


def local(coupling, tile_vals, tile_cols, cluster_graph, cluster_mass):
    shards = lax.axis_size(NODES)
    my_index = lax.axis_index(NODES)
    blocks_dev, slots = tile_cols.shape
    tile = tile_vals.shape[2]
    rows, clusters = coupling.shape
    far_slots = slots - NEAR
    nodes_total = rows * shards
    far_count = blocks_dev * far_slots
    cap = (far_count + shards - 1) // shards
    blocks = coupling.reshape(blocks_dev, tile, clusters)
    f32, bf16, i32 = jnp.float32, jnp.bfloat16, jnp.int32
    group = 4
    steps = blocks_dev // group

    ends = shards - 1
    left = lax.ppermute(blocks, NODES, [(i, i + 1) for i in range(ends)])
    right = lax.ppermute(blocks, NODES, [(i + 1, i) for i in range(ends)])

    asked = pl.pallas_call(
        functools.partial(requests_kernel, cap, nodes_total),
        out_shape=jax.ShapeDtypeStruct((shards, 2 * clusters), f32),
        in_specs=[VMEM, VMEM],
        out_specs=VMEM,
        name="requests",
    )(tile_cols, coupling)
    heard = lax.all_to_all(
        asked.reshape(shards, 1, 2 * clusters), NODES, split_axis=0, concat_axis=0, tiled=True
    ).reshape(shards, 2 * clusters)
    wanted = heard[:, clusters : clusters + cap].astype(i32).reshape(shards * cap)
    found = pl.pallas_call(
        gather_kernel,
        out_shape=jax.ShapeDtypeStruct((shards * cap, tile, clusters), bf16),
        in_specs=[SMEM, VMEM],
        out_specs=ANY,
        scratch_shapes=[pltpu.SemaphoreType.DMA],
        name="gather",
    )(wanted, blocks)
    fetched = lax.all_to_all(
        found.reshape(shards, cap, tile, clusters), NODES, split_axis=0, concat_axis=0, tiled=True
    ).reshape(shards * cap, tile, clusters)

    base = (my_index * blocks_dev - blocks_dev).astype(i32).reshape(1)
    flops = 2 * rows * clusters
    part, graph2, where = pl.pallas_call(
        functools.partial(near_kernel, group, cap),
        grid=(steps,),
        out_shape=(
            jax.ShapeDtypeStruct((rows, clusters), f32),
            jax.ShapeDtypeStruct((2 * clusters, clusters), bf16),
            jax.ShapeDtypeStruct((far_count,), i32),
        ),
        in_specs=[
            SMEM, SMEM, ANY, ANY, ANY,
            pl.BlockSpec((group, NEAR, tile, tile), lambda i: (i, 0, 0, 0)),
            pl.BlockSpec((group * tile, clusters), lambda i: (i, 0)),
            VMEM, VMEM,
        ],
        out_specs=(pl.BlockSpec((group * tile, clusters), lambda i: (i, 0)), VMEM, SMEM),
        scratch_shapes=[
            pltpu.VMEM((3 * blocks_dev, tile, clusters), bf16),
            pltpu.VMEM((8, clusters), f32),
            pltpu.SMEM((shards,), i32),
            pltpu.SemaphoreType.DMA((3,)),
        ],
        cost_estimate=pl.CostEstimate(
            flops=flops * (NEAR * tile + 2 * clusters), bytes_accessed=16 << 20, transcendentals=rows * clusters
        ),
        name="near",
    )(tile_cols.reshape(-1), base, left, blocks, right, tile_vals, coupling, cluster_graph, heard)

    logits, mass_part = pl.pallas_call(
        functools.partial(far_kernel, group, nodes_total),
        grid=(steps,),
        out_shape=(
            jax.ShapeDtypeStruct((rows, clusters), f32),
            jax.ShapeDtypeStruct((1, clusters), f32),
        ),
        in_specs=[
            SMEM, VMEM,
            pl.BlockSpec((group, far_slots, tile, tile), lambda i: (i, NEAR // far_slots, 0, 0)),
            pl.BlockSpec((group * tile, clusters), lambda i: (i, 0)),
            VMEM,
        ],
        out_specs=(pl.BlockSpec((group * tile, clusters), lambda i: (i, 0)), VMEM),
        scratch_shapes=[pltpu.VMEM((8, clusters), f32)],
        cost_estimate=pl.CostEstimate(
            flops=flops * (far_slots * tile + 2 * clusters), bytes_accessed=8 << 20, transcendentals=rows * clusters
        ),
        name="far",
    )(where, fetched, tile_vals, part, graph2)

    newmass = mass_part
    span = 1
    while span < shards:
        newmass = newmass + lax.ppermute(newmass, NODES, [(i, i ^ span) for i in range(shards)])
        span *= 2

    return pl.pallas_call(
        last_kernel,
        grid=(steps,),
        out_shape=jax.ShapeDtypeStruct((rows, clusters), f32),
        in_specs=[pl.BlockSpec((group * tile, clusters), lambda i: (i, 0)), VMEM, VMEM],
        out_specs=pl.BlockSpec((group * tile, clusters), lambda i: (i, 0)),
        name="last",
    )(logits, newmass, cluster_mass.reshape(1, clusters))


def solution(mesh):
    return jax.shard_map(
        local,
        mesh=mesh,
        in_specs=(
            P(("groups", "rows", "sub"), None),
            P(("groups", "rows", "sub"), None, None, None),
            P(("groups", "rows", "sub"), None),
            P("groups", None),
            P("groups"),
        ),
        out_specs=P(("groups", "rows", "sub"), None),
        check_vma=False,
    )
```

```python
import functools

import jax
import jax.numpy as jnp
from jax import lax
from jax.experimental import pallas as pl
from jax.experimental.pallas import tpu as pltpu
from jax.sharding import PartitionSpec as P


NEAR = 4
NODES = ("rows", "sub")

eta_step = 2.0
relax_power = 0.5

ANY = pl.BlockSpec(memory_space=pl.ANY)
VMEM = pl.BlockSpec(memory_space=pltpu.VMEM)
SMEM = pl.BlockSpec(memory_space=pltpu.SMEM)

f32, bf16, i32 = jnp.float32, jnp.bfloat16, jnp.int32


def on_chip(x):
    return pltpu.with_memory_space_constraint(x, pltpu.VMEM)


def in_hbm(x):
    return pltpu.with_memory_space_constraint(x, pltpu.HBM)


def params(mib):
    return pltpu.CompilerParams(vmem_limit_bytes=mib << 20)


def requests_kernel(nodes_total, cols_ref, coupling_ref, out_ref, rows, sems):
    slots, blocks_dev = cols_ref.shape
    shards = out_ref.shape[0]
    nodes, clusters = coupling_ref.shape
    parts = sems.shape[0]
    step = nodes // parts
    copies = [
        pltpu.make_async_copy(coupling_ref.at[pl.ds(i * step, step)], rows.at[pl.ds(i * step, step)], sems.at[i])
        for i in range(parts)
    ]
    for copy in copies:
        copy.start()

    owner = lax.broadcasted_iota(i32, (shards, blocks_dev), 0)
    place = lax.broadcasted_iota(i32, (clusters, blocks_dev), 0).astype(f32)
    before = (
        lax.broadcasted_iota(i32, (blocks_dev, blocks_dev), 0)
        < lax.broadcasted_iota(i32, (blocks_dev, blocks_dev), 1)
    ).astype(f32)
    count = jnp.zeros((shards, 1), f32)
    table = jnp.zeros((shards, clusters), f32)
    for slot_id in range(NEAR, slots):
        local = cols_ref[slot_id : slot_id + 1, :] - owner * blocks_dev
        hit = (local >= 0) & (local < blocks_dev)
        hits = hit.astype(f32)
        earlier = jnp.dot(hits, before, preferred_element_type=f32) + count
        rank = jnp.sum(earlier * hits, axis=0, keepdims=True)
        count = count + jnp.sum(hits, axis=1, keepdims=True)
        wanted = jnp.where(hit, local, 0).astype(f32)
        table = table + lax.dot_general(
            wanted,
            (rank == place).astype(f32),
            (((1,), (1,)), ((), ())),
            precision=lax.Precision.HIGHEST,
            preferred_element_type=f32,
        )
    out_ref[:, 0, clusters:] = table
    total = jnp.zeros((8, clusters), f32)
    for i in range(parts):
        copies[i].wait()
        part = rows[pl.ds(i * step, step), :].astype(f32)
        total = total + jnp.sum(part.reshape(step // 8, 8, clusters), axis=0)
    mass = jnp.sum(total, axis=0, keepdims=True) / nodes_total
    out_ref[:, 0, :clusters] = jnp.broadcast_to(mass, (shards, clusters))


def gather_kernel(cap, heard_ref, blocks_ref, out_ref, held, wanted_ref, wanted_smem, sems):
    clusters = blocks_ref.shape[2]
    fetch = pltpu.make_async_copy(blocks_ref, held, sems.at[0])
    fetch.start()
    wanted_ref[...] = heard_ref[:, 0, clusters:].astype(i32)
    copy = pltpu.make_async_copy(wanted_ref, wanted_smem, sems.at[1])
    copy.start()
    copy.wait()
    fetch.wait()

    @pl.loop(0, heard_ref.shape[0])
    def _(n):
        for j in range(cap):
            pltpu.make_async_copy(held.at[wanted_smem[n, j]], out_ref.at[n * cap + j], sems.at[2]).start()

    pltpu.make_async_copy(out_ref, out_ref, sems.at[2]).wait()


def split(x):
    high = x.astype(bf16)
    return jnp.concatenate([high, (x - high.astype(f32)).astype(bf16)], axis=1)


def near_kernel(
    group, cap, cols_ref, base_ref, left_ref, own_ref, right_ref, tiles_ref, graph_ref, mass_ref,
    part_ref, graph2_ref, where_ref, window, tiles, part, pull_ref, count_ref, sems, tile_sems, part_sems,
):
    blocks_dev, tile, clusters = own_ref.shape
    slots = tiles_ref.shape[1]
    shards = mass_ref.shape[0]
    steps = blocks_dev // group
    copies = [
        pltpu.make_async_copy(src, window.at[pl.ds(i * blocks_dev, blocks_dev)], sems.at[i])
        for i, src in enumerate((left_ref, own_ref, right_ref))
    ]
    for copy in copies:
        copy.start()

    def fetch(i):
        here = pl.ds(i * group, group)
        return pltpu.make_async_copy(tiles_ref.at[here, pl.ds(0, NEAR)], tiles.at[here], tile_sems.at[i])

    def store(i):
        here = pl.ds(pl.multiple_of(i * group * tile, group * tile), group * tile)
        return pltpu.make_async_copy(part.at[here], part_ref.at[here], part_sems.at[i])

    for i in range(steps):
        fetch(i).start()

    graph = graph_ref[...].astype(f32)
    colmass = jnp.sum(mass_ref[:, 0, :clusters], axis=0, keepdims=True)
    pull_ref[...] = (
        lax.dot_general(
            jnp.broadcast_to(colmass, (8, clusters)),
            graph * graph,
            (((1,), (1,)), ((), ())),
            precision=lax.Precision.HIGHEST,
            preferred_element_type=f32,
        )
        / clusters
    )
    turned = graph.T.astype(bf16)
    graph2_ref[:clusters, :] = turned
    graph2_ref[clusters:, :] = turned

    @pl.loop(0, shards)
    def _(o):
        count_ref[o] = 0

    for slot_id in range(NEAR, slots):

        @pl.loop(0, blocks_dev)
        def _(b):
            owner = cols_ref[slot_id, b] // blocks_dev
            rank = count_ref[owner]
            count_ref[owner] = rank + 1
            where_ref[b * (slots - NEAR) + slot_id - NEAR] = owner * cap + rank

    for copy in copies:
        copy.wait()

    scale = 2.0 * eta_step / clusters

    @pl.loop(0, steps)
    def _(step):
        fetch(step).wait()
        for i in range(group):
            b = step * group + i
            here = pl.ds(pl.multiple_of(b * tile, tile), tile)
            picked = [window[cols_ref[s, b] - base_ref[0]] for s in range(NEAR)]
            wide = jnp.concatenate([tiles[b, s] for s in range(NEAR)], axis=1)
            spread = jnp.dot(wide, jnp.concatenate(picked, axis=0), preferred_element_type=f32)
            affinity = jnp.dot(split(spread), graph2_ref[...], preferred_element_type=f32)
            part[here, :] = (
                jnp.log(window[blocks_dev + b].astype(f32)) - eta_step * pull_ref[0:1, :] + scale * affinity
            )
        store(step).start()

    @pl.loop(0, steps)
    def _(step):
        store(step).wait()


def far_kernel(
    group, nodes_total, where_ref, blocks_ref, tiles_ref, part_ref, graph2_ref,
    logits_ref, mass_ref, tiles, tile_sems, part_sems,
):
    tile, clusters = blocks_ref.shape[1:]
    blocks_dev, far_slots = tiles.shape[:2]
    steps = blocks_dev // group
    scale = 2.0 * eta_step / clusters

    def fetches(i):
        here = pl.ds(i * group, group)
        there = pl.ds(i * group * tile, group * tile)
        return (
            pltpu.make_async_copy(tiles_ref.at[here, pl.ds(NEAR, far_slots)], tiles.at[here], tile_sems.at[i]),
            pltpu.make_async_copy(part_ref.at[there], logits_ref.at[there], part_sems.at[i]),
        )

    for i in range(steps):
        for copy in fetches(i):
            copy.start()

    total = jnp.zeros((8, clusters), f32)
    for step in range(steps):
        for copy in fetches(step):
            copy.wait()
        spreads = []
        for i in range(group):
            b = step * group + i
            picked = [blocks_ref[where_ref[b * far_slots + s]] for s in range(far_slots)]
            wide = jnp.concatenate([tiles[b, s] for s in range(far_slots)], axis=1)
            spreads.append(split(jnp.dot(wide, jnp.concatenate(picked, axis=0), preferred_element_type=f32)))
        here = pl.ds(step * group * tile, group * tile)
        affinity = jnp.dot(jnp.concatenate(spreads, axis=0), graph2_ref[...], preferred_element_type=f32)
        logits = logits_ref[here, :] + scale * affinity
        logits_ref[here, :] = logits
        total = total + jnp.sum(jnp.exp(logits).reshape(group * tile // 8, 8, clusters), axis=0)

    mass_ref[...] = jnp.sum(total, axis=0, keepdims=True) / nodes_total


def last_kernel(parts, logits_ref, newmass_ref, more_ref, target_ref, out_ref, kept, sems):
    shift = relax_power * (jnp.log(target_ref[...]) - jnp.log(newmass_ref[...] + more_ref[...]))
    rows = logits_ref.shape[0]
    step = rows // parts
    copies = []
    for i in range(parts):
        here = pl.ds(i * step, step)
        shifted = logits_ref[here, :] + shift
        kept[here, :] = shifted - jnp.log(jnp.sum(jnp.exp(shifted), axis=1, keepdims=True))
        copies.append(pltpu.make_async_copy(kept.at[here], out_ref.at[here], sems.at[i]))
        copies[-1].start()
    for copy in copies:
        copy.wait()


def local(coupling, tile_vals, tile_cols, cluster_graph, cluster_mass):
    shards = lax.axis_size(NODES)
    my_index = lax.axis_index(NODES)
    blocks_dev, slots = tile_cols.shape
    tile = tile_vals.shape[2]
    rows, clusters = coupling.shape
    far_slots = slots - NEAR
    nodes_total = rows * shards
    far_count = blocks_dev * far_slots
    cap = (far_count + shards - 1) // shards
    blocks = coupling.reshape(blocks_dev, tile, clusters)
    cols = tile_cols.T
    group = 4
    steps = blocks_dev // group
    flops = 2 * rows * clusters

    ends = shards - 1
    left = lax.ppermute(blocks, NODES, [(i, i + 1) for i in range(ends)])
    right = lax.ppermute(blocks, NODES, [(i + 1, i) for i in range(ends)])

    asked = pl.pallas_call(
        functools.partial(requests_kernel, nodes_total),
        out_shape=pltpu.VMEM((shards, 1, 2 * clusters), f32),
        in_specs=[VMEM, ANY],
        out_specs=VMEM,
        scratch_shapes=[pltpu.VMEM((rows, clusters), bf16), pltpu.SemaphoreType.DMA((8,))],
        compiler_params=params(8),
        name="requests",
    )(cols, in_hbm(coupling))
    heard = lax.all_to_all(asked, NODES, split_axis=0, concat_axis=0, tiled=True)
    found = pl.pallas_call(
        functools.partial(gather_kernel, cap),
        out_shape=pltpu.HBM((shards * cap, tile, clusters), bf16),
        in_specs=[VMEM, ANY],
        out_specs=ANY,
        scratch_shapes=[
            pltpu.VMEM((blocks_dev, tile, clusters), bf16),
            pltpu.VMEM((shards, clusters), i32),
            pltpu.SMEM((shards, clusters), i32),
            pltpu.SemaphoreType.DMA((3,)),
        ],
        compiler_params=params(8),
        name="gather",
    )(on_chip(heard), in_hbm(blocks))
    fetched = lax.all_to_all(
        found.reshape(shards, cap, tile, clusters), NODES, split_axis=0, concat_axis=0, tiled=True
    ).reshape(shards * cap, tile, clusters)

    base = (my_index * blocks_dev - blocks_dev).astype(i32).reshape(1)
    part, graph2, where = pl.pallas_call(
        functools.partial(near_kernel, group, cap),
        out_shape=(
            pltpu.HBM((rows, clusters), f32),
            pltpu.VMEM((2 * clusters, clusters), bf16),
            jax.ShapeDtypeStruct((far_count,), i32),
        ),
        in_specs=[SMEM, SMEM, ANY, ANY, ANY, ANY, VMEM, VMEM],
        out_specs=(ANY, VMEM, SMEM),
        scratch_shapes=[
            pltpu.VMEM((3 * blocks_dev, tile, clusters), bf16),
            pltpu.VMEM((blocks_dev, NEAR, tile, tile), bf16),
            pltpu.VMEM((rows, clusters), f32),
            pltpu.VMEM((8, clusters), f32),
            pltpu.SMEM((shards,), i32),
            pltpu.SemaphoreType.DMA((3,)),
            pltpu.SemaphoreType.DMA((steps,)),
            pltpu.SemaphoreType.DMA((steps,)),
        ],
        compiler_params=params(20),
        cost_estimate=pl.CostEstimate(
            flops=flops * (NEAR * tile + 2 * clusters), bytes_accessed=16 << 20, transcendentals=rows * clusters
        ),
        name="near",
    )(cols, base, in_hbm(left), in_hbm(blocks), in_hbm(right), in_hbm(tile_vals), cluster_graph, on_chip(heard))

    logits, mass_part = pl.pallas_call(
        functools.partial(far_kernel, group, nodes_total),
        out_shape=(pltpu.VMEM((rows, clusters), f32), pltpu.VMEM((1, clusters), f32)),
        in_specs=[SMEM, VMEM, ANY, ANY, VMEM],
        out_specs=(VMEM, VMEM),
        scratch_shapes=[
            pltpu.VMEM((blocks_dev, far_slots, tile, tile), bf16),
            pltpu.SemaphoreType.DMA((steps,)),
            pltpu.SemaphoreType.DMA((steps,)),
        ],
        compiler_params=params(16),
        cost_estimate=pl.CostEstimate(
            flops=flops * (far_slots * tile + 2 * clusters), bytes_accessed=8 << 20, transcendentals=rows * clusters
        ),
        name="far",
    )(where, on_chip(fetched), in_hbm(tile_vals), in_hbm(part), on_chip(graph2))

    newmass, more = mass_part, jnp.zeros_like(mass_part)
    span = 1
    while span < shards:
        newmass = newmass + more if span > 1 else newmass
        more = lax.ppermute(newmass, NODES, [(i, i ^ span) for i in range(shards)])
        span *= 2

    return pl.pallas_call(
        functools.partial(last_kernel, 8),
        out_shape=jax.ShapeDtypeStruct((rows, clusters), f32),
        in_specs=[VMEM, VMEM, VMEM, VMEM],
        out_specs=ANY,
        scratch_shapes=[pltpu.VMEM((rows, clusters), f32), pltpu.SemaphoreType.DMA((8,))],
        compiler_params=params(8),
        name="last",
    )(on_chip(logits), on_chip(newmass), on_chip(more), cluster_mass.reshape(1, clusters))


def solution(mesh):
    return jax.shard_map(
        local,
        mesh=mesh,
        in_specs=(
            P(("groups", "rows", "sub"), None),
            P(("groups", "rows", "sub"), None, None, None),
            P(("groups", "rows", "sub"), None),
            P("groups", None),
            P("groups"),
        ),
        out_specs=P(("groups", "rows", "sub"), None),
        check_vma=False,
    )
```

```python
import functools

import jax
import jax.numpy as jnp
from jax import lax
from jax.experimental import pallas as pl
from jax.experimental.pallas import tpu as pltpu
from jax.sharding import PartitionSpec as P


NEAR = 4
NODES = ("rows", "sub")

eta_step = 2.0
relax_power = 0.5

ANY = pl.BlockSpec(memory_space=pl.ANY)
VMEM = pl.BlockSpec(memory_space=pltpu.VMEM)
SMEM = pl.BlockSpec(memory_space=pltpu.SMEM)

f32, bf16, i32 = jnp.float32, jnp.bfloat16, jnp.int32


def on_chip(x):
    return pltpu.with_memory_space_constraint(x, pltpu.VMEM)


def in_hbm(x):
    return pltpu.with_memory_space_constraint(x, pltpu.HBM)


def params(mib):
    return pltpu.CompilerParams(vmem_limit_bytes=mib << 20)


def requests_kernel(nodes_total, cols_ref, coupling_ref, out_ref, rows, sems):
    slots, blocks_dev = cols_ref.shape
    shards = out_ref.shape[0]
    nodes, clusters = coupling_ref.shape
    parts = sems.shape[0]
    step = nodes // parts
    copies = [
        pltpu.make_async_copy(coupling_ref.at[pl.ds(i * step, step)], rows.at[pl.ds(i * step, step)], sems.at[i])
        for i in range(parts)
    ]
    for copy in copies:
        copy.start()

    owner = lax.broadcasted_iota(i32, (shards, blocks_dev), 0)
    place = lax.broadcasted_iota(i32, (clusters, blocks_dev), 0).astype(f32)
    before = (
        lax.broadcasted_iota(i32, (blocks_dev, blocks_dev), 0)
        < lax.broadcasted_iota(i32, (blocks_dev, blocks_dev), 1)
    ).astype(f32)
    count = jnp.zeros((shards, 1), f32)
    table = jnp.zeros((shards, clusters), f32)
    for slot_id in range(NEAR, slots):
        local = cols_ref[slot_id : slot_id + 1, :] - owner * blocks_dev
        hit = (local >= 0) & (local < blocks_dev)
        hits = hit.astype(f32)
        earlier = jnp.dot(hits, before, preferred_element_type=f32) + count
        rank = jnp.sum(earlier * hits, axis=0, keepdims=True)
        count = count + jnp.sum(hits, axis=1, keepdims=True)
        wanted = jnp.where(hit, local, 0).astype(f32)
        table = table + lax.dot_general(
            wanted,
            (rank == place).astype(f32),
            (((1,), (1,)), ((), ())),
            precision=lax.Precision.HIGHEST,
            preferred_element_type=f32,
        )
    out_ref[:, 0, clusters:] = table
    total = jnp.zeros((8, clusters), f32)
    for i in range(parts):
        copies[i].wait()
        part = rows[pl.ds(i * step, step), :].astype(f32)
        total = total + jnp.sum(part.reshape(step // 8, 8, clusters), axis=0)
    mass = jnp.sum(total, axis=0, keepdims=True) / nodes_total
    out_ref[:, 0, :clusters] = jnp.broadcast_to(mass, (shards, clusters))


def gather_kernel(cap, heard_ref, blocks_ref, out_ref, held, wanted_ref, wanted_smem, sems):
    clusters = blocks_ref.shape[2]
    fetch = pltpu.make_async_copy(blocks_ref, held, sems.at[0])
    fetch.start()
    wanted_ref[...] = heard_ref[:, 0, clusters:].astype(i32)
    copy = pltpu.make_async_copy(wanted_ref, wanted_smem, sems.at[1])
    copy.start()
    copy.wait()
    fetch.wait()

    @pl.loop(0, heard_ref.shape[0])
    def _(n):
        for j in range(cap):
            pltpu.make_async_copy(held.at[wanted_smem[n, j]], out_ref.at[n * cap + j], sems.at[2]).start()

    pltpu.make_async_copy(out_ref, out_ref, sems.at[2]).wait()


def split(x):
    high = x.astype(bf16)
    return jnp.concatenate([high, (x - high.astype(f32)).astype(bf16)], axis=1)


def logs_kernel(parts, coupling_ref, out_ref, rows, kept, in_sems, out_sems):
    step = rows.shape[0] // parts
    here = [pl.ds(i * step, step) for i in range(parts)]
    loads = [pltpu.make_async_copy(coupling_ref.at[at], rows.at[at], in_sems.at[i]) for i, at in enumerate(here)]
    stores = [pltpu.make_async_copy(kept.at[at], out_ref.at[at], out_sems.at[i]) for i, at in enumerate(here)]
    for load in loads:
        load.start()
    for i, at in enumerate(here):
        loads[i].wait()
        kept[at, :] = jnp.log(rows[at, :].astype(f32))
        stores[i].start()
    for store in stores:
        store.wait()


def near_kernel(
    group, cap, cols_ref, base_ref, left_ref, own_ref, right_ref, tiles_ref, graph_ref, mass_ref,
    logs_ref, part_ref, graph2_ref, where_ref,
    window, tiles, part, pull_ref, count_ref, sems, tile_sems, logs_sems, part_sems,
):
    blocks_dev, tile, clusters = own_ref.shape
    slots = tiles_ref.shape[1]
    shards = mass_ref.shape[0]
    steps = blocks_dev // group
    copies = [
        pltpu.make_async_copy(src, window.at[pl.ds(i * blocks_dev, blocks_dev)], sems.at[i])
        for i, src in enumerate((left_ref, own_ref, right_ref))
    ]
    for copy in copies:
        copy.start()

    def fetch(i):
        here = pl.ds(i * group, group)
        return pltpu.make_async_copy(tiles_ref.at[here, pl.ds(0, NEAR)], tiles.at[here], tile_sems.at[i])

    def logs(i):
        here = pl.ds(pl.multiple_of(i * group * tile, group * tile), group * tile)
        return pltpu.make_async_copy(logs_ref.at[here], part.at[here], logs_sems.at[i])

    def store(i):
        here = pl.ds(pl.multiple_of(i * group * tile, group * tile), group * tile)
        return pltpu.make_async_copy(part.at[here], part_ref.at[here], part_sems.at[i])

    for i in range(steps):
        fetch(i).start()
        logs(i).start()

    graph = graph_ref[...].astype(f32)
    colmass = jnp.sum(mass_ref[:, 0, :clusters], axis=0, keepdims=True)
    pull_ref[...] = (
        lax.dot_general(
            jnp.broadcast_to(colmass, (8, clusters)),
            graph * graph,
            (((1,), (1,)), ((), ())),
            precision=lax.Precision.HIGHEST,
            preferred_element_type=f32,
        )
        / clusters
    )
    turned = graph.T.astype(bf16)
    graph2_ref[:clusters, :] = turned
    graph2_ref[clusters:, :] = turned

    @pl.loop(0, shards)
    def _(o):
        count_ref[o] = 0

    for slot_id in range(NEAR, slots):

        @pl.loop(0, blocks_dev)
        def _(b):
            owner = cols_ref[slot_id, b] // blocks_dev
            rank = count_ref[owner]
            count_ref[owner] = rank + 1
            where_ref[b * (slots - NEAR) + slot_id - NEAR] = owner * cap + rank

    for copy in copies:
        copy.wait()

    scale = 2.0 * eta_step / clusters

    @pl.loop(0, steps)
    def _(step):
        fetch(step).wait()
        logs(step).wait()
        for i in range(group):
            b = step * group + i
            here = pl.ds(pl.multiple_of(b * tile, tile), tile)
            picked = [window[cols_ref[s, b] - base_ref[0]] for s in range(NEAR)]
            wide = jnp.concatenate([tiles[b, s] for s in range(NEAR)], axis=1)
            spread = jnp.dot(wide, jnp.concatenate(picked, axis=0), preferred_element_type=f32)
            affinity = jnp.dot(split(spread), graph2_ref[...], preferred_element_type=f32)
            part[here, :] = part[here, :] - eta_step * pull_ref[0:1, :] + scale * affinity
        store(step).start()

    @pl.loop(0, steps)
    def _(step):
        store(step).wait()


def far_kernel(
    group, nodes_total, where_ref, blocks_ref, tiles_ref, part_ref, graph2_ref,
    logits_ref, mass_ref, tiles, tile_sems, part_sems,
):
    tile, clusters = blocks_ref.shape[1:]
    blocks_dev, far_slots = tiles.shape[:2]
    steps = blocks_dev // group
    scale = 2.0 * eta_step / clusters

    def fetches(i):
        here = pl.ds(i * group, group)
        there = pl.ds(i * group * tile, group * tile)
        return (
            pltpu.make_async_copy(tiles_ref.at[here, pl.ds(NEAR, far_slots)], tiles.at[here], tile_sems.at[i]),
            pltpu.make_async_copy(part_ref.at[there], logits_ref.at[there], part_sems.at[i]),
        )

    for i in range(steps):
        for copy in fetches(i):
            copy.start()

    total = jnp.zeros((8, clusters), f32)
    for step in range(steps):
        for copy in fetches(step):
            copy.wait()
        spreads = []
        for i in range(group):
            b = step * group + i
            picked = [blocks_ref[where_ref[b * far_slots + s]] for s in range(far_slots)]
            wide = jnp.concatenate([tiles[b, s] for s in range(far_slots)], axis=1)
            spreads.append(split(jnp.dot(wide, jnp.concatenate(picked, axis=0), preferred_element_type=f32)))
        here = pl.ds(step * group * tile, group * tile)
        affinity = jnp.dot(jnp.concatenate(spreads, axis=0), graph2_ref[...], preferred_element_type=f32)
        logits = logits_ref[here, :] + scale * affinity
        logits_ref[here, :] = logits
        total = total + jnp.sum(jnp.exp(logits).reshape(group * tile // 8, 8, clusters), axis=0)

    mass_ref[...] = jnp.sum(total, axis=0, keepdims=True) / nodes_total


def last_kernel(parts, logits_ref, newmass_ref, more_ref, target_ref, out_ref, kept, sems):
    shift = relax_power * (jnp.log(target_ref[...]) - jnp.log(newmass_ref[...] + more_ref[...]))
    rows = logits_ref.shape[0]
    step = rows // parts
    copies = []
    for i in range(parts):
        here = pl.ds(i * step, step)
        shifted = logits_ref[here, :] + shift
        kept[here, :] = shifted - jnp.log(jnp.sum(jnp.exp(shifted), axis=1, keepdims=True))
        copies.append(pltpu.make_async_copy(kept.at[here], out_ref.at[here], sems.at[i]))
        copies[-1].start()
    for copy in copies:
        copy.wait()


def local(coupling, tile_vals, tile_cols, cluster_graph, cluster_mass):
    shards = lax.axis_size(NODES)
    my_index = lax.axis_index(NODES)
    blocks_dev, slots = tile_cols.shape
    tile = tile_vals.shape[2]
    rows, clusters = coupling.shape
    far_slots = slots - NEAR
    nodes_total = rows * shards
    far_count = blocks_dev * far_slots
    cap = (far_count + shards - 1) // shards
    blocks = coupling.reshape(blocks_dev, tile, clusters)
    cols = tile_cols.T
    group = 4
    steps = blocks_dev // group
    flops = 2 * rows * clusters

    ends = shards - 1
    left = lax.ppermute(blocks, NODES, [(i, i + 1) for i in range(ends)])
    right = lax.ppermute(blocks, NODES, [(i + 1, i) for i in range(ends)])

    asked = pl.pallas_call(
        functools.partial(requests_kernel, nodes_total),
        out_shape=pltpu.VMEM((shards, 1, 2 * clusters), f32),
        in_specs=[VMEM, ANY],
        out_specs=VMEM,
        scratch_shapes=[pltpu.VMEM((rows, clusters), bf16), pltpu.SemaphoreType.DMA((8,))],
        compiler_params=params(8),
        name="requests",
    )(cols, in_hbm(coupling))
    heard = lax.all_to_all(asked, NODES, split_axis=0, concat_axis=0, tiled=True)
    logs = pl.pallas_call(
        functools.partial(logs_kernel, 8),
        out_shape=pltpu.HBM((rows, clusters), f32),
        in_specs=[ANY],
        out_specs=ANY,
        scratch_shapes=[
            pltpu.VMEM((rows, clusters), bf16),
            pltpu.VMEM((rows, clusters), f32),
            pltpu.SemaphoreType.DMA((8,)),
            pltpu.SemaphoreType.DMA((8,)),
        ],
        compiler_params=params(8),
        name="logs",
    )(in_hbm(coupling))
    found = pl.pallas_call(
        functools.partial(gather_kernel, cap),
        out_shape=pltpu.HBM((shards * cap, tile, clusters), bf16),
        in_specs=[VMEM, ANY],
        out_specs=ANY,
        scratch_shapes=[
            pltpu.VMEM((blocks_dev, tile, clusters), bf16),
            pltpu.VMEM((shards, clusters), i32),
            pltpu.SMEM((shards, clusters), i32),
            pltpu.SemaphoreType.DMA((3,)),
        ],
        compiler_params=params(8),
        name="gather",
    )(on_chip(heard), in_hbm(blocks))
    fetched = lax.all_to_all(
        found.reshape(shards, cap, tile, clusters), NODES, split_axis=0, concat_axis=0, tiled=True
    ).reshape(shards * cap, tile, clusters)

    base = (my_index * blocks_dev - blocks_dev).astype(i32).reshape(1)
    part, graph2, where = pl.pallas_call(
        functools.partial(near_kernel, group, cap),
        out_shape=(
            pltpu.HBM((rows, clusters), f32),
            pltpu.VMEM((2 * clusters, clusters), bf16),
            jax.ShapeDtypeStruct((far_count,), i32),
        ),
        in_specs=[SMEM, SMEM, ANY, ANY, ANY, ANY, VMEM, VMEM, ANY],
        out_specs=(ANY, VMEM, SMEM),
        scratch_shapes=[
            pltpu.VMEM((3 * blocks_dev, tile, clusters), bf16),
            pltpu.VMEM((blocks_dev, NEAR, tile, tile), bf16),
            pltpu.VMEM((rows, clusters), f32),
            pltpu.VMEM((8, clusters), f32),
            pltpu.SMEM((shards,), i32),
            pltpu.SemaphoreType.DMA((3,)),
            pltpu.SemaphoreType.DMA((steps,)),
            pltpu.SemaphoreType.DMA((steps,)),
            pltpu.SemaphoreType.DMA((steps,)),
        ],
        compiler_params=params(20),
        cost_estimate=pl.CostEstimate(
            flops=flops * (NEAR * tile + 2 * clusters), bytes_accessed=16 << 20, transcendentals=rows * clusters
        ),
        name="near",
    )(cols, base, in_hbm(left), in_hbm(blocks), in_hbm(right), in_hbm(tile_vals), cluster_graph, on_chip(heard), in_hbm(logs))

    logits, mass_part = pl.pallas_call(
        functools.partial(far_kernel, group, nodes_total),
        out_shape=(pltpu.VMEM((rows, clusters), f32), pltpu.VMEM((1, clusters), f32)),
        in_specs=[SMEM, VMEM, ANY, ANY, VMEM],
        out_specs=(VMEM, VMEM),
        scratch_shapes=[
            pltpu.VMEM((blocks_dev, far_slots, tile, tile), bf16),
            pltpu.SemaphoreType.DMA((steps,)),
            pltpu.SemaphoreType.DMA((steps,)),
        ],
        compiler_params=params(16),
        cost_estimate=pl.CostEstimate(
            flops=flops * (far_slots * tile + 2 * clusters), bytes_accessed=8 << 20, transcendentals=rows * clusters
        ),
        name="far",
    )(where, on_chip(fetched), in_hbm(tile_vals), in_hbm(part), on_chip(graph2))

    newmass, more = mass_part, jnp.zeros_like(mass_part)
    span = 1
    while span < shards:
        newmass = newmass + more if span > 1 else newmass
        more = lax.ppermute(newmass, NODES, [(i, i ^ span) for i in range(shards)])
        span *= 2

    return pl.pallas_call(
        functools.partial(last_kernel, 8),
        out_shape=jax.ShapeDtypeStruct((rows, clusters), f32),
        in_specs=[VMEM, VMEM, VMEM, VMEM],
        out_specs=ANY,
        scratch_shapes=[pltpu.VMEM((rows, clusters), f32), pltpu.SemaphoreType.DMA((8,))],
        compiler_params=params(8),
        name="last",
    )(on_chip(logits), on_chip(newmass), on_chip(more), cluster_mass.reshape(1, clusters))


def solution(mesh):
    return jax.shard_map(
        local,
        mesh=mesh,
        in_specs=(
            P(("groups", "rows", "sub"), None),
            P(("groups", "rows", "sub"), None, None, None),
            P(("groups", "rows", "sub"), None),
            P("groups", None),
            P("groups"),
        ),
        out_specs=P(("groups", "rows", "sub"), None),
        check_vma=False,
    )
```

```python
import functools

import jax
import jax.numpy as jnp
from jax import lax
from jax.experimental import pallas as pl
from jax.experimental.pallas import tpu as pltpu
from jax.sharding import PartitionSpec as P


NEAR = 4
NODES = ("rows", "sub")

eta_step = 2.0
relax_power = 0.5

ANY = pl.BlockSpec(memory_space=pl.ANY)
VMEM = pl.BlockSpec(memory_space=pltpu.VMEM)
SMEM = pl.BlockSpec(memory_space=pltpu.SMEM)

f32, bf16, i32 = jnp.float32, jnp.bfloat16, jnp.int32


def on_chip(x):
    return pltpu.with_memory_space_constraint(x, pltpu.VMEM)


def in_hbm(x):
    return pltpu.with_memory_space_constraint(x, pltpu.HBM)


def params(mib):
    return pltpu.CompilerParams(vmem_limit_bytes=mib << 20)


def requests_kernel(nodes_total, cols_ref, coupling_ref, out_ref, rows, sems):
    slots, blocks_dev = cols_ref.shape
    shards = out_ref.shape[0]
    nodes, clusters = coupling_ref.shape
    parts = sems.shape[0]
    step = nodes // parts
    copies = [
        pltpu.make_async_copy(coupling_ref.at[pl.ds(i * step, step)], rows.at[pl.ds(i * step, step)], sems.at[i])
        for i in range(parts)
    ]
    for copy in copies:
        copy.start()

    owner = lax.broadcasted_iota(i32, (shards, blocks_dev), 0)
    place = lax.broadcasted_iota(i32, (clusters, blocks_dev), 0).astype(f32)
    before = (
        lax.broadcasted_iota(i32, (blocks_dev, blocks_dev), 0)
        < lax.broadcasted_iota(i32, (blocks_dev, blocks_dev), 1)
    ).astype(f32)
    count = jnp.zeros((shards, 1), f32)
    table = jnp.zeros((shards, clusters), f32)
    for slot_id in range(NEAR, slots):
        local = cols_ref[slot_id : slot_id + 1, :] - owner * blocks_dev
        hit = (local >= 0) & (local < blocks_dev)
        hits = hit.astype(f32)
        earlier = jnp.dot(hits, before, preferred_element_type=f32) + count
        rank = jnp.sum(earlier * hits, axis=0, keepdims=True)
        count = count + jnp.sum(hits, axis=1, keepdims=True)
        wanted = jnp.where(hit, local, 0).astype(f32)
        table = table + lax.dot_general(
            wanted,
            (rank == place).astype(f32),
            (((1,), (1,)), ((), ())),
            precision=lax.Precision.HIGHEST,
            preferred_element_type=f32,
        )
    out_ref[:, 0, clusters:] = table
    total = jnp.zeros((8, clusters), f32)
    for i in range(parts):
        copies[i].wait()
        part = rows[pl.ds(i * step, step), :].astype(f32)
        total = total + jnp.sum(part.reshape(step // 8, 8, clusters), axis=0)
    mass = jnp.sum(total, axis=0, keepdims=True) / nodes_total
    out_ref[:, 0, :clusters] = jnp.broadcast_to(mass, (shards, clusters))


def gather_kernel(cap, heard_ref, blocks_ref, out_ref, wanted_ref, wanted_smem, sems):
    clusters = blocks_ref.shape[2]
    wanted_ref[...] = heard_ref[:, 0, clusters:].astype(i32)
    copy = pltpu.make_async_copy(wanted_ref, wanted_smem, sems.at[0])
    copy.start()
    copy.wait()

    @pl.loop(0, heard_ref.shape[0])
    def _(n):
        for j in range(cap):
            pltpu.make_async_copy(blocks_ref.at[wanted_smem[n, j]], out_ref.at[n * cap + j], sems.at[1]).start()

    pltpu.make_async_copy(out_ref, out_ref, sems.at[1]).wait()


def prep_kernel(cap, cols_ref, graph_ref, graph2_ref, where_ref, count_ref):
    slots, blocks_dev = cols_ref.shape
    clusters = graph_ref.shape[0]
    turned = graph_ref[...].astype(f32).T.astype(bf16)
    graph2_ref[:clusters, :] = turned
    graph2_ref[clusters:, :] = turned

    @pl.loop(0, count_ref.shape[0])
    def _(o):
        count_ref[o] = 0

    for slot_id in range(NEAR, slots):

        @pl.loop(0, blocks_dev)
        def _(b):
            owner = cols_ref[slot_id, b] // blocks_dev
            rank = count_ref[owner]
            count_ref[owner] = rank + 1
            where_ref[b * (slots - NEAR) + slot_id - NEAR] = owner * cap + rank


def split(x):
    high = x.astype(bf16)
    return jnp.concatenate([high, (x - high.astype(f32)).astype(bf16)], axis=1)


def near_kernel(
    group, middle, cols_ref, place_ref, left_ref, own_ref, right_ref, across_ref, tiles_ref, graph_ref, mass_ref,
    graph2_ref, part_ref, window, tiles, part, pull_ref, sems, tile_sems, part_sems,
):
    blocks_dev, tile, clusters = own_ref.shape
    steps = blocks_dev // group
    place = place_ref[0]

    def take(src, i):
        return pltpu.make_async_copy(src, window.at[pl.ds(i * blocks_dev, blocks_dev)], sems.at[i])

    take(own_ref, 1).start()
    for i, src, at in ((0, left_ref, middle), (2, right_ref, middle - 1)):

        @pl.when(place == at)
        def _():
            take(across_ref, i).start()

        @pl.when(place != at)
        def _():
            take(src, i).start()

    def fetch(i):
        here = pl.ds(i * group, group)
        return pltpu.make_async_copy(tiles_ref.at[here, pl.ds(0, NEAR)], tiles.at[here], tile_sems.at[i])

    def store(i):
        here = pl.ds(pl.multiple_of(i * group * tile, group * tile), group * tile)
        return pltpu.make_async_copy(part.at[here], part_ref.at[here], part_sems.at[i])

    for i in range(steps):
        fetch(i).start()

    graph = graph_ref[...].astype(f32)
    colmass = jnp.sum(mass_ref[:, 0, :clusters], axis=0, keepdims=True)
    pull_ref[...] = (
        lax.dot_general(
            jnp.broadcast_to(colmass, (8, clusters)),
            graph * graph,
            (((1,), (1,)), ((), ())),
            precision=lax.Precision.HIGHEST,
            preferred_element_type=f32,
        )
        / clusters
    )
    for i, src in enumerate((left_ref, own_ref, right_ref)):
        take(src, i).wait()

    base = (place - 1) * blocks_dev
    scale = 2.0 * eta_step / clusters

    @pl.loop(0, steps)
    def _(step):
        fetch(step).wait()
        for i in range(group):
            b = step * group + i
            here = pl.ds(pl.multiple_of(b * tile, tile), tile)
            picked = [window[cols_ref[s, b] - base] for s in range(NEAR)]
            wide = jnp.concatenate([tiles[b, s] for s in range(NEAR)], axis=1)
            spread = jnp.dot(wide, jnp.concatenate(picked, axis=0), preferred_element_type=f32)
            affinity = jnp.dot(split(spread), graph2_ref[...], preferred_element_type=f32)
            part[here, :] = (
                jnp.log(window[blocks_dev + b].astype(f32)) - eta_step * pull_ref[0:1, :] + scale * affinity
            )
        store(step).start()

    @pl.loop(0, steps)
    def _(step):
        store(step).wait()


def far_kernel(
    group, chunk, nodes_total, where_ref, blocks_ref, tiles_ref, part_ref, graph2_ref,
    logits_ref, mass_ref, tiles, tile_sems, part_sems,
):
    tile, clusters = blocks_ref.shape[1:]
    blocks_dev, far_slots = tiles.shape[:2]
    steps = blocks_dev // group
    scale = 2.0 * eta_step / clusters

    def fetches(i):
        here = pl.ds(i * chunk, chunk)
        there = pl.ds(i * chunk * tile, chunk * tile)
        return (
            pltpu.make_async_copy(tiles_ref.at[here, pl.ds(NEAR, far_slots)], tiles.at[here], tile_sems.at[i]),
            pltpu.make_async_copy(part_ref.at[there], logits_ref.at[there], part_sems.at[i]),
        )

    for i in range(blocks_dev // chunk):
        for copy in fetches(i):
            copy.start()

    def products(step):
        first = step * group
        if first % chunk == 0:
            for copy in fetches(first // chunk):
                copy.wait()
        spreads = []
        for b in range(first, first + group):
            picked = [blocks_ref[where_ref[b * far_slots + s]] for s in range(far_slots)]
            wide = jnp.concatenate([tiles[b, s] for s in range(far_slots)], axis=1)
            spreads.append(split(jnp.dot(wide, jnp.concatenate(picked, axis=0), preferred_element_type=f32)))
        return jnp.concatenate(spreads, axis=0)

    total = jnp.zeros((8, clusters), f32)
    ahead = products(0)
    for step in range(steps):
        spreads = ahead
        if step + 1 < steps:
            ahead = products(step + 1)
        here = pl.ds(step * group * tile, group * tile)
        affinity = jnp.dot(spreads, graph2_ref[...], preferred_element_type=f32)
        logits = logits_ref[here, :] + scale * affinity
        logits_ref[here, :] = logits
        total = total + jnp.sum(jnp.exp(logits).reshape(group * tile // 8, 8, clusters), axis=0)

    mass = jnp.sum(total, axis=0, keepdims=True) / nodes_total
    mass_ref[:, 0, :] = jnp.broadcast_to(mass, (mass_ref.shape[0], clusters))


def last_kernel(parts, logits_ref, mass_ref, target_ref, out_ref, kept, sems):
    newmass = jnp.sum(mass_ref[:, 0, :], axis=0, keepdims=True)
    shift = relax_power * (jnp.log(target_ref[...]) - jnp.log(newmass))
    rows = logits_ref.shape[0]
    step = rows // parts
    copies = []
    for i in range(parts):
        here = pl.ds(i * step, step)
        shifted = logits_ref[here, :] + shift
        kept[here, :] = shifted - jnp.log(jnp.sum(jnp.exp(shifted), axis=1, keepdims=True))
        copies.append(pltpu.make_async_copy(kept.at[here], out_ref.at[here], sems.at[i]))
        copies[-1].start()
    for copy in copies:
        copy.wait()


def local(coupling, tile_vals, tile_cols, cluster_graph, cluster_mass):
    shards = lax.axis_size(NODES)
    my_index = lax.axis_index(NODES)
    blocks_dev, slots = tile_cols.shape
    tile = tile_vals.shape[2]
    rows, clusters = coupling.shape
    far_slots = slots - NEAR
    nodes_total = rows * shards
    far_count = blocks_dev * far_slots
    cap = (far_count + shards - 1) // shards
    blocks = coupling.reshape(blocks_dev, tile, clusters)
    cols = tile_cols.T
    group = 4
    steps = blocks_dev // group
    flops = 2 * rows * clusters

    middle = shards // 2
    across = lax.ppermute(blocks, NODES, [(middle - 1, middle), (middle, middle - 1)])
    left = lax.ppermute(blocks, NODES, [(i, i + 1) for i in range(shards - 1) if i + 1 != middle])
    right = lax.ppermute(blocks, NODES, [(i + 1, i) for i in range(shards - 1) if i + 1 != middle])

    asked, held = pl.pallas_call(
        functools.partial(requests_kernel, nodes_total),
        out_shape=(jax.ShapeDtypeStruct((shards, 1, 2 * clusters), f32), pltpu.VMEM((rows, clusters), bf16)),
        in_specs=[VMEM, ANY],
        out_specs=(VMEM, VMEM),
        scratch_shapes=[pltpu.SemaphoreType.DMA((8,))],
        compiler_params=params(8),
        name="requests",
    )(cols, in_hbm(coupling))
    heard = lax.all_to_all(asked, NODES, split_axis=0, concat_axis=0, tiled=True)
    graph2, where = pl.pallas_call(
        functools.partial(prep_kernel, cap),
        out_shape=(
            jax.ShapeDtypeStruct((2 * clusters, clusters), bf16),
            jax.ShapeDtypeStruct((far_count,), i32),
        ),
        in_specs=[SMEM, VMEM],
        out_specs=(VMEM, SMEM),
        scratch_shapes=[pltpu.SMEM((shards,), i32)],
        compiler_params=params(4),
        name="prep",
    )(cols, cluster_graph)
    found = pl.pallas_call(
        functools.partial(gather_kernel, cap),
        out_shape=pltpu.HBM((shards * cap, tile, clusters), bf16),
        in_specs=[VMEM, VMEM],
        out_specs=ANY,
        scratch_shapes=[
            pltpu.VMEM((shards, clusters), i32),
            pltpu.SMEM((shards, clusters), i32),
            pltpu.SemaphoreType.DMA((2,)),
        ],
        compiler_params=params(8),
        name="gather",
    )(on_chip(heard), on_chip(held.reshape(blocks.shape)))
    fetched = lax.all_to_all(
        found.reshape(shards, cap, tile, clusters), NODES, split_axis=0, concat_axis=0, tiled=True
    ).reshape(shards * cap, tile, clusters)

    part = pl.pallas_call(
        functools.partial(near_kernel, group, middle),
        out_shape=pltpu.HBM((rows, clusters), f32),
        in_specs=[SMEM, SMEM, ANY, ANY, ANY, ANY, ANY, VMEM, VMEM, VMEM],
        out_specs=ANY,
        scratch_shapes=[
            pltpu.VMEM((3 * blocks_dev, tile, clusters), bf16),
            pltpu.VMEM((blocks_dev, NEAR, tile, tile), bf16),
            pltpu.VMEM((rows, clusters), f32),
            pltpu.VMEM((8, clusters), f32),
            pltpu.SemaphoreType.DMA((3,)),
            pltpu.SemaphoreType.DMA((steps,)),
            pltpu.SemaphoreType.DMA((steps,)),
        ],
        compiler_params=params(20),
        cost_estimate=pl.CostEstimate(
            flops=flops * (NEAR * tile + 2 * clusters), bytes_accessed=16 << 20, transcendentals=rows * clusters
        ),
        name="near",
    )(
        cols, my_index.astype(i32).reshape(1), in_hbm(left), in_hbm(blocks), in_hbm(right), in_hbm(across),
        in_hbm(tile_vals), cluster_graph, on_chip(heard), on_chip(graph2),
    )

    chunk = min(16, blocks_dev)
    logits, mass_parts = pl.pallas_call(
        functools.partial(far_kernel, group, chunk, nodes_total),
        out_shape=(pltpu.VMEM((rows, clusters), f32), pltpu.VMEM((shards, 1, clusters), f32)),
        in_specs=[SMEM, VMEM, ANY, ANY, VMEM],
        out_specs=(VMEM, VMEM),
        scratch_shapes=[
            pltpu.VMEM((blocks_dev, far_slots, tile, tile), bf16),
            pltpu.SemaphoreType.DMA((blocks_dev // chunk,)),
            pltpu.SemaphoreType.DMA((blocks_dev // chunk,)),
        ],
        compiler_params=params(16),
        cost_estimate=pl.CostEstimate(
            flops=flops * (far_slots * tile + 2 * clusters), bytes_accessed=8 << 20, transcendentals=rows * clusters
        ),
        name="far",
    )(where, on_chip(fetched), in_hbm(tile_vals), in_hbm(part), on_chip(graph2))

    masses = lax.all_to_all(mass_parts, NODES, split_axis=0, concat_axis=0, tiled=True)

    return pl.pallas_call(
        functools.partial(last_kernel, 8),
        out_shape=jax.ShapeDtypeStruct((rows, clusters), f32),
        in_specs=[VMEM, VMEM, VMEM],
        out_specs=ANY,
        scratch_shapes=[pltpu.VMEM((rows, clusters), f32), pltpu.SemaphoreType.DMA((8,))],
        compiler_params=params(8),
        name="last",
    )(on_chip(logits), on_chip(masses), cluster_mass.reshape(1, clusters))


def solution(mesh):
    return jax.shard_map(
        local,
        mesh=mesh,
        in_specs=(
            P(("groups", "rows", "sub"), None),
            P(("groups", "rows", "sub"), None, None, None),
            P(("groups", "rows", "sub"), None),
            P("groups", None),
            P("groups"),
        ),
        out_specs=P(("groups", "rows", "sub"), None),
        check_vma=False,
    )
```

```python
import functools

import jax
import jax.numpy as jnp
from jax import lax
from jax.experimental import pallas as pl
from jax.experimental.pallas import tpu as pltpu
from jax.sharding import PartitionSpec as P


NEAR = 4
NODES = ("rows", "sub")

eta_step = 2.0
relax_power = 0.5

ANY = pl.BlockSpec(memory_space=pl.ANY)
VMEM = pl.BlockSpec(memory_space=pltpu.VMEM)
SMEM = pl.BlockSpec(memory_space=pltpu.SMEM)

f32, bf16, i32 = jnp.float32, jnp.bfloat16, jnp.int32


def on_chip(x):
    return pltpu.with_memory_space_constraint(x, pltpu.VMEM)


def in_hbm(x):
    return pltpu.with_memory_space_constraint(x, pltpu.HBM)


def params(mib):
    return pltpu.CompilerParams(vmem_limit_bytes=mib << 20)


def requests_kernel(nodes_total, cols_ref, coupling_ref, out_ref, rows, sems):
    slots, blocks_dev = cols_ref.shape
    shards = out_ref.shape[0]
    nodes, clusters = coupling_ref.shape
    parts = sems.shape[0]
    step = nodes // parts
    copies = [
        pltpu.make_async_copy(coupling_ref.at[pl.ds(i * step, step)], rows.at[pl.ds(i * step, step)], sems.at[i])
        for i in range(parts)
    ]
    for copy in copies:
        copy.start()

    owner = lax.broadcasted_iota(i32, (shards, blocks_dev), 0)
    place = lax.broadcasted_iota(i32, (clusters, blocks_dev), 0).astype(f32)
    before = (
        lax.broadcasted_iota(i32, (blocks_dev, blocks_dev), 0)
        < lax.broadcasted_iota(i32, (blocks_dev, blocks_dev), 1)
    ).astype(f32)
    count = jnp.zeros((shards, 1), f32)
    table = jnp.zeros((shards, clusters), f32)
    for slot_id in range(NEAR, slots):
        local = cols_ref[slot_id : slot_id + 1, :] - owner * blocks_dev
        hit = (local >= 0) & (local < blocks_dev)
        hits = hit.astype(f32)
        earlier = jnp.dot(hits, before, preferred_element_type=f32) + count
        rank = jnp.sum(earlier * hits, axis=0, keepdims=True)
        count = count + jnp.sum(hits, axis=1, keepdims=True)
        wanted = jnp.where(hit, local, 0).astype(f32)
        table = table + lax.dot_general(
            wanted,
            (rank == place).astype(f32),
            (((1,), (1,)), ((), ())),
            precision=lax.Precision.HIGHEST,
            preferred_element_type=f32,
        )
    out_ref[:, 0, clusters:] = table
    total = jnp.zeros((8, clusters), f32)
    for i in range(parts):
        copies[i].wait()
        part = rows[pl.ds(i * step, step), :].astype(f32)
        total = total + jnp.sum(part.reshape(step // 8, 8, clusters), axis=0)
    mass = jnp.sum(total, axis=0, keepdims=True) / nodes_total
    out_ref[:, 0, :clusters] = jnp.broadcast_to(mass, (shards, clusters))


def gather_kernel(cap, heard_ref, blocks_ref, out_ref, wanted_ref, wanted_smem, sems):
    clusters = blocks_ref.shape[2]
    wanted_ref[...] = heard_ref[:, 0, clusters:].astype(i32)
    copy = pltpu.make_async_copy(wanted_ref, wanted_smem, sems.at[0])
    copy.start()
    copy.wait()

    @pl.loop(0, heard_ref.shape[0])
    def _(n):
        for j in range(cap):
            pltpu.make_async_copy(blocks_ref.at[wanted_smem[n, j]], out_ref.at[n * cap + j], sems.at[1]).start()

    pltpu.make_async_copy(out_ref, out_ref, sems.at[1]).wait()


def split(x):
    high = x.astype(bf16)
    return jnp.concatenate([high, (x - high.astype(f32)).astype(bf16)], axis=1)


def near_kernel(
    group, cap, cols_ref, place_ref, left_ref, own_ref, right_ref, tiles_ref, graph_ref, mass_ref,
    part_ref, graph2_ref, where_ref, window, tiles, part, pull_ref, count_ref, sems, tile_sems, part_sems,
):
    blocks_dev, tile, clusters = own_ref.shape
    slots = tiles_ref.shape[1]
    steps = blocks_dev // group
    copies = [
        pltpu.make_async_copy(src, window.at[pl.ds(i * blocks_dev, blocks_dev)], sems.at[i])
        for i, src in enumerate((left_ref, own_ref, right_ref))
    ]
    for copy in copies:
        copy.start()

    def fetch(i):
        here = pl.ds(i * group, group)
        return pltpu.make_async_copy(tiles_ref.at[here, pl.ds(0, NEAR)], tiles.at[here], tile_sems.at[i])

    def store(i):
        here = pl.ds(pl.multiple_of(i * group * tile, group * tile), group * tile)
        return pltpu.make_async_copy(part.at[here], part_ref.at[here], part_sems.at[i])

    for i in range(steps):
        fetch(i).start()

    graph = graph_ref[...].astype(f32)
    colmass = jnp.sum(mass_ref[:, 0, :clusters], axis=0, keepdims=True)
    pull_ref[...] = (
        lax.dot_general(
            jnp.broadcast_to(colmass, (8, clusters)),
            graph * graph,
            (((1,), (1,)), ((), ())),
            precision=lax.Precision.HIGHEST,
            preferred_element_type=f32,
        )
        / clusters
    )
    turned = graph.T.astype(bf16)
    graph2_ref[:clusters, :] = turned
    graph2_ref[clusters:, :] = turned

    @pl.loop(0, count_ref.shape[0])
    def _(o):
        count_ref[o] = 0

    for slot_id in range(NEAR, slots):

        @pl.loop(0, blocks_dev)
        def _(b):
            owner = cols_ref[slot_id, b] // blocks_dev
            rank = count_ref[owner]
            count_ref[owner] = rank + 1
            where_ref[b * (slots - NEAR) + slot_id - NEAR] = owner * cap + rank

    for copy in copies:
        copy.wait()

    base = (place_ref[0] - 1) * blocks_dev
    scale = 2.0 * eta_step / clusters

    @pl.loop(0, steps)
    def _(step):
        fetch(step).wait()
        for i in range(group):
            b = step * group + i
            here = pl.ds(pl.multiple_of(b * tile, tile), tile)
            picked = [window[cols_ref[s, b] - base] for s in range(NEAR)]
            wide = jnp.concatenate([tiles[b, s] for s in range(NEAR)], axis=1)
            spread = jnp.dot(wide, jnp.concatenate(picked, axis=0), preferred_element_type=f32)
            affinity = jnp.dot(split(spread), graph2_ref[...], preferred_element_type=f32)
            part[here, :] = (
                jnp.log(window[blocks_dev + b].astype(f32)) - eta_step * pull_ref[0:1, :] + scale * affinity
            )
        store(step).start()

    @pl.loop(0, steps)
    def _(step):
        store(step).wait()


def far_kernel(
    group, chunk, nodes_total, where_ref, blocks_ref, tiles_ref, part_ref, graph2_ref,
    logits_ref, mass_ref, tiles, tile_sems, part_sems,
):
    tile, clusters = blocks_ref.shape[1:]
    blocks_dev, far_slots = tiles.shape[:2]
    steps = blocks_dev // group
    scale = 2.0 * eta_step / clusters

    def fetches(i):
        here = pl.ds(i * chunk, chunk)
        there = pl.ds(i * chunk * tile, chunk * tile)
        return (
            pltpu.make_async_copy(tiles_ref.at[here, pl.ds(NEAR, far_slots)], tiles.at[here], tile_sems.at[i]),
            pltpu.make_async_copy(part_ref.at[there], logits_ref.at[there], part_sems.at[i]),
        )

    for i in range(blocks_dev // chunk):
        for copy in fetches(i):
            copy.start()

    def products(step):
        first = step * group
        if first % chunk == 0:
            for copy in fetches(first // chunk):
                copy.wait()
        spreads = []
        for b in range(first, first + group):
            picked = [blocks_ref[where_ref[b * far_slots + s]] for s in range(far_slots)]
            wide = jnp.concatenate([tiles[b, s] for s in range(far_slots)], axis=1)
            spreads.append(split(jnp.dot(wide, jnp.concatenate(picked, axis=0), preferred_element_type=f32)))
        return jnp.concatenate(spreads, axis=0)

    total = jnp.zeros((8, clusters), f32)
    ahead = products(0)
    for step in range(steps):
        spreads = ahead
        if step + 1 < steps:
            ahead = products(step + 1)
        here = pl.ds(step * group * tile, group * tile)
        affinity = jnp.dot(spreads, graph2_ref[...], preferred_element_type=f32)
        logits = logits_ref[here, :] + scale * affinity
        logits_ref[here, :] = logits
        total = total + jnp.sum(jnp.exp(logits).reshape(group * tile // 8, 8, clusters), axis=0)

    mass = jnp.sum(total, axis=0, keepdims=True) / nodes_total
    mass_ref[:, 0, :] = jnp.broadcast_to(mass, (mass_ref.shape[0], clusters))


def last_kernel(parts, logits_ref, mass_ref, target_ref, out_ref, kept, sems):
    newmass = jnp.sum(mass_ref[:, 0, :], axis=0, keepdims=True)
    shift = relax_power * (jnp.log(target_ref[...]) - jnp.log(newmass))
    rows = logits_ref.shape[0]
    step = rows // parts
    copies = []
    for i in range(parts):
        here = pl.ds(i * step, step)
        shifted = logits_ref[here, :] + shift
        kept[here, :] = shifted - jnp.log(jnp.sum(jnp.exp(shifted), axis=1, keepdims=True))
        copies.append(pltpu.make_async_copy(kept.at[here], out_ref.at[here], sems.at[i]))
        copies[-1].start()
    for copy in copies:
        copy.wait()


def local(coupling, tile_vals, tile_cols, cluster_graph, cluster_mass):
    shards = lax.axis_size(NODES)
    my_index = lax.axis_index(NODES)
    blocks_dev, slots = tile_cols.shape
    tile = tile_vals.shape[2]
    rows, clusters = coupling.shape
    far_slots = slots - NEAR
    nodes_total = rows * shards
    far_count = blocks_dev * far_slots
    cap = (far_count + shards - 1) // shards
    blocks = coupling.reshape(blocks_dev, tile, clusters)
    cols = tile_cols.T
    group = 4
    steps = blocks_dev // group
    flops = 2 * rows * clusters

    left = lax.ppermute(blocks, NODES, [(i, i + 1) for i in range(shards - 1)])
    right = lax.ppermute(blocks, NODES, [(i + 1, i) for i in range(shards - 1)])

    asked, held = pl.pallas_call(
        functools.partial(requests_kernel, nodes_total),
        out_shape=(jax.ShapeDtypeStruct((shards, 1, 2 * clusters), f32), pltpu.VMEM((rows, clusters), bf16)),
        in_specs=[VMEM, ANY],
        out_specs=(VMEM, VMEM),
        scratch_shapes=[pltpu.SemaphoreType.DMA((8,))],
        compiler_params=params(8),
        name="requests",
    )(cols, in_hbm(coupling))
    heard = lax.all_to_all(asked, NODES, split_axis=0, concat_axis=0, tiled=True)
    found = pl.pallas_call(
        functools.partial(gather_kernel, cap),
        out_shape=pltpu.HBM((shards * cap, tile, clusters), bf16),
        in_specs=[VMEM, VMEM],
        out_specs=ANY,
        scratch_shapes=[
            pltpu.VMEM((shards, clusters), i32),
            pltpu.SMEM((shards, clusters), i32),
            pltpu.SemaphoreType.DMA((2,)),
        ],
        compiler_params=params(8),
        name="gather",
    )(on_chip(heard), on_chip(held.reshape(blocks.shape)))
    fetched = lax.all_to_all(
        found.reshape(shards, cap, tile, clusters), NODES, split_axis=0, concat_axis=0, tiled=True
    ).reshape(shards * cap, tile, clusters)

    part, graph2, where = pl.pallas_call(
        functools.partial(near_kernel, group, cap),
        out_shape=(
            pltpu.HBM((rows, clusters), f32),
            pltpu.VMEM((2 * clusters, clusters), bf16),
            jax.ShapeDtypeStruct((far_count,), i32),
        ),
        in_specs=[SMEM, SMEM, ANY, ANY, ANY, ANY, VMEM, VMEM],
        out_specs=(ANY, VMEM, SMEM),
        scratch_shapes=[
            pltpu.VMEM((3 * blocks_dev, tile, clusters), bf16),
            pltpu.VMEM((blocks_dev, NEAR, tile, tile), bf16),
            pltpu.VMEM((rows, clusters), f32),
            pltpu.VMEM((8, clusters), f32),
            pltpu.SMEM((shards,), i32),
            pltpu.SemaphoreType.DMA((3,)),
            pltpu.SemaphoreType.DMA((steps,)),
            pltpu.SemaphoreType.DMA((steps,)),
        ],
        compiler_params=params(20),
        cost_estimate=pl.CostEstimate(
            flops=flops * (NEAR * tile + 2 * clusters), bytes_accessed=16 << 20, transcendentals=rows * clusters
        ),
        name="near",
    )(
        cols, my_index.astype(i32).reshape(1), in_hbm(left), in_hbm(blocks), in_hbm(right),
        in_hbm(tile_vals), cluster_graph, on_chip(heard),
    )

    chunk = min(16, blocks_dev)
    logits, mass_parts = pl.pallas_call(
        functools.partial(far_kernel, group, chunk, nodes_total),
        out_shape=(pltpu.VMEM((rows, clusters), f32), pltpu.VMEM((shards, 1, clusters), f32)),
        in_specs=[SMEM, VMEM, ANY, ANY, VMEM],
        out_specs=(VMEM, VMEM),
        scratch_shapes=[
            pltpu.VMEM((blocks_dev, far_slots, tile, tile), bf16),
            pltpu.SemaphoreType.DMA((blocks_dev // chunk,)),
            pltpu.SemaphoreType.DMA((blocks_dev // chunk,)),
        ],
        compiler_params=params(16),
        cost_estimate=pl.CostEstimate(
            flops=flops * (far_slots * tile + 2 * clusters), bytes_accessed=8 << 20, transcendentals=rows * clusters
        ),
        name="far",
    )(where, on_chip(fetched), in_hbm(tile_vals), in_hbm(part), on_chip(graph2))

    masses = lax.all_to_all(mass_parts, NODES, split_axis=0, concat_axis=0, tiled=True)

    return pl.pallas_call(
        functools.partial(last_kernel, 8),
        out_shape=jax.ShapeDtypeStruct((rows, clusters), f32),
        in_specs=[VMEM, VMEM, VMEM],
        out_specs=ANY,
        scratch_shapes=[pltpu.VMEM((rows, clusters), f32), pltpu.SemaphoreType.DMA((8,))],
        compiler_params=params(8),
        name="last",
    )(on_chip(logits), on_chip(masses), cluster_mass.reshape(1, clusters))


def solution(mesh):
    return jax.shard_map(
        local,
        mesh=mesh,
        in_specs=(
            P(("groups", "rows", "sub"), None),
            P(("groups", "rows", "sub"), None, None, None),
            P(("groups", "rows", "sub"), None),
            P("groups", None),
            P("groups"),
        ),
        out_specs=P(("groups", "rows", "sub"), None),
        check_vma=False,
    )
```

```python
import functools

import jax
import jax.numpy as jnp
from jax import lax
from jax.experimental import pallas as pl
from jax.experimental.pallas import tpu as pltpu
from jax.sharding import PartitionSpec as P


NEAR = 4
NODES = ("rows", "sub")

eta_step = 2.0
relax_power = 0.5

ANY = pl.BlockSpec(memory_space=pl.ANY)
VMEM = pl.BlockSpec(memory_space=pltpu.VMEM)
SMEM = pl.BlockSpec(memory_space=pltpu.SMEM)

f32, bf16, i32 = jnp.float32, jnp.bfloat16, jnp.int32


def on_chip(x):
    return pltpu.with_memory_space_constraint(x, pltpu.VMEM)


def in_hbm(x):
    return pltpu.with_memory_space_constraint(x, pltpu.HBM)


def params(mib):
    return pltpu.CompilerParams(vmem_limit_bytes=mib << 20)


def requests_kernel(nodes_total, cols_ref, coupling_ref, out_ref, rows, sems):
    slots, blocks_dev = cols_ref.shape
    shards = out_ref.shape[0]
    nodes, clusters = coupling_ref.shape
    parts = sems.shape[0]
    step = nodes // parts
    copies = [
        pltpu.make_async_copy(coupling_ref.at[pl.ds(i * step, step)], rows.at[pl.ds(i * step, step)], sems.at[i])
        for i in range(parts)
    ]
    for copy in copies:
        copy.start()

    owner = lax.broadcasted_iota(i32, (shards, blocks_dev), 0)
    place = lax.broadcasted_iota(i32, (clusters, blocks_dev), 0).astype(f32)
    before = (
        lax.broadcasted_iota(i32, (blocks_dev, blocks_dev), 0)
        < lax.broadcasted_iota(i32, (blocks_dev, blocks_dev), 1)
    ).astype(f32)
    count = jnp.zeros((shards, 1), f32)
    table = jnp.zeros((shards, clusters), f32)
    for slot_id in range(NEAR, slots):
        local = cols_ref[slot_id : slot_id + 1, :] - owner * blocks_dev
        hit = (local >= 0) & (local < blocks_dev)
        hits = hit.astype(f32)
        earlier = jnp.dot(hits, before, preferred_element_type=f32) + count
        rank = jnp.sum(earlier * hits, axis=0, keepdims=True)
        count = count + jnp.sum(hits, axis=1, keepdims=True)
        wanted = jnp.where(hit, local, 0).astype(f32)
        table = table + lax.dot_general(
            wanted,
            (rank == place).astype(f32),
            (((1,), (1,)), ((), ())),
            precision=lax.Precision.HIGHEST,
            preferred_element_type=f32,
        )
    out_ref[:, 0, clusters:] = table
    total = jnp.zeros((8, clusters), f32)
    for i in range(parts):
        copies[i].wait()
        part = rows[pl.ds(i * step, step), :].astype(f32)
        total = total + jnp.sum(part.reshape(step // 8, 8, clusters), axis=0)
    mass = jnp.sum(total, axis=0, keepdims=True) / nodes_total
    out_ref[:, 0, :clusters] = jnp.broadcast_to(mass, (shards, clusters))


def gather_kernel(cap, heard_ref, blocks_ref, out_ref, wanted_ref, wanted_smem, sems):
    clusters = blocks_ref.shape[2]
    wanted_ref[...] = heard_ref[:, 0, clusters:].astype(i32)
    copy = pltpu.make_async_copy(wanted_ref, wanted_smem, sems.at[0])
    copy.start()
    copy.wait()

    @pl.loop(0, heard_ref.shape[0])
    def _(n):
        for j in range(cap):
            pltpu.make_async_copy(blocks_ref.at[wanted_smem[n, j]], out_ref.at[n * cap + j], sems.at[1]).start()

    pltpu.make_async_copy(out_ref, out_ref, sems.at[1]).wait()


def split(x):
    high = x.astype(bf16)
    return jnp.concatenate([high, (x - high.astype(f32)).astype(bf16)], axis=1)


def near_kernel(
    group, cap, middle, cols_ref, place_ref, left_ref, own_ref, right_ref, across_ref, tiles_ref, graph_ref, mass_ref,
    part_ref, graph2_ref, where_ref, window, tiles, part, pull_ref, count_ref, sems, tile_sems, part_sems,
):
    blocks_dev, tile, clusters = own_ref.shape
    slots = tiles_ref.shape[1]
    steps = blocks_dev // group
    place = place_ref[0]

    def take(src, i):
        return pltpu.make_async_copy(src, window.at[pl.ds(i * blocks_dev, blocks_dev)], sems.at[i])

    take(own_ref, 1).start()
    for i, src, at in ((0, left_ref, middle), (2, right_ref, middle - 1)):

        @pl.when(place == at)
        def _():
            take(across_ref, i).start()

        @pl.when(place != at)
        def _():
            take(src, i).start()

    def fetch(i):
        here = pl.ds(i * group, group)
        return pltpu.make_async_copy(tiles_ref.at[here, pl.ds(0, NEAR)], tiles.at[here], tile_sems.at[i])

    def store(i):
        here = pl.ds(pl.multiple_of(i * group * tile, group * tile), group * tile)
        return pltpu.make_async_copy(part.at[here], part_ref.at[here], part_sems.at[i])

    for i in range(steps):
        fetch(i).start()

    graph = graph_ref[...].astype(f32)
    colmass = jnp.sum(mass_ref[:, 0, :clusters], axis=0, keepdims=True)
    pull_ref[...] = (
        lax.dot_general(
            jnp.broadcast_to(colmass, (8, clusters)),
            graph * graph,
            (((1,), (1,)), ((), ())),
            precision=lax.Precision.HIGHEST,
            preferred_element_type=f32,
        )
        / clusters
    )
    turned = graph.T.astype(bf16)
    graph2_ref[:clusters, :] = turned
    graph2_ref[clusters:, :] = turned

    @pl.loop(0, count_ref.shape[0])
    def _(o):
        count_ref[o] = 0

    for slot_id in range(NEAR, slots):

        @pl.loop(0, blocks_dev)
        def _(b):
            owner = cols_ref[slot_id, b] // blocks_dev
            rank = count_ref[owner]
            count_ref[owner] = rank + 1
            where_ref[b * (slots - NEAR) + slot_id - NEAR] = owner * cap + rank

    for i, src in enumerate((left_ref, own_ref, right_ref)):
        take(src, i).wait()

    base = (place - 1) * blocks_dev
    scale = 2.0 * eta_step / clusters

    @pl.loop(0, steps)
    def _(step):
        fetch(step).wait()
        for i in range(group):
            b = step * group + i
            here = pl.ds(pl.multiple_of(b * tile, tile), tile)
            picked = [window[cols_ref[s, b] - base] for s in range(NEAR)]
            wide = jnp.concatenate([tiles[b, s] for s in range(NEAR)], axis=1)
            spread = jnp.dot(wide, jnp.concatenate(picked, axis=0), preferred_element_type=f32)
            affinity = jnp.dot(split(spread), graph2_ref[...], preferred_element_type=f32)
            part[here, :] = (
                jnp.log(window[blocks_dev + b].astype(f32)) - eta_step * pull_ref[0:1, :] + scale * affinity
            )
        store(step).start()

    @pl.loop(0, steps)
    def _(step):
        store(step).wait()


def far_kernel(
    group, chunk, nodes_total, where_ref, blocks_ref, tiles_ref, part_ref, graph2_ref,
    logits_ref, mass_ref, tiles, tile_sems, part_sems,
):
    tile, clusters = blocks_ref.shape[1:]
    blocks_dev, far_slots = tiles.shape[:2]
    steps = blocks_dev // group
    scale = 2.0 * eta_step / clusters

    def fetches(i):
        here = pl.ds(i * chunk, chunk)
        there = pl.ds(i * chunk * tile, chunk * tile)
        return (
            pltpu.make_async_copy(tiles_ref.at[here, pl.ds(NEAR, far_slots)], tiles.at[here], tile_sems.at[i]),
            pltpu.make_async_copy(part_ref.at[there], logits_ref.at[there], part_sems.at[i]),
        )

    for i in range(blocks_dev // chunk):
        for copy in fetches(i):
            copy.start()

    def products(step):
        first = step * group
        if first % chunk == 0:
            for copy in fetches(first // chunk):
                copy.wait()
        spreads = []
        for b in range(first, first + group):
            picked = [blocks_ref[where_ref[b * far_slots + s]] for s in range(far_slots)]
            wide = jnp.concatenate([tiles[b, s] for s in range(far_slots)], axis=1)
            spreads.append(split(jnp.dot(wide, jnp.concatenate(picked, axis=0), preferred_element_type=f32)))
        return jnp.concatenate(spreads, axis=0)

    total = jnp.zeros((8, clusters), f32)
    ahead = products(0)
    for step in range(steps):
        spreads = ahead
        if step + 1 < steps:
            ahead = products(step + 1)
        here = pl.ds(step * group * tile, group * tile)
        affinity = jnp.dot(spreads, graph2_ref[...], preferred_element_type=f32)
        logits = logits_ref[here, :] + scale * affinity
        logits_ref[here, :] = logits
        total = total + jnp.sum(jnp.exp(logits).reshape(group * tile // 8, 8, clusters), axis=0)

    mass = jnp.sum(total, axis=0, keepdims=True) / nodes_total
    mass_ref[:, 0, :] = jnp.broadcast_to(mass, (mass_ref.shape[0], clusters))


def last_kernel(parts, logits_ref, mass_ref, target_ref, out_ref, kept, sems):
    newmass = jnp.sum(mass_ref[:, 0, :], axis=0, keepdims=True)
    shift = relax_power * (jnp.log(target_ref[...]) - jnp.log(newmass))
    rows = logits_ref.shape[0]
    step = rows // parts
    copies = []
    for i in range(parts):
        here = pl.ds(i * step, step)
        shifted = logits_ref[here, :] + shift
        kept[here, :] = shifted - jnp.log(jnp.sum(jnp.exp(shifted), axis=1, keepdims=True))
        copies.append(pltpu.make_async_copy(kept.at[here], out_ref.at[here], sems.at[i]))
        copies[-1].start()
    for copy in copies:
        copy.wait()


def local(coupling, tile_vals, tile_cols, cluster_graph, cluster_mass):
    shards = lax.axis_size(NODES)
    my_index = lax.axis_index(NODES)
    blocks_dev, slots = tile_cols.shape
    tile = tile_vals.shape[2]
    rows, clusters = coupling.shape
    far_slots = slots - NEAR
    nodes_total = rows * shards
    far_count = blocks_dev * far_slots
    cap = (far_count + shards - 1) // shards
    blocks = coupling.reshape(blocks_dev, tile, clusters)
    cols = tile_cols.T
    group = 4
    steps = blocks_dev // group
    flops = 2 * rows * clusters

    middle = shards // 2
    across = lax.ppermute(blocks, NODES, [(middle - 1, middle), (middle, middle - 1)])
    left = lax.ppermute(blocks, NODES, [(i, i + 1) for i in range(shards - 1) if i + 1 != middle])
    right = lax.ppermute(blocks, NODES, [(i + 1, i) for i in range(shards - 1) if i + 1 != middle])

    asked, held = pl.pallas_call(
        functools.partial(requests_kernel, nodes_total),
        out_shape=(jax.ShapeDtypeStruct((shards, 1, 2 * clusters), f32), pltpu.VMEM((rows, clusters), bf16)),
        in_specs=[VMEM, ANY],
        out_specs=(VMEM, VMEM),
        scratch_shapes=[pltpu.SemaphoreType.DMA((8,))],
        compiler_params=params(8),
        name="requests",
    )(cols, in_hbm(coupling))
    heard = lax.all_to_all(asked, NODES, split_axis=0, concat_axis=0, tiled=True)
    found = pl.pallas_call(
        functools.partial(gather_kernel, cap),
        out_shape=pltpu.HBM((shards * cap, tile, clusters), bf16),
        in_specs=[VMEM, VMEM],
        out_specs=ANY,
        scratch_shapes=[
            pltpu.VMEM((shards, clusters), i32),
            pltpu.SMEM((shards, clusters), i32),
            pltpu.SemaphoreType.DMA((2,)),
        ],
        compiler_params=params(8),
        name="gather",
    )(on_chip(heard), on_chip(held.reshape(blocks.shape)))
    fetched = lax.all_to_all(
        found.reshape(shards, cap, tile, clusters), NODES, split_axis=0, concat_axis=0, tiled=True
    ).reshape(shards * cap, tile, clusters)

    part, graph2, where = pl.pallas_call(
        functools.partial(near_kernel, group, cap, middle),
        out_shape=(
            pltpu.HBM((rows, clusters), f32),
            pltpu.VMEM((2 * clusters, clusters), bf16),
            jax.ShapeDtypeStruct((far_count,), i32),
        ),
        in_specs=[SMEM, SMEM, ANY, ANY, ANY, ANY, ANY, VMEM, VMEM],
        out_specs=(ANY, VMEM, SMEM),
        scratch_shapes=[
            pltpu.VMEM((3 * blocks_dev, tile, clusters), bf16),
            pltpu.VMEM((blocks_dev, NEAR, tile, tile), bf16),
            pltpu.VMEM((rows, clusters), f32),
            pltpu.VMEM((8, clusters), f32),
            pltpu.SMEM((shards,), i32),
            pltpu.SemaphoreType.DMA((3,)),
            pltpu.SemaphoreType.DMA((steps,)),
            pltpu.SemaphoreType.DMA((steps,)),
        ],
        compiler_params=params(20),
        cost_estimate=pl.CostEstimate(
            flops=flops * (NEAR * tile + 2 * clusters), bytes_accessed=16 << 20, transcendentals=rows * clusters
        ),
        name="near",
    )(
        cols, my_index.astype(i32).reshape(1), in_hbm(left), in_hbm(blocks), in_hbm(right), in_hbm(across),
        in_hbm(tile_vals), cluster_graph, on_chip(heard),
    )

    chunk = min(16, blocks_dev)
    logits, mass_parts = pl.pallas_call(
        functools.partial(far_kernel, group, chunk, nodes_total),
        out_shape=(pltpu.VMEM((rows, clusters), f32), pltpu.VMEM((shards, 1, clusters), f32)),
        in_specs=[SMEM, VMEM, ANY, ANY, VMEM],
        out_specs=(VMEM, VMEM),
        scratch_shapes=[
            pltpu.VMEM((blocks_dev, far_slots, tile, tile), bf16),
            pltpu.SemaphoreType.DMA((blocks_dev // chunk,)),
            pltpu.SemaphoreType.DMA((blocks_dev // chunk,)),
        ],
        compiler_params=params(16),
        cost_estimate=pl.CostEstimate(
            flops=flops * (far_slots * tile + 2 * clusters), bytes_accessed=8 << 20, transcendentals=rows * clusters
        ),
        name="far",
    )(where, on_chip(fetched), in_hbm(tile_vals), in_hbm(part), on_chip(graph2))

    masses = lax.all_to_all(mass_parts, NODES, split_axis=0, concat_axis=0, tiled=True)

    return pl.pallas_call(
        functools.partial(last_kernel, 8),
        out_shape=jax.ShapeDtypeStruct((rows, clusters), f32),
        in_specs=[VMEM, VMEM, VMEM],
        out_specs=ANY,
        scratch_shapes=[pltpu.VMEM((rows, clusters), f32), pltpu.SemaphoreType.DMA((8,))],
        compiler_params=params(8),
        name="last",
    )(on_chip(logits), on_chip(masses), cluster_mass.reshape(1, clusters))


def solution(mesh):
    return jax.shard_map(
        local,
        mesh=mesh,
        in_specs=(
            P(("groups", "rows", "sub"), None),
            P(("groups", "rows", "sub"), None, None, None),
            P(("groups", "rows", "sub"), None),
            P("groups", None),
            P("groups"),
        ),
        out_specs=P(("groups", "rows", "sub"), None),
        check_vma=False,
    )
```

```python
import functools

import jax
import jax.numpy as jnp
from jax import lax
from jax.experimental import pallas as pl
from jax.experimental.pallas import tpu as pltpu
from jax.sharding import PartitionSpec as P


NEAR = 4
LEVEL = 4
NODES = ("rows", "sub")

eta_step = 2.0
relax_power = 0.5

ANY = pl.BlockSpec(memory_space=pl.ANY)
VMEM = pl.BlockSpec(memory_space=pltpu.VMEM)
SMEM = pl.BlockSpec(memory_space=pltpu.SMEM)

f32, bf16, i32 = jnp.float32, jnp.bfloat16, jnp.int32


def on_chip(x):
    return pltpu.with_memory_space_constraint(x, pltpu.VMEM)


def in_hbm(x):
    return pltpu.with_memory_space_constraint(x, pltpu.HBM)


def params(mib):
    return pltpu.CompilerParams(vmem_limit_bytes=mib << 20)


def requests_kernel(nodes_total, place_ref, cols_ref, coupling_ref, *refs):
    *out_refs, own_ref, rows, table_ref, sems = refs
    slots, blocks_dev = cols_ref.shape
    shards = table_ref.shape[0]
    nodes, clusters = coupling_ref.shape
    parts = sems.shape[0]
    step = nodes // parts
    copies = [
        pltpu.make_async_copy(coupling_ref.at[pl.ds(i * step, step)], rows.at[pl.ds(i * step, step)], sems.at[i])
        for i in range(parts)
    ]
    for copy in copies:
        copy.start()

    owner = lax.broadcasted_iota(i32, (shards, blocks_dev), 0)
    place = lax.broadcasted_iota(i32, (clusters, blocks_dev), 0).astype(f32)
    before = (
        lax.broadcasted_iota(i32, (blocks_dev, blocks_dev), 0)
        < lax.broadcasted_iota(i32, (blocks_dev, blocks_dev), 1)
    ).astype(f32)
    count = jnp.zeros((shards, 1), f32)
    table = jnp.zeros((shards, clusters), f32)
    for slot_id in range(NEAR, slots):
        local = cols_ref[slot_id : slot_id + 1, :] - owner * blocks_dev
        hit = (local >= 0) & (local < blocks_dev)
        hits = hit.astype(f32)
        earlier = jnp.dot(hits, before, preferred_element_type=f32) + count
        rank = jnp.sum(earlier * hits, axis=0, keepdims=True)
        count = count + jnp.sum(hits, axis=1, keepdims=True)
        wanted = jnp.where(hit, local, 0).astype(f32)
        table = table + lax.dot_general(
            wanted,
            (rank == place).astype(f32),
            (((1,), (1,)), ((), ())),
            precision=lax.Precision.HIGHEST,
            preferred_element_type=f32,
        )
    table_ref[:, 0, :] = table
    level = place_ref[0] // LEVEL
    for dz, ref in enumerate((own_ref, *out_refs)):
        for row in range(LEVEL):
            ref[row] = table_ref[(level ^ dz) * LEVEL + row]
    total = jnp.zeros((8, clusters), f32)
    for i in range(parts):
        copies[i].wait()
        part = rows[pl.ds(i * step, step), :].astype(f32)
        total = total + jnp.sum(part.reshape(step // 8, 8, clusters), axis=0)
    mass = jnp.sum(total, axis=0, keepdims=True) / nodes_total
    for ref in (own_ref, *out_refs):
        ref[LEVEL] = mass


def gather_kernel(cap, stage, place_ref, *refs):
    count = (len(refs) - 5) // 2
    heard_refs, sources, out_refs = refs[:count], refs[count : count + 2], refs[count + 2 : 2 * count + 2]
    wanted_ref, wanted_smem, sems = refs[2 * count + 2 :]
    for n, heard in enumerate(heard_refs):
        wanted_ref[n * 8 : n * 8 + LEVEL, :] = heard[:LEVEL, 0, :].astype(i32)
    copy = pltpu.make_async_copy(wanted_ref, wanted_smem, sems.at[0])
    copy.start()
    copy.wait()
    spot = place_ref[0] % LEVEL
    for n, out_ref in enumerate(out_refs):
        for sub, src in enumerate(sources):
            row = n * 8 + (spot ^ (2 * stage + sub))
            for j in range(cap):
                pltpu.make_async_copy(src.at[wanted_smem[row, j]], out_ref.at[sub * cap + j], sems.at[n + 1]).start()
    for n, out_ref in enumerate(out_refs):
        pltpu.make_async_copy(out_ref, out_ref, sems.at[n + 1]).wait()


def split(x):
    high = x.astype(bf16)
    return jnp.concatenate([high, (x - high.astype(f32)).astype(bf16)], axis=1)


def near_kernel(
    group, cap, shards, place_ref, cols_ref, own_ref, chip_ref, level_ref, beyond_ref, across_ref, tiles_ref, graph_ref,
    *refs,
):
    *mass_refs, part_ref, graph2_ref, where_ref = refs[:-9]
    window, tiles, part, pull_ref, count_ref, own_sem, sems, tile_sems, part_sems = refs[-9:]
    blocks_dev, tile, clusters = own_ref.shape
    slots = tiles_ref.shape[1]
    steps = blocks_dev // group
    place = place_ref[0]
    spot, level = place % LEVEL, place // LEVEL

    def take(src, i, sem):
        return pltpu.make_async_copy(src, window.at[pl.ds(i * blocks_dev, blocks_dev)], sem)

    take(own_ref, 1, own_sem).start()
    even = spot % 2 == 0
    middle = shards // 2
    split_here = (place == middle) | (place == middle - 1)
    edge = ((spot == 0) | (spot == LEVEL - 1)) & jnp.logical_not(split_here)
    inside = (spot != 0) & (spot != LEVEL - 1)
    for flag, src in ((split_here, across_ref), (edge, beyond_ref), (inside, level_ref)):
        for is_even, chip_at, other_at in ((True, 2, 0), (False, 0, 2)):

            @pl.when(flag & (even == is_even))
            def _():
                take(chip_ref, chip_at, sems.at[0]).start()
                take(src, other_at, sems.at[1]).start()

    def fetch(i):
        here = pl.ds(i * group, group)
        return pltpu.make_async_copy(tiles_ref.at[here, pl.ds(0, NEAR)], tiles.at[here], tile_sems.at[i])

    def store(i):
        here = pl.ds(pl.multiple_of(i * group * tile, group * tile), group * tile)
        return pltpu.make_async_copy(part.at[here], part_ref.at[here], part_sems.at[i])

    for i in range(steps):
        fetch(i).start()

    graph = graph_ref[...].astype(f32)
    colmass = mass_refs[0][...]
    for ref in mass_refs[1:]:
        colmass = colmass + ref[...]
    pull_ref[...] = (
        lax.dot_general(
            jnp.broadcast_to(colmass, (8, clusters)),
            graph * graph,
            (((1,), (1,)), ((), ())),
            precision=lax.Precision.HIGHEST,
            preferred_element_type=f32,
        )
        / clusters
    )
    turned = graph.T.astype(bf16)
    graph2_ref[:clusters, :] = turned
    graph2_ref[clusters:, :] = turned

    @pl.loop(0, count_ref.shape[0])
    def _(o):
        count_ref[o] = 0

    for slot_id in range(NEAR, slots):

        @pl.loop(0, blocks_dev)
        def _(b):
            owner = cols_ref[slot_id, b] // blocks_dev
            rank = count_ref[owner]
            count_ref[owner] = rank + 1
            turn = (owner % LEVEL) ^ spot
            row = ((turn // 2) * (shards // LEVEL) + ((owner // LEVEL) ^ level)) * 2 + turn % 2
            where_ref[b * (slots - NEAR) + slot_id - NEAR] = row * cap + rank

    take(own_ref, 1, own_sem).wait()
    take(chip_ref, 0, sems.at[0]).wait()
    take(chip_ref, 2, sems.at[1]).wait()

    base = (place - 1) * blocks_dev
    scale = 2.0 * eta_step / clusters

    @pl.loop(0, steps)
    def _(step):
        fetch(step).wait()
        for i in range(group):
            b = step * group + i
            here = pl.ds(pl.multiple_of(b * tile, tile), tile)
            picked = [window[cols_ref[s, b] - base] for s in range(NEAR)]
            wide = jnp.concatenate([tiles[b, s] for s in range(NEAR)], axis=1)
            spread = jnp.dot(wide, jnp.concatenate(picked, axis=0), preferred_element_type=f32)
            affinity = jnp.dot(split(spread), graph2_ref[...], preferred_element_type=f32)
            part[here, :] = (
                jnp.log(window[blocks_dev + b].astype(f32)) - eta_step * pull_ref[0:1, :] + scale * affinity
            )
        store(step).start()

    @pl.loop(0, steps)
    def _(step):
        store(step).wait()


def far_kernel(
    group, chunk, nodes_total, where_ref, tiles_ref, part_ref, graph2_ref, *refs
):
    *found_refs, logits_ref, mass_ref = refs[:-5]
    blocks_ref, tiles, block_sem, tile_sems, part_sems = refs[-5:]
    tile, clusters = blocks_ref.shape[1:]
    blocks_dev, far_slots = tiles.shape[:2]
    steps = blocks_dev // group
    scale = 2.0 * eta_step / clusters
    width = found_refs[0].shape[0]
    for i, found in enumerate(found_refs):
        pltpu.make_async_copy(found, blocks_ref.at[pl.ds(i * width, width)], block_sem).start()

    def fetches(i):
        here = pl.ds(i * chunk, chunk)
        there = pl.ds(i * chunk * tile, chunk * tile)
        return (
            pltpu.make_async_copy(tiles_ref.at[here, pl.ds(NEAR, far_slots)], tiles.at[here], tile_sems.at[i]),
            pltpu.make_async_copy(part_ref.at[there], logits_ref.at[there], part_sems.at[i]),
        )

    for i in range(blocks_dev // chunk):
        for copy in fetches(i):
            copy.start()

    def products(step):
        first = step * group
        if first % chunk == 0:
            for copy in fetches(first // chunk):
                copy.wait()
        spreads = []
        for b in range(first, first + group):
            picked = [blocks_ref[where_ref[b * far_slots + s]] for s in range(far_slots)]
            wide = jnp.concatenate([tiles[b, s] for s in range(far_slots)], axis=1)
            spreads.append(split(jnp.dot(wide, jnp.concatenate(picked, axis=0), preferred_element_type=f32)))
        return jnp.concatenate(spreads, axis=0)

    pltpu.make_async_copy(blocks_ref, blocks_ref, block_sem).wait()
    total = jnp.zeros((8, clusters), f32)
    ahead = products(0)
    for step in range(steps):
        spreads = ahead
        if step + 1 < steps:
            ahead = products(step + 1)
        here = pl.ds(step * group * tile, group * tile)
        affinity = jnp.dot(spreads, graph2_ref[...], preferred_element_type=f32)
        logits = logits_ref[here, :] + scale * affinity
        logits_ref[here, :] = logits
        total = total + jnp.sum(jnp.exp(logits).reshape(group * tile // 8, 8, clusters), axis=0)

    mass = jnp.sum(total, axis=0, keepdims=True) / nodes_total
    mass_ref[:, 0, :] = jnp.broadcast_to(mass, (mass_ref.shape[0], clusters))


def last_kernel(parts, logits_ref, mass_ref, target_ref, out_ref, kept, sems):
    newmass = jnp.sum(mass_ref[:, 0, :], axis=0, keepdims=True)
    shift = relax_power * (jnp.log(target_ref[...]) - jnp.log(newmass))
    rows = logits_ref.shape[0]
    step = rows // parts
    copies = []
    for i in range(parts):
        here = pl.ds(i * step, step)
        shifted = logits_ref[here, :] + shift
        kept[here, :] = shifted - jnp.log(jnp.sum(jnp.exp(shifted), axis=1, keepdims=True))
        copies.append(pltpu.make_async_copy(kept.at[here], out_ref.at[here], sems.at[i]))
        copies[-1].start()
    for copy in copies:
        copy.wait()


def local(coupling, tile_vals, tile_cols, cluster_graph, cluster_mass):
    shards = lax.axis_size(NODES)
    my_index = lax.axis_index(NODES)
    blocks_dev, slots = tile_cols.shape
    tile = tile_vals.shape[2]
    rows, clusters = coupling.shape
    far_slots = slots - NEAR
    nodes_total = rows * shards
    far_count = blocks_dev * far_slots
    cap = (far_count + shards - 1) // shards
    blocks = coupling.reshape(blocks_dev, tile, clusters)
    cols = tile_cols.T
    group = 4
    steps = blocks_dev // group
    flops = 2 * rows * clusters

    levels = shards // LEVEL
    others = range(1, levels)
    place = my_index.astype(i32).reshape(1)

    def swap(x, bits):
        return lax.ppermute(x, NODES, [(i, i ^ bits) for i in range(shards)])

    middle = shards // 2
    across = lax.ppermute(blocks, NODES, [(middle - 1, middle), (middle, middle - 1)])

    *asked, mine, held = pl.pallas_call(
        functools.partial(requests_kernel, nodes_total),
        out_shape=(
            *[pltpu.VMEM((LEVEL + 1, 1, clusters), f32)] * levels,
            pltpu.VMEM((rows, clusters), bf16),
        ),
        in_specs=[SMEM, VMEM, ANY],
        out_specs=[VMEM] * (levels + 1),
        scratch_shapes=[pltpu.VMEM((shards, 1, clusters), f32), pltpu.SemaphoreType.DMA((8,))],
        compiler_params=params(8),
        name="requests",
    )(place, cols, in_hbm(coupling))
    heard = [swap(x, dz * LEVEL) for dz, x in zip(others, asked)]
    over = swap(blocks, 2)
    chip = swap(blocks, 1)

    def gather(stage, heard, sources):
        return pl.pallas_call(
            functools.partial(gather_kernel, cap, stage),
            out_shape=[pltpu.HBM((2 * cap, tile, clusters), bf16)] * len(heard),
            in_specs=[SMEM] + [VMEM] * (len(heard) + 2),
            out_specs=[ANY] * len(heard),
            scratch_shapes=[
                pltpu.VMEM((8 * len(heard), clusters), i32),
                pltpu.SMEM((8 * len(heard), clusters), i32),
                pltpu.SemaphoreType.DMA((len(heard) + 1,)),
            ],
            compiler_params=params(8),
        )(place, *[on_chip(x) for x in heard], *[on_chip(x) for x in sources])

    found = gather(0, heard, (held.reshape(blocks.shape), chip))
    fetched = [swap(x, dz * LEVEL) for dz, x in zip(others, found)]
    over_chip = swap(over, 1)
    edges = [z * LEVEL for z in range(1, levels) if z * LEVEL != middle]
    beyond = lax.ppermute(over, NODES, [(i - LEVEL + 1, i) for i in edges] + [(i + LEVEL - 2, i - 1) for i in edges])
    found = gather(1, (*heard, mine), (over, over_chip))
    there = [swap(x, dz * LEVEL) for dz, x in zip(others, found)]
    home_late = found[-1]
    (home,) = gather(0, (mine,), (held.reshape(blocks.shape), chip))

    mass = mine[LEVEL]
    for x in heard:
        mass = mass + x[LEVEL]
    mass_chip = swap(mass, 1)
    mass = mass + mass_chip
    mass_over = swap(mass, 2)

    part, graph2, where = pl.pallas_call(
        functools.partial(near_kernel, group, cap, shards),
        out_shape=(
            pltpu.HBM((rows, clusters), f32),
            pltpu.VMEM((2 * clusters, clusters), bf16),
            jax.ShapeDtypeStruct((far_count,), i32),
        ),
        in_specs=[SMEM, SMEM, ANY, ANY, ANY, ANY, ANY, ANY, VMEM, VMEM, VMEM],
        out_specs=(ANY, VMEM, SMEM),
        scratch_shapes=[
            pltpu.VMEM((3 * blocks_dev, tile, clusters), bf16),
            pltpu.VMEM((blocks_dev, NEAR, tile, tile), bf16),
            pltpu.VMEM((rows, clusters), f32),
            pltpu.VMEM((8, clusters), f32),
            pltpu.SMEM((shards,), i32),
            pltpu.SemaphoreType.DMA,
            pltpu.SemaphoreType.DMA((2,)),
            pltpu.SemaphoreType.DMA((steps,)),
            pltpu.SemaphoreType.DMA((steps,)),
        ],
        compiler_params=params(20),
        cost_estimate=pl.CostEstimate(
            flops=flops * (NEAR * tile + 2 * clusters), bytes_accessed=16 << 20, transcendentals=rows * clusters
        ),
        name="near",
    )(
        place, cols, in_hbm(blocks), in_hbm(chip), in_hbm(over_chip), in_hbm(beyond), in_hbm(across),
        in_hbm(tile_vals), cluster_graph, mass, mass_over,
    )

    chunk = min(16, blocks_dev)
    parts = [home, *fetched, home_late, *there]
    logits, mass_parts = pl.pallas_call(
        functools.partial(far_kernel, group, chunk, nodes_total),
        out_shape=(pltpu.VMEM((rows, clusters), f32), pltpu.VMEM((shards, 1, clusters), f32)),
        in_specs=[SMEM, ANY, ANY, VMEM] + [ANY] * len(parts),
        out_specs=(VMEM, VMEM),
        scratch_shapes=[
            pltpu.VMEM((2 * cap * len(parts), tile, clusters), bf16),
            pltpu.VMEM((blocks_dev, far_slots, tile, tile), bf16),
            pltpu.SemaphoreType.DMA,
            pltpu.SemaphoreType.DMA((blocks_dev // chunk,)),
            pltpu.SemaphoreType.DMA((blocks_dev // chunk,)),
        ],
        compiler_params=params(16),
        cost_estimate=pl.CostEstimate(
            flops=flops * (far_slots * tile + 2 * clusters), bytes_accessed=8 << 20, transcendentals=rows * clusters
        ),
        name="far",
    )(where, in_hbm(tile_vals), in_hbm(part), on_chip(graph2), *parts)

    masses = lax.all_to_all(mass_parts, NODES, split_axis=0, concat_axis=0, tiled=True)

    return pl.pallas_call(
        functools.partial(last_kernel, 8),
        out_shape=jax.ShapeDtypeStruct((rows, clusters), f32),
        in_specs=[VMEM, VMEM, VMEM],
        out_specs=ANY,
        scratch_shapes=[pltpu.VMEM((rows, clusters), f32), pltpu.SemaphoreType.DMA((8,))],
        compiler_params=params(8),
        name="last",
    )(on_chip(logits), on_chip(masses), cluster_mass.reshape(1, clusters))


def solution(mesh):
    return jax.shard_map(
        local,
        mesh=mesh,
        in_specs=(
            P(("groups", "rows", "sub"), None),
            P(("groups", "rows", "sub"), None, None, None),
            P(("groups", "rows", "sub"), None),
            P("groups", None),
            P("groups"),
        ),
        out_specs=P(("groups", "rows", "sub"), None),
        check_vma=False,
    )
```

```python
import functools

import jax
import jax.numpy as jnp
from jax import lax
from jax.experimental import pallas as pl
from jax.experimental.pallas import tpu as pltpu
from jax.sharding import PartitionSpec as P


NEAR = 4
LEVEL = 4
NODES = ("rows", "sub")

eta_step = 2.0
relax_power = 0.5

ANY = pl.BlockSpec(memory_space=pl.ANY)
VMEM = pl.BlockSpec(memory_space=pltpu.VMEM)
SMEM = pl.BlockSpec(memory_space=pltpu.SMEM)

f32, bf16, i32 = jnp.float32, jnp.bfloat16, jnp.int32


def on_chip(x):
    return pltpu.with_memory_space_constraint(x, pltpu.VMEM)


def in_hbm(x):
    return pltpu.with_memory_space_constraint(x, pltpu.HBM)


def params(mib):
    return pltpu.CompilerParams(vmem_limit_bytes=mib << 20)


def requests_kernel(nodes_total, place_ref, all_cols_ref, coupling_ref, *refs):
    *out_refs, own_ref, rows, cols_ref, table_ref, cols_sem, sems = refs
    slots, blocks_dev = cols_ref.shape
    cols_copy = pltpu.make_async_copy(all_cols_ref, cols_ref, cols_sem)
    cols_copy.start()
    shards = table_ref.shape[0]
    nodes, clusters = coupling_ref.shape
    parts = sems.shape[0]
    step = nodes // parts
    copies = [
        pltpu.make_async_copy(coupling_ref.at[pl.ds(i * step, step)], rows.at[pl.ds(i * step, step)], sems.at[i])
        for i in range(parts)
    ]
    for copy in copies:
        copy.start()

    owner = lax.broadcasted_iota(i32, (shards, blocks_dev), 0)
    place = lax.broadcasted_iota(i32, (clusters, blocks_dev), 0).astype(f32)
    before = (
        lax.broadcasted_iota(i32, (blocks_dev, blocks_dev), 0)
        < lax.broadcasted_iota(i32, (blocks_dev, blocks_dev), 1)
    ).astype(f32)
    count = jnp.zeros((shards, 1), f32)
    table = jnp.zeros((shards, clusters), f32)
    cols_copy.wait()
    for slot_id in range(NEAR, slots):
        local = cols_ref[slot_id : slot_id + 1, :] - owner * blocks_dev
        hit = (local >= 0) & (local < blocks_dev)
        hits = hit.astype(f32)
        earlier = jnp.dot(hits, before, preferred_element_type=f32) + count
        rank = jnp.sum(earlier * hits, axis=0, keepdims=True)
        count = count + jnp.sum(hits, axis=1, keepdims=True)
        wanted = jnp.where(hit, local, 0).astype(f32)
        table = table + lax.dot_general(
            wanted,
            (rank == place).astype(f32),
            (((1,), (1,)), ((), ())),
            precision=lax.Precision.HIGHEST,
            preferred_element_type=f32,
        )
    table_ref[:, 0, :] = table
    level = place_ref[0] // LEVEL
    for dz, ref in enumerate((own_ref, *out_refs)):
        for row in range(LEVEL):
            ref[row] = table_ref[(level ^ dz) * LEVEL + row]
    total = jnp.zeros((8, clusters), f32)
    for i in range(parts):
        copies[i].wait()
        part = rows[pl.ds(i * step, step), :].astype(f32)
        total = total + jnp.sum(part.reshape(step // 8, 8, clusters), axis=0)
    mass = jnp.sum(total, axis=0, keepdims=True) / nodes_total
    for ref in (own_ref, *out_refs):
        ref[LEVEL] = mass


def gather_kernel(cap, stage, place_ref, *refs):
    count = (len(refs) - 5) // 2
    heard_refs, sources, out_refs = refs[:count], refs[count : count + 2], refs[count + 2 : 2 * count + 2]
    wanted_ref, wanted_smem, sems = refs[2 * count + 2 :]
    for n, heard in enumerate(heard_refs):
        wanted_ref[n * 8 : n * 8 + LEVEL, :] = heard[:LEVEL, 0, :].astype(i32)
    copy = pltpu.make_async_copy(wanted_ref, wanted_smem, sems.at[0])
    copy.start()
    copy.wait()
    spot = place_ref[0] % LEVEL
    for n, out_ref in enumerate(out_refs):
        for sub, src in enumerate(sources):
            row = n * 8 + (spot ^ (2 * stage + sub))
            for j in range(cap):
                pltpu.make_async_copy(src.at[wanted_smem[row, j]], out_ref.at[sub * cap + j], sems.at[n + 1]).start()
    for n, out_ref in enumerate(out_refs):
        pltpu.make_async_copy(out_ref, out_ref, sems.at[n + 1]).wait()


def split(x):
    high = x.astype(bf16)
    return jnp.concatenate([high, (x - high.astype(f32)).astype(bf16)], axis=1)


def prep_kernel(cap, shards, place_ref, cols_ref, graph_ref, *refs):
    *mass_refs, graph2_ref, pull_ref, where_ref, count_ref = refs
    slots, blocks_dev = cols_ref.shape
    clusters = graph_ref.shape[0]
    spot, level = place_ref[0] % LEVEL, place_ref[0] // LEVEL
    graph = graph_ref[...].astype(f32)
    colmass = mass_refs[0][...]
    for ref in mass_refs[1:]:
        colmass = colmass + ref[...]
    pull_ref[...] = (
        lax.dot_general(
            jnp.broadcast_to(colmass, (8, clusters)),
            graph * graph,
            (((1,), (1,)), ((), ())),
            precision=lax.Precision.HIGHEST,
            preferred_element_type=f32,
        )
        / clusters
    )
    turned = graph.T.astype(bf16)
    graph2_ref[:clusters, :] = turned
    graph2_ref[clusters:, :] = turned

    @pl.loop(0, shards)
    def _(o):
        count_ref[o] = 0

    for slot_id in range(NEAR, slots):

        @pl.loop(0, blocks_dev)
        def _(b):
            owner = cols_ref[slot_id, b] // blocks_dev
            rank = count_ref[owner]
            count_ref[owner] = rank + 1
            turn = (owner % LEVEL) ^ spot
            row = ((turn // 2) * (shards // LEVEL) + ((owner // LEVEL) ^ level)) * 2 + turn % 2
            where_ref[b * (slots - NEAR) + slot_id - NEAR] = row * cap + rank


def near_kernel(
    group, chunk, shards, place_ref, cols_ref, own_ref, chip_ref, level_ref, beyond_ref, across_ref, tiles_ref,
    graph2_ref, pull_ref, part_ref, window, tiles, part, own_sem, sems, tile_sems, part_sems,
):
    blocks_dev, tile, clusters = own_ref.shape
    steps = blocks_dev // group
    place = place_ref[0]
    spot = place % LEVEL

    def take(src, i, sem):
        return pltpu.make_async_copy(src, window.at[pl.ds(i * blocks_dev, blocks_dev)], sem)

    take(own_ref, 1, own_sem).start()
    even = spot % 2 == 0
    middle = shards // 2
    split_here = (place == middle) | (place == middle - 1)
    edge = ((spot == 0) | (spot == LEVEL - 1)) & jnp.logical_not(split_here)
    inside = (spot != 0) & (spot != LEVEL - 1)
    for flag, src in ((split_here, across_ref), (edge, beyond_ref), (inside, level_ref)):
        for is_even, chip_at, other_at in ((True, 2, 0), (False, 0, 2)):

            @pl.when(flag & (even == is_even))
            def _():
                take(chip_ref, chip_at, sems.at[0]).start()
                take(src, other_at, sems.at[1]).start()

    def fetch(i):
        here = pl.ds(i * chunk, chunk)
        return pltpu.make_async_copy(tiles_ref.at[here, pl.ds(0, NEAR)], tiles.at[here], tile_sems.at[i])

    def store(i):
        here = pl.ds(i * chunk * tile, chunk * tile)
        return pltpu.make_async_copy(part.at[here], part_ref.at[here], part_sems.at[i])

    for i in range(blocks_dev // chunk):
        fetch(i).start()
    take(own_ref, 1, own_sem).wait()
    take(chip_ref, 0, sems.at[0]).wait()
    take(chip_ref, 2, sems.at[1]).wait()

    base = (place - 1) * blocks_dev
    scale = 2.0 * eta_step / clusters

    def products(step):
        first = step * group
        if first % chunk == 0:
            fetch(first // chunk).wait()
        spreads = []
        for b in range(first, first + group):
            picked = [window[cols_ref[s, b] - base] for s in range(NEAR)]
            wide = jnp.concatenate([tiles[b, s] for s in range(NEAR)], axis=1)
            spreads.append(split(jnp.dot(wide, jnp.concatenate(picked, axis=0), preferred_element_type=f32)))
        return jnp.concatenate(spreads, axis=0)

    ahead = products(0)
    for step in range(steps):
        spreads = ahead
        if step + 1 < steps:
            ahead = products(step + 1)
        first = step * group
        affinity = jnp.dot(spreads, graph2_ref[...], preferred_element_type=f32)
        own = window[blocks_dev + first : blocks_dev + first + group].reshape(group * tile, clusters)
        part[first * tile : (first + group) * tile, :] = (
            jnp.log(own.astype(f32)) - eta_step * pull_ref[0:1, :] + scale * affinity
        )
        if (first + group) % chunk == 0:
            store(first // chunk).start()
    for i in range(blocks_dev // chunk):
        store(i).wait()


def far_kernel(
    group, chunk, nodes_total, where_ref, tiles_ref, part_ref, graph2_ref, *refs
):
    *found_refs, logits_ref, mass_ref = refs[:-5]
    blocks_ref, tiles, block_sem, tile_sems, part_sems = refs[-5:]
    tile, clusters = blocks_ref.shape[1:]
    blocks_dev, far_slots = tiles.shape[:2]
    steps = blocks_dev // group
    scale = 2.0 * eta_step / clusters
    width = found_refs[0].shape[0]
    for i, found in enumerate(found_refs):
        pltpu.make_async_copy(found, blocks_ref.at[pl.ds(i * width, width)], block_sem).start()

    def fetches(i):
        here = pl.ds(i * chunk, chunk)
        there = pl.ds(i * chunk * tile, chunk * tile)
        return (
            pltpu.make_async_copy(tiles_ref.at[here, pl.ds(NEAR, far_slots)], tiles.at[here], tile_sems.at[i]),
            pltpu.make_async_copy(part_ref.at[there], logits_ref.at[there], part_sems.at[i]),
        )

    for i in range(blocks_dev // chunk):
        for copy in fetches(i):
            copy.start()

    def products(step):
        first = step * group
        if first % chunk == 0:
            for copy in fetches(first // chunk):
                copy.wait()
        spreads = []
        for b in range(first, first + group):
            picked = [blocks_ref[where_ref[b * far_slots + s]] for s in range(far_slots)]
            wide = jnp.concatenate([tiles[b, s] for s in range(far_slots)], axis=1)
            spreads.append(split(jnp.dot(wide, jnp.concatenate(picked, axis=0), preferred_element_type=f32)))
        return jnp.concatenate(spreads, axis=0)

    pltpu.make_async_copy(blocks_ref, blocks_ref, block_sem).wait()
    total = jnp.zeros((8, clusters), f32)
    ahead = products(0)
    for step in range(steps):
        spreads = ahead
        if step + 1 < steps:
            ahead = products(step + 1)
        here = pl.ds(step * group * tile, group * tile)
        affinity = jnp.dot(spreads, graph2_ref[...], preferred_element_type=f32)
        logits = logits_ref[here, :] + scale * affinity
        logits_ref[here, :] = logits
        total = total + jnp.sum(jnp.exp(logits).reshape(group * tile // 8, 8, clusters), axis=0)

    mass = jnp.sum(total, axis=0, keepdims=True) / nodes_total
    mass_ref[:, 0, :] = jnp.broadcast_to(mass, (mass_ref.shape[0], clusters))


def last_kernel(parts, logits_ref, mass_ref, target_ref, out_ref, kept, sems):
    newmass = jnp.sum(mass_ref[:, 0, :], axis=0, keepdims=True)
    shift = relax_power * (jnp.log(target_ref[...]) - jnp.log(newmass))
    rows = logits_ref.shape[0]
    step = rows // parts
    copies = []
    for i in range(parts):
        here = pl.ds(i * step, step)
        shifted = logits_ref[here, :] + shift
        kept[here, :] = shifted - jnp.log(jnp.sum(jnp.exp(shifted), axis=1, keepdims=True))
        copies.append(pltpu.make_async_copy(kept.at[here], out_ref.at[here], sems.at[i]))
        copies[-1].start()
    for copy in copies:
        copy.wait()


def local(coupling, tile_vals, tile_cols, cluster_graph, cluster_mass):
    shards = lax.axis_size(NODES)
    my_index = lax.axis_index(NODES)
    blocks_dev, slots = tile_cols.shape
    tile = tile_vals.shape[2]
    rows, clusters = coupling.shape
    far_slots = slots - NEAR
    nodes_total = rows * shards
    far_count = blocks_dev * far_slots
    cap = (far_count + shards - 1) // shards
    blocks = coupling.reshape(blocks_dev, tile, clusters)
    cols = tile_cols.T
    group = 4
    steps = blocks_dev // group
    flops = 2 * rows * clusters

    levels = shards // LEVEL
    others = range(1, levels)
    place = my_index.astype(i32).reshape(1)

    def swap(x, bits):
        return lax.ppermute(x, NODES, [(i, i ^ bits) for i in range(shards)])

    middle = shards // 2
    over = swap(blocks, 2)
    chip = swap(blocks, 1)
    across = lax.ppermute(blocks, NODES, [(middle - 1, middle + 2), (middle, middle - 3)])

    *asked, mine, held = pl.pallas_call(
        functools.partial(requests_kernel, nodes_total),
        out_shape=(
            *[pltpu.VMEM((LEVEL + 1, 1, clusters), f32)] * levels,
            pltpu.VMEM((rows, clusters), bf16),
        ),
        in_specs=[SMEM, ANY, ANY],
        out_specs=[VMEM] * (levels + 1),
        scratch_shapes=[
            pltpu.VMEM((slots, blocks_dev), i32),
            pltpu.VMEM((shards, 1, clusters), f32),
            pltpu.SemaphoreType.DMA,
            pltpu.SemaphoreType.DMA((8,)),
        ],
        compiler_params=params(8),
        name="requests",
    )(place, in_hbm(cols), in_hbm(coupling))
    heard = [swap(x, dz * LEVEL) for dz, x in zip(others, asked)]

    def gather(stage, heard, sources):
        return pl.pallas_call(
            functools.partial(gather_kernel, cap, stage),
            out_shape=[pltpu.HBM((2 * cap, tile, clusters), bf16)] * len(heard),
            in_specs=[SMEM] + [VMEM] * (len(heard) + 2),
            out_specs=[ANY] * len(heard),
            scratch_shapes=[
                pltpu.VMEM((8 * len(heard), clusters), i32),
                pltpu.SMEM((8 * len(heard), clusters), i32),
                pltpu.SemaphoreType.DMA((len(heard) + 1,)),
            ],
            compiler_params=params(8),
        )(place, *[on_chip(x) for x in heard], *[on_chip(x) for x in sources])

    found = gather(0, heard, (held.reshape(blocks.shape), chip))
    fetched = [swap(x, dz * LEVEL) for dz, x in zip(others, found)]
    over_chip = swap(over, 1)
    edges = [z * LEVEL for z in range(1, levels) if z * LEVEL != middle]
    beyond = lax.ppermute(over, NODES, [(i - LEVEL + 1, i) for i in edges] + [(i + LEVEL - 2, i - 1) for i in edges])
    across = lax.ppermute(across, NODES, [(middle + 2, middle), (middle - 3, middle - 1)])
    found = gather(1, (*heard, mine), (over, over_chip))
    there = [swap(x, dz * LEVEL) for dz, x in zip(others, found)]
    home_late = found[-1]
    (home,) = gather(0, (mine,), (held.reshape(blocks.shape), chip))

    mass = mine[LEVEL]
    for x in heard:
        mass = mass + x[LEVEL]
    mass_chip = swap(mass, 1)
    mass = mass + mass_chip
    mass_over = swap(mass, 2)

    graph2, pull, where = pl.pallas_call(
        functools.partial(prep_kernel, cap, shards),
        out_shape=(
            pltpu.VMEM((2 * clusters, clusters), bf16),
            pltpu.VMEM((8, clusters), f32),
            jax.ShapeDtypeStruct((far_count,), i32),
        ),
        in_specs=[SMEM, SMEM, VMEM, VMEM, VMEM],
        out_specs=(VMEM, VMEM, SMEM),
        scratch_shapes=[pltpu.SMEM((shards,), i32)],
        compiler_params=params(4),
        name="prep",
    )(place, cols, cluster_graph, mass, mass_over)

    chunk = min(16, blocks_dev)
    part = pl.pallas_call(
        functools.partial(near_kernel, group, group, shards),
        out_shape=pltpu.HBM((rows, clusters), f32),
        in_specs=[SMEM, SMEM, ANY, ANY, ANY, ANY, ANY, ANY, VMEM, VMEM],
        out_specs=ANY,
        scratch_shapes=[
            pltpu.VMEM((3 * blocks_dev, tile, clusters), bf16),
            pltpu.VMEM((blocks_dev, NEAR, tile, tile), bf16),
            pltpu.VMEM((rows, clusters), f32),
            pltpu.SemaphoreType.DMA,
            pltpu.SemaphoreType.DMA((2,)),
            pltpu.SemaphoreType.DMA((steps,)),
            pltpu.SemaphoreType.DMA((steps,)),
        ],
        compiler_params=params(20),
        cost_estimate=pl.CostEstimate(
            flops=flops * (NEAR * tile + 2 * clusters), bytes_accessed=16 << 20, transcendentals=rows * clusters
        ),
        name="near",
    )(place, cols, in_hbm(blocks), chip, over_chip, beyond, across, in_hbm(tile_vals), on_chip(graph2), on_chip(pull))

    parts = [home, *fetched, home_late, *there]
    logits, mass_parts = pl.pallas_call(
        functools.partial(far_kernel, group, chunk, nodes_total),
        out_shape=(pltpu.VMEM((rows, clusters), f32), pltpu.VMEM((shards, 1, clusters), f32)),
        in_specs=[SMEM, ANY, ANY, VMEM] + [ANY] * len(parts),
        out_specs=(VMEM, VMEM),
        scratch_shapes=[
            pltpu.VMEM((2 * cap * len(parts), tile, clusters), bf16),
            pltpu.VMEM((blocks_dev, far_slots, tile, tile), bf16),
            pltpu.SemaphoreType.DMA,
            pltpu.SemaphoreType.DMA((blocks_dev // chunk,)),
            pltpu.SemaphoreType.DMA((blocks_dev // chunk,)),
        ],
        compiler_params=params(16),
        cost_estimate=pl.CostEstimate(
            flops=flops * (far_slots * tile + 2 * clusters), bytes_accessed=8 << 20, transcendentals=rows * clusters
        ),
        name="far",
    )(where, in_hbm(tile_vals), in_hbm(part), on_chip(graph2), *parts)

    masses = lax.all_to_all(mass_parts, NODES, split_axis=0, concat_axis=0, tiled=True)

    return pl.pallas_call(
        functools.partial(last_kernel, 8),
        out_shape=jax.ShapeDtypeStruct((rows, clusters), f32),
        in_specs=[VMEM, VMEM, VMEM],
        out_specs=ANY,
        scratch_shapes=[pltpu.VMEM((rows, clusters), f32), pltpu.SemaphoreType.DMA((8,))],
        compiler_params=params(8),
        name="last",
    )(on_chip(logits), on_chip(masses), cluster_mass.reshape(1, clusters))


def solution(mesh):
    return jax.shard_map(
        local,
        mesh=mesh,
        in_specs=(
            P(("groups", "rows", "sub"), None),
            P(("groups", "rows", "sub"), None, None, None),
            P(("groups", "rows", "sub"), None),
            P("groups", None),
            P("groups"),
        ),
        out_specs=P(("groups", "rows", "sub"), None),
        check_vma=False,
    )
```

```python
import functools

import jax
import jax.numpy as jnp
from jax import lax
from jax.experimental import pallas as pl
from jax.experimental.pallas import tpu as pltpu
from jax.sharding import PartitionSpec as P


NEAR = 4
LEVEL = 4
NODES = ("rows", "sub")

eta_step = 2.0
relax_power = 0.5

ANY = pl.BlockSpec(memory_space=pl.ANY)
VMEM = pl.BlockSpec(memory_space=pltpu.VMEM)
SMEM = pl.BlockSpec(memory_space=pltpu.SMEM)

f32, bf16, i32 = jnp.float32, jnp.bfloat16, jnp.int32


def on_chip(x):
    return pltpu.with_memory_space_constraint(x, pltpu.VMEM)


def in_hbm(x):
    return pltpu.with_memory_space_constraint(x, pltpu.HBM)


def params(mib):
    return pltpu.CompilerParams(vmem_limit_bytes=mib << 20)


def requests_kernel(nodes_total, place_ref, all_cols_ref, coupling_ref, *refs):
    *out_refs, own_ref, rows, cols_ref, table_ref, cols_sem, sems = refs
    slots, blocks_dev = cols_ref.shape
    cols_copy = pltpu.make_async_copy(all_cols_ref, cols_ref, cols_sem)
    cols_copy.start()
    shards = table_ref.shape[0]
    nodes, clusters = coupling_ref.shape
    parts = sems.shape[0]
    step = nodes // parts
    copies = [
        pltpu.make_async_copy(coupling_ref.at[pl.ds(i * step, step)], rows.at[pl.ds(i * step, step)], sems.at[i])
        for i in range(parts)
    ]
    for copy in copies:
        copy.start()

    owner = lax.broadcasted_iota(i32, (shards, blocks_dev), 0)
    place = lax.broadcasted_iota(i32, (clusters, blocks_dev), 0).astype(f32)
    before = (
        lax.broadcasted_iota(i32, (blocks_dev, blocks_dev), 0)
        < lax.broadcasted_iota(i32, (blocks_dev, blocks_dev), 1)
    ).astype(f32)
    count = jnp.zeros((shards, 1), f32)
    table = jnp.zeros((shards, clusters), f32)
    cols_copy.wait()
    for slot_id in range(NEAR, slots):
        local = cols_ref[slot_id : slot_id + 1, :] - owner * blocks_dev
        hit = (local >= 0) & (local < blocks_dev)
        hits = hit.astype(f32)
        earlier = jnp.dot(hits, before, preferred_element_type=f32) + count
        rank = jnp.sum(earlier * hits, axis=0, keepdims=True)
        count = count + jnp.sum(hits, axis=1, keepdims=True)
        wanted = jnp.where(hit, local, 0).astype(f32)
        table = table + lax.dot_general(
            wanted,
            (rank == place).astype(f32),
            (((1,), (1,)), ((), ())),
            precision=lax.Precision.HIGHEST,
            preferred_element_type=f32,
        )
    table_ref[:, 0, :] = table
    level = place_ref[0] // LEVEL
    for dz, ref in enumerate((own_ref, *out_refs)):
        for row in range(LEVEL):
            ref[row] = table_ref[(level ^ dz) * LEVEL + row]
    total = jnp.zeros((8, clusters), f32)
    for i in range(parts):
        copies[i].wait()
        part = rows[pl.ds(i * step, step), :].astype(f32)
        total = total + jnp.sum(part.reshape(step // 8, 8, clusters), axis=0)
    mass = jnp.sum(total, axis=0, keepdims=True) / nodes_total
    for ref in (own_ref, *out_refs):
        ref[LEVEL] = mass


def gather_kernel(cap, stage, place_ref, *refs):
    count = (len(refs) - 5) // 2
    heard_refs, sources, out_refs = refs[:count], refs[count : count + 2], refs[count + 2 : 2 * count + 2]
    wanted_ref, wanted_smem, sems = refs[2 * count + 2 :]
    for n, heard in enumerate(heard_refs):
        wanted_ref[n * 8 : n * 8 + LEVEL, :] = heard[:LEVEL, 0, :].astype(i32)
    copy = pltpu.make_async_copy(wanted_ref, wanted_smem, sems.at[0])
    copy.start()
    copy.wait()
    spot = place_ref[0] % LEVEL
    for n, out_ref in enumerate(out_refs):
        for sub, src in enumerate(sources):
            row = n * 8 + (spot ^ (2 * stage + sub))
            for j in range(cap):
                pltpu.make_async_copy(src.at[wanted_smem[row, j]], out_ref.at[sub * cap + j], sems.at[n + 1]).start()
    for n, out_ref in enumerate(out_refs):
        pltpu.make_async_copy(out_ref, out_ref, sems.at[n + 1]).wait()


def split(x):
    high = x.astype(bf16)
    return jnp.concatenate([high, (x - high.astype(f32)).astype(bf16)], axis=1)


def prep_kernel(cap, shards, place_ref, cols_ref, graph_ref, *refs):
    *mass_refs, graph2_ref, pull_ref, where_ref, count_ref = refs
    slots, blocks_dev = cols_ref.shape
    clusters = graph_ref.shape[0]
    spot, level = place_ref[0] % LEVEL, place_ref[0] // LEVEL
    graph = graph_ref[...].astype(f32)
    colmass = mass_refs[0][...]
    for ref in mass_refs[1:]:
        colmass = colmass + ref[...]
    pull_ref[...] = (
        lax.dot_general(
            jnp.broadcast_to(colmass, (8, clusters)),
            graph * graph,
            (((1,), (1,)), ((), ())),
            precision=lax.Precision.HIGHEST,
            preferred_element_type=f32,
        )
        / clusters
    )
    turned = graph.T.astype(bf16)
    graph2_ref[:clusters, :] = turned
    graph2_ref[clusters:, :] = turned

    @pl.loop(0, shards)
    def _(o):
        count_ref[o] = 0

    for slot_id in range(NEAR, slots):

        @pl.loop(0, blocks_dev)
        def _(b):
            owner = cols_ref[slot_id, b] // blocks_dev
            rank = count_ref[owner]
            count_ref[owner] = rank + 1
            turn = (owner % LEVEL) ^ spot
            row = ((turn // 2) * (shards // LEVEL) + ((owner // LEVEL) ^ level)) * 2 + turn % 2
            where_ref[b * (slots - NEAR) + slot_id - NEAR] = row * cap + rank


def near_kernel(
    group, chunk, place_ref, cols_ref, own_ref, chip_ref, level_ref, edge_ref, tiles_ref, graph2_ref, pull_ref, part_ref, window, tiles, part, own_sem, sems, tile_sems, part_sems,
):
    blocks_dev, tile, clusters = own_ref.shape
    steps = blocks_dev // group
    place = place_ref[0]
    spot = place % LEVEL

    def take(src, i, sem):
        return pltpu.make_async_copy(src, window.at[pl.ds(i * blocks_dev, blocks_dev)], sem)

    take(own_ref, 1, own_sem).start()
    even = spot % 2 == 0
    edge = (spot == 0) | (spot == LEVEL - 1)
    for flag, src in ((edge, edge_ref), (jnp.logical_not(edge), level_ref)):
        for is_even, chip_at, other_at in ((True, 2, 0), (False, 0, 2)):

            @pl.when(flag & (even == is_even))
            def _():
                take(chip_ref, chip_at, sems.at[0]).start()
                take(src, other_at, sems.at[1]).start()

    def fetch(i):
        here = pl.ds(i * chunk, chunk)
        return pltpu.make_async_copy(tiles_ref.at[here, pl.ds(0, NEAR)], tiles.at[here], tile_sems.at[i])

    def store(i):
        here = pl.ds(i * chunk * tile, chunk * tile)
        return pltpu.make_async_copy(part.at[here], part_ref.at[here], part_sems.at[i])

    for i in range(blocks_dev // chunk):
        fetch(i).start()
    take(own_ref, 1, own_sem).wait()
    take(chip_ref, 0, sems.at[0]).wait()
    take(chip_ref, 2, sems.at[1]).wait()

    base = (place - 1) * blocks_dev
    scale = 2.0 * eta_step / clusters

    def products(step):
        first = step * group
        if first % chunk == 0:
            fetch(first // chunk).wait()
        spreads = []
        for b in range(first, first + group):
            picked = [window[cols_ref[s, b] - base] for s in range(NEAR)]
            wide = jnp.concatenate([tiles[b, s] for s in range(NEAR)], axis=1)
            spreads.append(split(jnp.dot(wide, jnp.concatenate(picked, axis=0), preferred_element_type=f32)))
        return jnp.concatenate(spreads, axis=0)

    ahead = products(0)
    for step in range(steps):
        spreads = ahead
        if step + 1 < steps:
            ahead = products(step + 1)
        first = step * group
        affinity = jnp.dot(spreads, graph2_ref[...], preferred_element_type=f32)
        own = window[blocks_dev + first : blocks_dev + first + group].reshape(group * tile, clusters)
        part[first * tile : (first + group) * tile, :] = (
            jnp.log(own.astype(f32)) - eta_step * pull_ref[0:1, :] + scale * affinity
        )
        if (first + group) % chunk == 0:
            store(first // chunk).start()
    for i in range(blocks_dev // chunk):
        store(i).wait()


def far_kernel(
    group, chunk, nodes_total, where_ref, tiles_ref, part_ref, graph2_ref, *refs
):
    *found_refs, logits_ref, mass_ref = refs[:-5]
    blocks_ref, tiles, block_sem, tile_sems, part_sems = refs[-5:]
    tile, clusters = blocks_ref.shape[1:]
    blocks_dev, far_slots = tiles.shape[:2]
    steps = blocks_dev // group
    scale = 2.0 * eta_step / clusters
    width = found_refs[0].shape[0]
    for i, found in enumerate(found_refs):
        pltpu.make_async_copy(found, blocks_ref.at[pl.ds(i * width, width)], block_sem).start()

    def fetches(i):
        here = pl.ds(i * chunk, chunk)
        there = pl.ds(i * chunk * tile, chunk * tile)
        return (
            pltpu.make_async_copy(tiles_ref.at[here, pl.ds(NEAR, far_slots)], tiles.at[here], tile_sems.at[i]),
            pltpu.make_async_copy(part_ref.at[there], logits_ref.at[there], part_sems.at[i]),
        )

    for i in range(blocks_dev // chunk):
        for copy in fetches(i):
            copy.start()

    def products(step):
        first = step * group
        if first % chunk == 0:
            for copy in fetches(first // chunk):
                copy.wait()
        spreads = []
        for b in range(first, first + group):
            picked = [blocks_ref[where_ref[b * far_slots + s]] for s in range(far_slots)]
            wide = jnp.concatenate([tiles[b, s] for s in range(far_slots)], axis=1)
            spreads.append(split(jnp.dot(wide, jnp.concatenate(picked, axis=0), preferred_element_type=f32)))
        return jnp.concatenate(spreads, axis=0)

    pltpu.make_async_copy(blocks_ref, blocks_ref, block_sem).wait()
    total = jnp.zeros((8, clusters), f32)
    ahead = products(0)
    for step in range(steps):
        spreads = ahead
        if step + 1 < steps:
            ahead = products(step + 1)
        here = pl.ds(step * group * tile, group * tile)
        affinity = jnp.dot(spreads, graph2_ref[...], preferred_element_type=f32)
        logits = logits_ref[here, :] + scale * affinity
        logits_ref[here, :] = logits
        total = total + jnp.sum(jnp.exp(logits).reshape(group * tile // 8, 8, clusters), axis=0)

    mass = jnp.sum(total, axis=0, keepdims=True) / nodes_total
    mass_ref[:, 0, :] = jnp.broadcast_to(mass, (mass_ref.shape[0], clusters))


def last_kernel(parts, logits_ref, mass_ref, target_ref, out_ref, kept, sems):
    newmass = jnp.sum(mass_ref[:, 0, :], axis=0, keepdims=True)
    shift = relax_power * (jnp.log(target_ref[...]) - jnp.log(newmass))
    rows = logits_ref.shape[0]
    step = rows // parts
    copies = []
    for i in range(parts):
        here = pl.ds(i * step, step)
        shifted = logits_ref[here, :] + shift
        kept[here, :] = shifted - jnp.log(jnp.sum(jnp.exp(shifted), axis=1, keepdims=True))
        copies.append(pltpu.make_async_copy(kept.at[here], out_ref.at[here], sems.at[i]))
        copies[-1].start()
    for copy in copies:
        copy.wait()


def local(coupling, tile_vals, tile_cols, cluster_graph, cluster_mass):
    shards = lax.axis_size(NODES)
    my_index = lax.axis_index(NODES)
    blocks_dev, slots = tile_cols.shape
    tile = tile_vals.shape[2]
    rows, clusters = coupling.shape
    far_slots = slots - NEAR
    nodes_total = rows * shards
    far_count = blocks_dev * far_slots
    cap = (far_count + shards - 1) // shards
    blocks = coupling.reshape(blocks_dev, tile, clusters)
    cols = tile_cols.T
    group = 4
    steps = blocks_dev // group
    flops = 2 * rows * clusters

    levels = shards // LEVEL
    others = range(1, levels)
    place = my_index.astype(i32).reshape(1)

    def swap(x, bits):
        return lax.ppermute(x, NODES, [(i, i ^ bits) for i in range(shards)])

    over = swap(blocks, 2)
    chip = swap(blocks, 1)

    *asked, mine, held = pl.pallas_call(
        functools.partial(requests_kernel, nodes_total),
        out_shape=(
            *[pltpu.VMEM((LEVEL + 1, 1, clusters), f32)] * levels,
            pltpu.VMEM((rows, clusters), bf16),
        ),
        in_specs=[SMEM, ANY, ANY],
        out_specs=[VMEM] * (levels + 1),
        scratch_shapes=[
            pltpu.VMEM((slots, blocks_dev), i32),
            pltpu.VMEM((shards, 1, clusters), f32),
            pltpu.SemaphoreType.DMA,
            pltpu.SemaphoreType.DMA((8,)),
        ],
        compiler_params=params(8),
        name="requests",
    )(place, in_hbm(cols), in_hbm(coupling))
    heard = [swap(x, dz * LEVEL) for dz, x in zip(others, asked)]
    edges = [z * LEVEL for z in range(1, levels)]
    edge = lax.ppermute(blocks, NODES, [(i - 1, i + 2) for i in edges] + [(i, i - 3) for i in edges])

    def gather(stage, heard, sources):
        return pl.pallas_call(
            functools.partial(gather_kernel, cap, stage),
            out_shape=[pltpu.HBM((2 * cap, tile, clusters), bf16)] * len(heard),
            in_specs=[SMEM] + [VMEM] * (len(heard) + 2),
            out_specs=[ANY] * len(heard),
            scratch_shapes=[
                pltpu.VMEM((8 * len(heard), clusters), i32),
                pltpu.SMEM((8 * len(heard), clusters), i32),
                pltpu.SemaphoreType.DMA((len(heard) + 1,)),
            ],
            compiler_params=params(8),
        )(place, *[on_chip(x) for x in heard], *[on_chip(x) for x in sources])

    found = gather(0, heard, (held.reshape(blocks.shape), chip))
    fetched = [swap(x, dz * LEVEL) for dz, x in zip(others, found)]
    over_chip = swap(over, 1)
    edge = lax.ppermute(edge, NODES, [(i + 2, i) for i in edges] + [(i - 3, i - 1) for i in edges])
    found = gather(1, (*heard, mine), (over, over_chip))
    there = [swap(x, dz * LEVEL) for dz, x in zip(others, found)]
    home_late = found[-1]
    (home,) = gather(0, (mine,), (held.reshape(blocks.shape), chip))

    mass = mine[LEVEL]
    for x in heard:
        mass = mass + x[LEVEL]
    mass_chip = swap(mass, 1)
    mass = mass + mass_chip
    mass_over = swap(mass, 2)

    graph2, pull, where = pl.pallas_call(
        functools.partial(prep_kernel, cap, shards),
        out_shape=(
            pltpu.VMEM((2 * clusters, clusters), bf16),
            pltpu.VMEM((8, clusters), f32),
            jax.ShapeDtypeStruct((far_count,), i32),
        ),
        in_specs=[SMEM, SMEM, VMEM, VMEM, VMEM],
        out_specs=(VMEM, VMEM, SMEM),
        scratch_shapes=[pltpu.SMEM((shards,), i32)],
        compiler_params=params(4),
        name="prep",
    )(place, cols, cluster_graph, mass, mass_over)

    chunk = min(16, blocks_dev)
    part = pl.pallas_call(
        functools.partial(near_kernel, group, group),
        out_shape=pltpu.HBM((rows, clusters), f32),
        in_specs=[SMEM, SMEM, ANY, ANY, ANY, ANY, ANY, VMEM, VMEM],
        out_specs=ANY,
        scratch_shapes=[
            pltpu.VMEM((3 * blocks_dev, tile, clusters), bf16),
            pltpu.VMEM((blocks_dev, NEAR, tile, tile), bf16),
            pltpu.VMEM((rows, clusters), f32),
            pltpu.SemaphoreType.DMA,
            pltpu.SemaphoreType.DMA((2,)),
            pltpu.SemaphoreType.DMA((steps,)),
            pltpu.SemaphoreType.DMA((steps,)),
        ],
        compiler_params=params(20),
        cost_estimate=pl.CostEstimate(
            flops=flops * (NEAR * tile + 2 * clusters), bytes_accessed=16 << 20, transcendentals=rows * clusters
        ),
        name="near",
    )(place, cols, in_hbm(blocks), chip, over_chip, edge, in_hbm(tile_vals), on_chip(graph2), on_chip(pull))

    parts = [home, *fetched, home_late, *there]
    logits, mass_parts = pl.pallas_call(
        functools.partial(far_kernel, group, chunk, nodes_total),
        out_shape=(pltpu.VMEM((rows, clusters), f32), pltpu.VMEM((shards, 1, clusters), f32)),
        in_specs=[SMEM, ANY, ANY, VMEM] + [ANY] * len(parts),
        out_specs=(VMEM, VMEM),
        scratch_shapes=[
            pltpu.VMEM((2 * cap * len(parts), tile, clusters), bf16),
            pltpu.VMEM((blocks_dev, far_slots, tile, tile), bf16),
            pltpu.SemaphoreType.DMA,
            pltpu.SemaphoreType.DMA((blocks_dev // chunk,)),
            pltpu.SemaphoreType.DMA((blocks_dev // chunk,)),
        ],
        compiler_params=params(16),
        cost_estimate=pl.CostEstimate(
            flops=flops * (far_slots * tile + 2 * clusters), bytes_accessed=8 << 20, transcendentals=rows * clusters
        ),
        name="far",
    )(where, in_hbm(tile_vals), in_hbm(part), on_chip(graph2), *parts)

    masses = lax.all_to_all(mass_parts, NODES, split_axis=0, concat_axis=0, tiled=True)

    return pl.pallas_call(
        functools.partial(last_kernel, 8),
        out_shape=jax.ShapeDtypeStruct((rows, clusters), f32),
        in_specs=[VMEM, VMEM, VMEM],
        out_specs=ANY,
        scratch_shapes=[pltpu.VMEM((rows, clusters), f32), pltpu.SemaphoreType.DMA((8,))],
        compiler_params=params(8),
        name="last",
    )(on_chip(logits), on_chip(masses), cluster_mass.reshape(1, clusters))


def solution(mesh):
    return jax.shard_map(
        local,
        mesh=mesh,
        in_specs=(
            P(("groups", "rows", "sub"), None),
            P(("groups", "rows", "sub"), None, None, None),
            P(("groups", "rows", "sub"), None),
            P("groups", None),
            P("groups"),
        ),
        out_specs=P(("groups", "rows", "sub"), None),
        check_vma=False,
    )
```

```python
import functools

import jax
import jax.numpy as jnp
from jax import lax
from jax.experimental import pallas as pl
from jax.experimental.pallas import tpu as pltpu
from jax.sharding import PartitionSpec as P


NEAR = 4
LEVEL = 4
NODES = ("rows", "sub")

eta_step = 2.0
relax_power = 0.5

ANY = pl.BlockSpec(memory_space=pl.ANY)
VMEM = pl.BlockSpec(memory_space=pltpu.VMEM)
SMEM = pl.BlockSpec(memory_space=pltpu.SMEM)

f32, bf16, i32 = jnp.float32, jnp.bfloat16, jnp.int32


def on_chip(x):
    return pltpu.with_memory_space_constraint(x, pltpu.VMEM)


def in_hbm(x):
    return pltpu.with_memory_space_constraint(x, pltpu.HBM)


def params(mib):
    return pltpu.CompilerParams(vmem_limit_bytes=mib << 20)


def requests_kernel(nodes_total, place_ref, all_cols_ref, coupling_ref, *refs):
    *out_refs, own_ref, rows, half_ref, cols_ref, table_ref, cols_sem, half_sem, sems = refs
    slots, blocks_dev = cols_ref.shape
    cols_copy = pltpu.make_async_copy(all_cols_ref, cols_ref, cols_sem)
    cols_copy.start()
    shards = table_ref.shape[0]
    nodes, clusters = coupling_ref.shape
    parts = sems.shape[0]
    step = nodes // parts
    copies = [
        pltpu.make_async_copy(coupling_ref.at[pl.ds(i * step, step)], rows.at[pl.ds(i * step, step)], sems.at[i])
        for i in range(parts)
    ]
    for copy in copies:
        copy.start()
    half_copy = pltpu.make_async_copy(coupling_ref.at[pl.ds(0, nodes // 2)], half_ref, half_sem)
    half_copy.start()

    owner = lax.broadcasted_iota(i32, (shards, blocks_dev), 0)
    place = lax.broadcasted_iota(i32, (clusters, blocks_dev), 0).astype(f32)
    before = (
        lax.broadcasted_iota(i32, (blocks_dev, blocks_dev), 0)
        < lax.broadcasted_iota(i32, (blocks_dev, blocks_dev), 1)
    ).astype(f32)
    count = jnp.zeros((shards, 1), f32)
    table = jnp.zeros((shards, clusters), f32)
    cols_copy.wait()
    for slot_id in range(NEAR, slots):
        local = cols_ref[slot_id : slot_id + 1, :] - owner * blocks_dev
        hit = (local >= 0) & (local < blocks_dev)
        hits = hit.astype(f32)
        earlier = jnp.dot(hits, before, preferred_element_type=f32) + count
        rank = jnp.sum(earlier * hits, axis=0, keepdims=True)
        count = count + jnp.sum(hits, axis=1, keepdims=True)
        wanted = jnp.where(hit, local, 0).astype(f32)
        table = table + lax.dot_general(
            wanted,
            (rank == place).astype(f32),
            (((1,), (1,)), ((), ())),
            precision=lax.Precision.HIGHEST,
            preferred_element_type=f32,
        )
    table_ref[:, 0, :] = table
    level = place_ref[0] // LEVEL
    for dz, ref in enumerate((own_ref, *out_refs)):
        for row in range(LEVEL):
            ref[row] = table_ref[(level ^ dz) * LEVEL + row]
    total = jnp.zeros((8, clusters), f32)
    for i in range(parts):
        copies[i].wait()
        part = rows[pl.ds(i * step, step), :].astype(f32)
        total = total + jnp.sum(part.reshape(step // 8, 8, clusters), axis=0)
    mass = jnp.sum(total, axis=0, keepdims=True) / nodes_total
    for ref in (own_ref, *out_refs):
        ref[LEVEL] = mass
    half_copy.wait()


def gather_kernel(cap, stage, place_ref, *refs):
    count = (len(refs) - 5) // 2
    heard_refs, sources, out_refs = refs[:count], refs[count : count + 2], refs[count + 2 : 2 * count + 2]
    wanted_ref, wanted_smem, sems = refs[2 * count + 2 :]
    for n, heard in enumerate(heard_refs):
        wanted_ref[n * 8 : n * 8 + LEVEL, :] = heard[:LEVEL, 0, :].astype(i32)
    copy = pltpu.make_async_copy(wanted_ref, wanted_smem, sems.at[0])
    copy.start()
    copy.wait()
    spot = place_ref[0] % LEVEL
    for n, out_ref in enumerate(out_refs):
        for sub, src in enumerate(sources):
            row = n * 8 + (spot ^ (2 * stage + sub))
            for j in range(cap):
                pltpu.make_async_copy(src.at[wanted_smem[row, j]], out_ref.at[sub * cap + j], sems.at[n + 1]).start()
    for n, out_ref in enumerate(out_refs):
        pltpu.make_async_copy(out_ref, out_ref, sems.at[n + 1]).wait()


def split(x):
    high = x.astype(bf16)
    return jnp.concatenate([high, (x - high.astype(f32)).astype(bf16)], axis=1)


def prep_kernel(cap, shards, place_ref, cols_ref, graph_ref, *refs):
    *mass_refs, graph2_ref, pull_ref, where_ref, count_ref = refs
    slots, blocks_dev = cols_ref.shape
    clusters = graph_ref.shape[0]
    spot, level = place_ref[0] % LEVEL, place_ref[0] // LEVEL
    graph = graph_ref[...].astype(f32)
    colmass = mass_refs[0][...]
    for ref in mass_refs[1:]:
        colmass = colmass + ref[...]
    pull_ref[...] = (
        lax.dot_general(
            jnp.broadcast_to(colmass, (8, clusters)),
            graph * graph,
            (((1,), (1,)), ((), ())),
            precision=lax.Precision.HIGHEST,
            preferred_element_type=f32,
        )
        / clusters
    )
    turned = graph.T.astype(bf16)
    graph2_ref[:clusters, :] = turned
    graph2_ref[clusters:, :] = turned

    @pl.loop(0, shards)
    def _(o):
        count_ref[o] = 0

    for slot_id in range(NEAR, slots):

        @pl.loop(0, blocks_dev)
        def _(b):
            owner = cols_ref[slot_id, b] // blocks_dev
            rank = count_ref[owner]
            count_ref[owner] = rank + 1
            turn = (owner % LEVEL) ^ spot
            row = ((turn // 2) * (shards // LEVEL) + ((owner // LEVEL) ^ level)) * 2 + turn % 2
            where_ref[b * (slots - NEAR) + slot_id - NEAR] = row * cap + rank


def near_kernel(
    group, chunk, place_ref, cols_ref, own_ref, chip_ref, level_ref, edge_ref, beyond_ref, tiles_ref,
    graph2_ref, pull_ref, part_ref, window, tiles, part, own_sem, sems, tile_sems, part_sems,
):
    blocks_dev, tile, clusters = own_ref.shape
    steps = blocks_dev // group
    place = place_ref[0]
    spot = place % LEVEL

    def take(src, i, sem):
        return pltpu.make_async_copy(src, window.at[pl.ds(i * blocks_dev, blocks_dev)], sem)

    take(own_ref, 1, own_sem).start()
    even = spot % 2 == 0
    edge = (spot == 0) | (spot == LEVEL - 1)
    half = blocks_dev // 2
    for is_even, chip_at, other_at in ((True, 2, 0), (False, 0, 2)):

        @pl.when(even == is_even)
        def _():
            take(chip_ref, chip_at, sems.at[0]).start()

        @pl.when((even == is_even) & jnp.logical_not(edge))
        def _():
            take(level_ref, other_at, sems.at[1]).start()

        @pl.when((even == is_even) & edge)
        def _():
            low = window.at[pl.ds(other_at * blocks_dev, half)]
            high = window.at[pl.ds(other_at * blocks_dev + half, half)]
            pltpu.make_async_copy(edge_ref, low, sems.at[1]).start()
            pltpu.make_async_copy(beyond_ref, high, sems.at[1]).start()

    def fetch(i):
        here = pl.ds(i * chunk, chunk)
        return pltpu.make_async_copy(tiles_ref.at[here, pl.ds(0, NEAR)], tiles.at[here], tile_sems.at[i])

    def store(i):
        here = pl.ds(i * chunk * tile, chunk * tile)
        return pltpu.make_async_copy(part.at[here], part_ref.at[here], part_sems.at[i])

    for i in range(blocks_dev // chunk):
        fetch(i).start()
    take(own_ref, 1, own_sem).wait()
    take(chip_ref, 0, sems.at[0]).wait()
    take(chip_ref, 2, sems.at[1]).wait()

    base = (place - 1) * blocks_dev
    scale = 2.0 * eta_step / clusters

    def products(step):
        first = step * group
        if first % chunk == 0:
            fetch(first // chunk).wait()
        spreads = []
        for b in range(first, first + group):
            picked = [window[cols_ref[s, b] - base] for s in range(NEAR)]
            wide = jnp.concatenate([tiles[b, s] for s in range(NEAR)], axis=1)
            spreads.append(split(jnp.dot(wide, jnp.concatenate(picked, axis=0), preferred_element_type=f32)))
        return jnp.concatenate(spreads, axis=0)

    ahead = products(0)
    for step in range(steps):
        spreads = ahead
        if step + 1 < steps:
            ahead = products(step + 1)
        first = step * group
        affinity = jnp.dot(spreads, graph2_ref[...], preferred_element_type=f32)
        own = window[blocks_dev + first : blocks_dev + first + group].reshape(group * tile, clusters)
        part[first * tile : (first + group) * tile, :] = (
            jnp.log(own.astype(f32)) - eta_step * pull_ref[0:1, :] + scale * affinity
        )
        if (first + group) % chunk == 0:
            store(first // chunk).start()
    for i in range(blocks_dev // chunk):
        store(i).wait()


def far_kernel(
    group, chunk, nodes_total, where_ref, tiles_ref, part_ref, graph2_ref, *refs
):
    *found_refs, logits_ref, mass_ref = refs[:-5]
    blocks_ref, tiles, block_sem, tile_sems, part_sems = refs[-5:]
    tile, clusters = blocks_ref.shape[1:]
    blocks_dev, far_slots = tiles.shape[:2]
    steps = blocks_dev // group
    scale = 2.0 * eta_step / clusters
    width = found_refs[0].shape[0]
    for i, found in enumerate(found_refs):
        pltpu.make_async_copy(found, blocks_ref.at[pl.ds(i * width, width)], block_sem).start()

    def fetches(i):
        here = pl.ds(i * chunk, chunk)
        there = pl.ds(i * chunk * tile, chunk * tile)
        return (
            pltpu.make_async_copy(tiles_ref.at[here, pl.ds(NEAR, far_slots)], tiles.at[here], tile_sems.at[i]),
            pltpu.make_async_copy(part_ref.at[there], logits_ref.at[there], part_sems.at[i]),
        )

    for i in range(blocks_dev // chunk):
        for copy in fetches(i):
            copy.start()

    def products(step):
        first = step * group
        if first % chunk == 0:
            for copy in fetches(first // chunk):
                copy.wait()
        spreads = []
        for b in range(first, first + group):
            picked = [blocks_ref[where_ref[b * far_slots + s]] for s in range(far_slots)]
            wide = jnp.concatenate([tiles[b, s] for s in range(far_slots)], axis=1)
            spreads.append(split(jnp.dot(wide, jnp.concatenate(picked, axis=0), preferred_element_type=f32)))
        return jnp.concatenate(spreads, axis=0)

    pltpu.make_async_copy(blocks_ref, blocks_ref, block_sem).wait()
    total = jnp.zeros((8, clusters), f32)
    ahead = products(0)
    for step in range(steps):
        spreads = ahead
        if step + 1 < steps:
            ahead = products(step + 1)
        here = pl.ds(step * group * tile, group * tile)
        affinity = jnp.dot(spreads, graph2_ref[...], preferred_element_type=f32)
        logits = logits_ref[here, :] + scale * affinity
        logits_ref[here, :] = logits
        total = total + jnp.sum(jnp.exp(logits).reshape(group * tile // 8, 8, clusters), axis=0)

    mass = jnp.sum(total, axis=0, keepdims=True) / nodes_total
    mass_ref[:, 0, :] = jnp.broadcast_to(mass, (mass_ref.shape[0], clusters))


def last_kernel(parts, logits_ref, mass_ref, target_ref, out_ref, kept, sems):
    newmass = jnp.sum(mass_ref[:, 0, :], axis=0, keepdims=True)
    shift = relax_power * (jnp.log(target_ref[...]) - jnp.log(newmass))
    rows = logits_ref.shape[0]
    step = rows // parts
    copies = []
    for i in range(parts):
        here = pl.ds(i * step, step)
        shifted = logits_ref[here, :] + shift
        kept[here, :] = shifted - jnp.log(jnp.sum(jnp.exp(shifted), axis=1, keepdims=True))
        copies.append(pltpu.make_async_copy(kept.at[here], out_ref.at[here], sems.at[i]))
        copies[-1].start()
    for copy in copies:
        copy.wait()


def local(coupling, tile_vals, tile_cols, cluster_graph, cluster_mass):
    shards = lax.axis_size(NODES)
    my_index = lax.axis_index(NODES)
    blocks_dev, slots = tile_cols.shape
    tile = tile_vals.shape[2]
    rows, clusters = coupling.shape
    far_slots = slots - NEAR
    nodes_total = rows * shards
    far_count = blocks_dev * far_slots
    cap = (far_count + shards - 1) // shards
    blocks = coupling.reshape(blocks_dev, tile, clusters)
    cols = tile_cols.T
    group = 4
    steps = blocks_dev // group
    flops = 2 * rows * clusters

    levels = shards // LEVEL
    others = range(1, levels)
    place = my_index.astype(i32).reshape(1)

    def swap(x, bits):
        return lax.ppermute(x, NODES, [(i, i ^ bits) for i in range(shards)])

    over = swap(blocks, 2)
    chip = swap(blocks, 1)

    *asked, mine, held, half = pl.pallas_call(
        functools.partial(requests_kernel, nodes_total),
        out_shape=(
            *[pltpu.VMEM((LEVEL + 1, 1, clusters), f32)] * levels,
            pltpu.VMEM((rows, clusters), bf16),
            pltpu.VMEM((rows // 2, clusters), bf16),
        ),
        in_specs=[SMEM, ANY, ANY],
        out_specs=[VMEM] * (levels + 2),
        scratch_shapes=[
            pltpu.VMEM((slots, blocks_dev), i32),
            pltpu.VMEM((shards, 1, clusters), f32),
            pltpu.SemaphoreType.DMA,
            pltpu.SemaphoreType.DMA,
            pltpu.SemaphoreType.DMA((8,)),
        ],
        compiler_params=params(8),
        name="requests",
    )(place, in_hbm(cols), in_hbm(coupling))
    heard = [swap(x, dz * LEVEL) for dz, x in zip(others, asked)]
    edges = [z * LEVEL for z in range(1, levels)]
    edge = lax.ppermute(half, NODES, [(i - 1, i + 2) for i in edges] + [(i, i - 3) for i in edges])

    def gather(stage, heard, sources):
        return pl.pallas_call(
            functools.partial(gather_kernel, cap, stage),
            out_shape=[pltpu.HBM((2 * cap, tile, clusters), bf16)] * len(heard),
            in_specs=[SMEM] + [VMEM] * (len(heard) + 2),
            out_specs=[ANY] * len(heard),
            scratch_shapes=[
                pltpu.VMEM((8 * len(heard), clusters), i32),
                pltpu.SMEM((8 * len(heard), clusters), i32),
                pltpu.SemaphoreType.DMA((len(heard) + 1,)),
            ],
            compiler_params=params(8),
        )(place, *[on_chip(x) for x in heard], *[on_chip(x) for x in sources])

    found = gather(0, heard, (held.reshape(blocks.shape), chip))
    fetched = [swap(x, dz * LEVEL) for dz, x in zip(others, found)]
    over_chip = swap(over, 1)
    beyond = lax.ppermute(over[blocks_dev // 2 :], NODES, [(i - 3, i) for i in edges] + [(i + 2, i - 1) for i in edges])
    edge = lax.ppermute(edge, NODES, [(i + 2, i) for i in edges] + [(i - 3, i - 1) for i in edges])
    found = gather(1, (*heard, mine), (over, over_chip))
    there = [swap(x, dz * LEVEL) for dz, x in zip(others, found)]
    home_late = found[-1]
    (home,) = gather(0, (mine,), (held.reshape(blocks.shape), chip))

    mass = mine[LEVEL]
    for x in heard:
        mass = mass + x[LEVEL]
    mass_chip = swap(mass, 1)
    mass = mass + mass_chip
    mass_over = swap(mass, 2)

    graph2, pull, where = pl.pallas_call(
        functools.partial(prep_kernel, cap, shards),
        out_shape=(
            pltpu.VMEM((2 * clusters, clusters), bf16),
            pltpu.VMEM((8, clusters), f32),
            jax.ShapeDtypeStruct((far_count,), i32),
        ),
        in_specs=[SMEM, SMEM, VMEM, VMEM, VMEM],
        out_specs=(VMEM, VMEM, SMEM),
        scratch_shapes=[pltpu.SMEM((shards,), i32)],
        compiler_params=params(4),
        name="prep",
    )(place, cols, cluster_graph, mass, mass_over)

    chunk = min(16, blocks_dev)
    part = pl.pallas_call(
        functools.partial(near_kernel, group, group),
        out_shape=pltpu.HBM((rows, clusters), f32),
        in_specs=[SMEM, SMEM, ANY, ANY, ANY, ANY, ANY, ANY, VMEM, VMEM],
        out_specs=ANY,
        scratch_shapes=[
            pltpu.VMEM((3 * blocks_dev, tile, clusters), bf16),
            pltpu.VMEM((blocks_dev, NEAR, tile, tile), bf16),
            pltpu.VMEM((rows, clusters), f32),
            pltpu.SemaphoreType.DMA,
            pltpu.SemaphoreType.DMA((2,)),
            pltpu.SemaphoreType.DMA((steps,)),
            pltpu.SemaphoreType.DMA((steps,)),
        ],
        compiler_params=params(20),
        cost_estimate=pl.CostEstimate(
            flops=flops * (NEAR * tile + 2 * clusters), bytes_accessed=16 << 20, transcendentals=rows * clusters
        ),
        name="near",
    )(
        place, cols, in_hbm(blocks), chip, over_chip, edge.reshape(blocks_dev // 2, tile, clusters), beyond,
        in_hbm(tile_vals), on_chip(graph2), on_chip(pull),
    )

    parts = [home, *fetched, home_late, *there]
    logits, mass_parts = pl.pallas_call(
        functools.partial(far_kernel, group, chunk, nodes_total),
        out_shape=(pltpu.VMEM((rows, clusters), f32), pltpu.VMEM((shards, 1, clusters), f32)),
        in_specs=[SMEM, ANY, ANY, VMEM] + [ANY] * len(parts),
        out_specs=(VMEM, VMEM),
        scratch_shapes=[
            pltpu.VMEM((2 * cap * len(parts), tile, clusters), bf16),
            pltpu.VMEM((blocks_dev, far_slots, tile, tile), bf16),
            pltpu.SemaphoreType.DMA,
            pltpu.SemaphoreType.DMA((blocks_dev // chunk,)),
            pltpu.SemaphoreType.DMA((blocks_dev // chunk,)),
        ],
        compiler_params=params(16),
        cost_estimate=pl.CostEstimate(
            flops=flops * (far_slots * tile + 2 * clusters), bytes_accessed=8 << 20, transcendentals=rows * clusters
        ),
        name="far",
    )(where, in_hbm(tile_vals), in_hbm(part), on_chip(graph2), *parts)

    masses = lax.all_to_all(mass_parts, NODES, split_axis=0, concat_axis=0, tiled=True)

    return pl.pallas_call(
        functools.partial(last_kernel, 8),
        out_shape=jax.ShapeDtypeStruct((rows, clusters), f32),
        in_specs=[VMEM, VMEM, VMEM],
        out_specs=ANY,
        scratch_shapes=[pltpu.VMEM((rows, clusters), f32), pltpu.SemaphoreType.DMA((8,))],
        compiler_params=params(8),
        name="last",
    )(on_chip(logits), on_chip(masses), cluster_mass.reshape(1, clusters))


def solution(mesh):
    return jax.shard_map(
        local,
        mesh=mesh,
        in_specs=(
            P(("groups", "rows", "sub"), None),
            P(("groups", "rows", "sub"), None, None, None),
            P(("groups", "rows", "sub"), None),
            P("groups", None),
            P("groups"),
        ),
        out_specs=P(("groups", "rows", "sub"), None),
        check_vma=False,
    )
```

```python
import functools

import jax
import jax.numpy as jnp
from jax import lax
from jax.experimental import pallas as pl
from jax.experimental.pallas import tpu as pltpu
from jax.sharding import PartitionSpec as P


NEAR = 4
LEVEL = 4
NODES = ("rows", "sub")

eta_step = 2.0
relax_power = 0.5

ANY = pl.BlockSpec(memory_space=pl.ANY)
VMEM = pl.BlockSpec(memory_space=pltpu.VMEM)
SMEM = pl.BlockSpec(memory_space=pltpu.SMEM)

f32, bf16, i32 = jnp.float32, jnp.bfloat16, jnp.int32


def order_of(levels):
    return [*range(levels // 2, levels), *range(1, levels // 2)]


def on_chip(x):
    return pltpu.with_memory_space_constraint(x, pltpu.VMEM)


def in_hbm(x):
    return pltpu.with_memory_space_constraint(x, pltpu.HBM)


def params(mib):
    return pltpu.CompilerParams(vmem_limit_bytes=mib << 20)


def requests_kernel(nodes_total, place_ref, all_cols_ref, coupling_ref, *refs):
    *out_refs, own_ref, rows, half_ref, cols_ref, table_ref, cols_sem, half_sem, sem = refs
    slots, blocks_dev = cols_ref.shape
    cols_copy = pltpu.make_async_copy(all_cols_ref, cols_ref, cols_sem)
    cols_copy.start()
    shards = table_ref.shape[0]
    nodes, clusters = coupling_ref.shape
    coupling_copy = pltpu.make_async_copy(coupling_ref, rows, sem)
    coupling_copy.start()
    half_copy = pltpu.make_async_copy(coupling_ref.at[pl.ds(0, half_ref.shape[0])], half_ref, half_sem)
    half_copy.start()

    owner = lax.broadcasted_iota(i32, (shards, blocks_dev), 0)
    place = lax.broadcasted_iota(i32, (clusters, blocks_dev), 0).astype(f32)
    before = (
        lax.broadcasted_iota(i32, (blocks_dev, blocks_dev), 0)
        < lax.broadcasted_iota(i32, (blocks_dev, blocks_dev), 1)
    ).astype(f32)
    count = jnp.zeros((shards, 1), f32)
    table = jnp.zeros((shards, clusters), f32)
    cols_copy.wait()
    coupling_copy.wait()
    for slot_id in range(NEAR, slots):
        local = cols_ref[slot_id : slot_id + 1, :] - owner * blocks_dev
        hit = (local >= 0) & (local < blocks_dev)
        hits = hit.astype(f32)
        earlier = jnp.dot(hits, before, preferred_element_type=f32) + count
        rank = jnp.sum(earlier * hits, axis=0, keepdims=True)
        count = count + jnp.sum(hits, axis=1, keepdims=True)
        wanted = jnp.where(hit, local, 0).astype(f32)
        table = table + lax.dot_general(
            wanted,
            (rank == place).astype(f32),
            (((1,), (1,)), ((), ())),
            precision=lax.Precision.HIGHEST,
            preferred_element_type=f32,
        )
    table_ref[:, 0, :] = table
    level = place_ref[0] // LEVEL
    for dz, ref in enumerate((own_ref, *out_refs)):
        for row in range(LEVEL):
            ref[row] = table_ref[(level ^ dz) * LEVEL + row]
    part = rows[...].astype(f32)
    mass = jnp.sum(jnp.sum(part.reshape(nodes // 8, 8, clusters), axis=0), axis=0, keepdims=True) / nodes_total
    for ref in (own_ref, *out_refs):
        ref[LEVEL] = mass
    half_copy.wait()


def gather_kernel(cap, stage, place_ref, *refs):
    count = (len(refs) - 5) // 2
    heard_refs, sources, out_refs = refs[:count], refs[count : count + 2], refs[count + 2 : 2 * count + 2]
    wanted_ref, wanted_smem, sems = refs[2 * count + 2 :]
    for n, heard in enumerate(heard_refs):
        wanted_ref[n * 8 : n * 8 + LEVEL, :] = heard[:LEVEL, 0, :].astype(i32)
    copy = pltpu.make_async_copy(wanted_ref, wanted_smem, sems.at[0])
    copy.start()
    copy.wait()
    spot = place_ref[0] % LEVEL
    for n, out_ref in enumerate(out_refs):
        for sub, src in enumerate(sources):
            row = n * 8 + (spot ^ (2 * stage + sub))
            for j in range(cap):
                pltpu.make_async_copy(src.at[wanted_smem[row, j]], out_ref.at[sub * cap + j], sems.at[n + 1]).start()
    for n, out_ref in enumerate(out_refs):
        pltpu.make_async_copy(out_ref, out_ref, sems.at[n + 1]).wait()


def split(x):
    high = x.astype(bf16)
    return jnp.concatenate([high, (x - high.astype(f32)).astype(bf16)], axis=1)


def prep_kernel(cap, shards, place_ref, cols_ref, graph_ref, *refs):
    *mass_refs, graph2_ref, pull_ref, where_ref, count_ref = refs
    slots, blocks_dev = cols_ref.shape
    clusters = graph_ref.shape[0]
    spot, level = place_ref[0] % LEVEL, place_ref[0] // LEVEL
    graph = graph_ref[...].astype(f32)
    colmass = mass_refs[0][...]
    for ref in mass_refs[1:]:
        colmass = colmass + ref[...]
    pull_ref[...] = (
        lax.dot_general(
            jnp.broadcast_to(colmass, (8, clusters)),
            graph * graph,
            (((1,), (1,)), ((), ())),
            precision=lax.Precision.HIGHEST,
            preferred_element_type=f32,
        )
        / clusters
    )
    turned = graph.T.astype(bf16)
    graph2_ref[:clusters, :] = turned
    graph2_ref[clusters:, :] = turned

    @pl.loop(0, shards)
    def _(o):
        count_ref[o] = 0

    for slot_id in range(NEAR, slots):

        @pl.loop(0, blocks_dev)
        def _(b):
            owner = cols_ref[slot_id, b] // blocks_dev
            rank = count_ref[owner]
            count_ref[owner] = rank + 1
            turn = (owner % LEVEL) ^ spot
            row = ((turn // 2) * (shards // LEVEL) + ((owner // LEVEL) ^ level)) * 2 + turn % 2
            where_ref[b * (slots - NEAR) + slot_id - NEAR] = row * cap + rank


def near_kernel(
    group, chunk, place_ref, cols_ref, own_ref, chip_ref, level_ref, edge_ref, beyond_ref, tiles_ref,
    graph2_ref, pull_ref, part_ref, far_tiles_ref, window, tiles, own_sem, far_sem, sems, tile_sems,
):
    blocks_dev, tile, clusters = own_ref.shape
    steps = blocks_dev // group
    place = place_ref[0]
    spot = place % LEVEL

    def take(src, i, sem):
        return pltpu.make_async_copy(src, window.at[pl.ds(i * blocks_dev, blocks_dev)], sem)

    take(own_ref, 1, own_sem).start()
    even = spot % 2 == 0
    edge = (spot == 0) | (spot == LEVEL - 1)
    early, late = edge_ref.shape[0], beyond_ref.shape[0]
    for is_even, chip_at, other_at in ((True, 2, 0), (False, 0, 2)):

        @pl.when(even == is_even)
        def _():
            take(chip_ref, chip_at, sems.at[0]).start()

        @pl.when((even == is_even) & jnp.logical_not(edge))
        def _():
            take(level_ref, other_at, sems.at[1]).start()

        @pl.when((even == is_even) & edge)
        def _():
            low = window.at[pl.ds(other_at * blocks_dev, early)]
            high = window.at[pl.ds(other_at * blocks_dev + early, late)]
            pltpu.make_async_copy(edge_ref, low, sems.at[1]).start()
            pltpu.make_async_copy(beyond_ref, high, sems.at[1]).start()

    def fetch(i):
        here = pl.ds(i * chunk, chunk)
        return pltpu.make_async_copy(tiles_ref.at[here, pl.ds(0, NEAR)], tiles.at[here], tile_sems.at[i])

    for i in range(blocks_dev // chunk):
        fetch(i).start()
    far_tiles = pltpu.make_async_copy(tiles_ref.at[:, pl.ds(NEAR, far_tiles_ref.shape[1])], far_tiles_ref, far_sem)
    far_tiles.start()
    take(own_ref, 1, own_sem).wait()
    take(chip_ref, 0, sems.at[0]).wait()
    take(chip_ref, 2, sems.at[1]).wait()

    base = (place - 1) * blocks_dev
    scale = 2.0 * eta_step / clusters

    def products(step):
        first = step * group
        if first % chunk == 0:
            fetch(first // chunk).wait()
        spreads = []
        for b in range(first, first + group):
            picked = [window[cols_ref[s, b] - base] for s in range(NEAR)]
            wide = jnp.concatenate([tiles[b, s] for s in range(NEAR)], axis=1)
            spreads.append(split(jnp.dot(wide, jnp.concatenate(picked, axis=0), preferred_element_type=f32)))
        return jnp.concatenate(spreads, axis=0)

    ahead = products(0)
    for step in range(steps):
        spreads = ahead
        if step + 1 < steps:
            ahead = products(step + 1)
        first = step * group
        affinity = jnp.dot(spreads, graph2_ref[...], preferred_element_type=f32)
        own = window[blocks_dev + first : blocks_dev + first + group].reshape(group * tile, clusters)
        part_ref[first * tile : (first + group) * tile, :] = (
            jnp.log(own.astype(f32)) - eta_step * pull_ref[0:1, :] + scale * affinity
        )
    far_tiles.wait()


def far_kernel(group, nodes_total, where_ref, tiles_ref, part_ref, graph2_ref, *refs):
    *found_refs, logits_ref, mass_ref, blocks_ref, sem = refs
    tile, clusters = blocks_ref.shape[1:]
    blocks_dev, far_slots = tiles_ref.shape[:2]
    steps = blocks_dev // group
    scale = 2.0 * eta_step / clusters
    width = found_refs[0].shape[0]
    for i, found in enumerate(found_refs):
        pltpu.make_async_copy(found, blocks_ref.at[pl.ds(i * width, width)], sem).start()
    pltpu.make_async_copy(blocks_ref, blocks_ref, sem).wait()

    def products(step):
        spreads = []
        for b in range(step * group, (step + 1) * group):
            picked = [blocks_ref[where_ref[b * far_slots + s]] for s in range(far_slots)]
            wide = jnp.concatenate([tiles_ref[b, s] for s in range(far_slots)], axis=1)
            spreads.append(split(jnp.dot(wide, jnp.concatenate(picked, axis=0), preferred_element_type=f32)))
        return jnp.concatenate(spreads, axis=0)

    total = jnp.zeros((8, clusters), f32)
    ahead = products(0)
    for step in range(steps):
        spreads = ahead
        if step + 1 < steps:
            ahead = products(step + 1)
        here = pl.ds(step * group * tile, group * tile)
        affinity = jnp.dot(spreads, graph2_ref[...], preferred_element_type=f32)
        logits = part_ref[here, :] + scale * affinity
        logits_ref[here, :] = logits
        total = total + jnp.sum(jnp.exp(logits).reshape(group * tile // 8, 8, clusters), axis=0)

    mass = jnp.sum(total, axis=0, keepdims=True) / nodes_total
    mass_ref[:, 0, :] = jnp.broadcast_to(mass, (mass_ref.shape[0], clusters))


def last_kernel(parts, logits_ref, mass_ref, target_ref, out_ref, kept, sems):
    newmass = jnp.sum(mass_ref[:, 0, :], axis=0, keepdims=True)
    shift = relax_power * (jnp.log(target_ref[...]) - jnp.log(newmass))
    rows = logits_ref.shape[0]
    step = rows // parts
    copies = []
    for i in range(parts):
        here = pl.ds(i * step, step)
        shifted = logits_ref[here, :] + shift
        kept[here, :] = shifted - jnp.log(jnp.sum(jnp.exp(shifted), axis=1, keepdims=True))
        copies.append(pltpu.make_async_copy(kept.at[here], out_ref.at[here], sems.at[i]))
        copies[-1].start()
    for copy in copies:
        copy.wait()


def local(coupling, tile_vals, tile_cols, cluster_graph, cluster_mass):
    shards = lax.axis_size(NODES)
    my_index = lax.axis_index(NODES)
    blocks_dev, slots = tile_cols.shape
    tile = tile_vals.shape[2]
    rows, clusters = coupling.shape
    far_slots = slots - NEAR
    nodes_total = rows * shards
    far_count = blocks_dev * far_slots
    cap = (far_count + shards - 1) // shards
    blocks = coupling.reshape(blocks_dev, tile, clusters)
    cols = tile_cols.T
    group = 4
    steps = blocks_dev // group
    flops = 2 * rows * clusters

    levels = shards // LEVEL
    others = order_of(levels)
    early = blocks_dev - blocks_dev * 3 // 8
    place = my_index.astype(i32).reshape(1)

    def swap(x, bits):
        return lax.ppermute(x, NODES, [(i, i ^ bits) for i in range(shards)])

    over = swap(blocks, 2)
    chip = swap(blocks, 1)

    *asked, mine, held, half = pl.pallas_call(
        functools.partial(requests_kernel, nodes_total),
        out_shape=(
            *[pltpu.VMEM((LEVEL + 1, 1, clusters), f32)] * levels,
            pltpu.VMEM((rows, clusters), bf16),
            pltpu.VMEM((early * tile, clusters), bf16),
        ),
        in_specs=[SMEM, ANY, ANY],
        out_specs=[VMEM] * (levels + 2),
        scratch_shapes=[
            pltpu.VMEM((slots, blocks_dev), i32),
            pltpu.VMEM((shards, 1, clusters), f32),
            pltpu.SemaphoreType.DMA,
            pltpu.SemaphoreType.DMA,
            pltpu.SemaphoreType.DMA,
        ],
        compiler_params=params(8),
        name="requests",
    )(place, in_hbm(cols), in_hbm(coupling))
    heard = [swap(x, dz * LEVEL) for dz, x in ((dz, asked[dz - 1]) for dz in others)]
    edges = [z * LEVEL for z in range(1, levels)]
    edge = lax.ppermute(half, NODES, [(i - 1, i + 2) for i in edges] + [(i, i - 3) for i in edges])

    def gather(stage, heard, sources):
        return pl.pallas_call(
            functools.partial(gather_kernel, cap, stage),
            out_shape=[pltpu.HBM((2 * cap, tile, clusters), bf16)] * len(heard),
            in_specs=[SMEM] + [VMEM] * (len(heard) + 2),
            out_specs=[ANY] * len(heard),
            scratch_shapes=[
                pltpu.VMEM((8 * len(heard), clusters), i32),
                pltpu.SMEM((8 * len(heard), clusters), i32),
                pltpu.SemaphoreType.DMA((len(heard) + 1,)),
            ],
            compiler_params=params(8),
        )(place, *[on_chip(x) for x in heard], *[on_chip(x) for x in sources])

    found = gather(0, heard, (held.reshape(blocks.shape), chip))
    fetched = [swap(x, dz * LEVEL) for dz, x in zip(others, found)]
    over_chip = swap(over, 1)
    beyond = lax.ppermute(
        over[early:], NODES, [(i - 3, i) for i in edges] + [(i + 2, i - 1) for i in edges]
    )
    edge = lax.ppermute(edge, NODES, [(i + 2, i) for i in edges] + [(i - 3, i - 1) for i in edges])
    found = gather(1, (*heard, mine), (over, over_chip))
    there = [swap(x, dz * LEVEL) for dz, x in zip(others, found)]
    home_late = found[-1]
    (home,) = gather(0, (mine,), (held.reshape(blocks.shape), chip))

    mass = mine[LEVEL]
    for x in heard:
        mass = mass + x[LEVEL]
    mass_chip = swap(mass, 1)
    mass = mass + mass_chip
    mass_over = swap(mass, 2)

    graph2, pull, where = pl.pallas_call(
        functools.partial(prep_kernel, cap, shards),
        out_shape=(
            pltpu.VMEM((2 * clusters, clusters), bf16),
            pltpu.VMEM((8, clusters), f32),
            jax.ShapeDtypeStruct((far_count,), i32),
        ),
        in_specs=[SMEM, SMEM, VMEM, VMEM, VMEM],
        out_specs=(VMEM, VMEM, SMEM),
        scratch_shapes=[pltpu.SMEM((shards,), i32)],
        compiler_params=params(4),
        name="prep",
    )(place, cols, cluster_graph, mass, mass_over)

    part, far_tiles = pl.pallas_call(
        functools.partial(near_kernel, group, group),
        out_shape=(
            pltpu.VMEM((rows, clusters), f32),
            pltpu.VMEM((blocks_dev, far_slots, tile, tile), bf16),
        ),
        in_specs=[SMEM, SMEM, ANY, ANY, ANY, ANY, ANY, ANY, VMEM, VMEM],
        out_specs=(VMEM, VMEM),
        scratch_shapes=[
            pltpu.VMEM((3 * blocks_dev, tile, clusters), bf16),
            pltpu.VMEM((blocks_dev, NEAR, tile, tile), bf16),
            pltpu.SemaphoreType.DMA,
            pltpu.SemaphoreType.DMA,
            pltpu.SemaphoreType.DMA((2,)),
            pltpu.SemaphoreType.DMA((steps,)),
        ],
        compiler_params=params(20),
        cost_estimate=pl.CostEstimate(
            flops=flops * (NEAR * tile + 2 * clusters), bytes_accessed=16 << 20, transcendentals=rows * clusters
        ),
        name="near",
    )(
        place, cols, in_hbm(blocks), chip, over_chip, edge.reshape(early, tile, clusters), beyond,
        in_hbm(tile_vals), on_chip(graph2), on_chip(pull),
    )

    at = [others.index(dz) for dz in range(1, levels)]
    parts = [home, *[fetched[i] for i in at], home_late, *[there[i] for i in at]]
    logits, mass_parts = pl.pallas_call(
        functools.partial(far_kernel, group, nodes_total),
        out_shape=(pltpu.VMEM((rows, clusters), f32), pltpu.VMEM((shards, 1, clusters), f32)),
        in_specs=[SMEM, VMEM, VMEM, VMEM] + [ANY] * len(parts),
        out_specs=(VMEM, VMEM),
        scratch_shapes=[pltpu.VMEM((2 * cap * len(parts), tile, clusters), bf16), pltpu.SemaphoreType.DMA],
        compiler_params=params(16),
        cost_estimate=pl.CostEstimate(
            flops=flops * (far_slots * tile + 2 * clusters), bytes_accessed=8 << 20, transcendentals=rows * clusters
        ),
        name="far",
    )(where, on_chip(far_tiles), on_chip(part), on_chip(graph2), *parts)

    masses = lax.all_to_all(mass_parts, NODES, split_axis=0, concat_axis=0, tiled=True)

    return pl.pallas_call(
        functools.partial(last_kernel, 8),
        out_shape=jax.ShapeDtypeStruct((rows, clusters), f32),
        in_specs=[VMEM, VMEM, VMEM],
        out_specs=ANY,
        scratch_shapes=[pltpu.VMEM((rows, clusters), f32), pltpu.SemaphoreType.DMA((8,))],
        compiler_params=params(8),
        name="last",
    )(on_chip(logits), on_chip(masses), cluster_mass.reshape(1, clusters))


def solution(mesh):
    return jax.shard_map(
        local,
        mesh=mesh,
        in_specs=(
            P(("groups", "rows", "sub"), None),
            P(("groups", "rows", "sub"), None, None, None),
            P(("groups", "rows", "sub"), None),
            P("groups", None),
            P("groups"),
        ),
        out_specs=P(("groups", "rows", "sub"), None),
        check_vma=False,
    )
```

```python
import functools

import jax
import jax.numpy as jnp
from jax import lax
from jax.experimental import pallas as pl
from jax.experimental.pallas import tpu as pltpu
from jax.sharding import PartitionSpec as P


NEAR = 4
LEVEL = 4
NODES = ("rows", "sub")

eta_step = 2.0
relax_power = 0.5

ANY = pl.BlockSpec(memory_space=pl.ANY)
VMEM = pl.BlockSpec(memory_space=pltpu.VMEM)
SMEM = pl.BlockSpec(memory_space=pltpu.SMEM)

f32, bf16, i32 = jnp.float32, jnp.bfloat16, jnp.int32


def order_of(levels):
    return [*range(levels // 2, levels), *range(1, levels // 2)]


def on_chip(x):
    return pltpu.with_memory_space_constraint(x, pltpu.VMEM)


def in_hbm(x):
    return pltpu.with_memory_space_constraint(x, pltpu.HBM)


def params(mib):
    return pltpu.CompilerParams(vmem_limit_bytes=mib << 20)


def requests_kernel(nodes_total, place_ref, all_cols_ref, coupling_ref, *refs):
    *out_refs, own_ref, rows, half_ref, cols_ref, table_ref, cols_sem, half_sem, sem = refs
    slots, blocks_dev = cols_ref.shape
    cols_copy = pltpu.make_async_copy(all_cols_ref, cols_ref, cols_sem)
    cols_copy.start()
    shards = table_ref.shape[0]
    nodes, clusters = coupling_ref.shape
    coupling_copy = pltpu.make_async_copy(coupling_ref, rows, sem)
    coupling_copy.start()
    half_copy = pltpu.make_async_copy(coupling_ref.at[pl.ds(0, half_ref.shape[0])], half_ref, half_sem)
    half_copy.start()

    count = (slots - NEAR) * blocks_dev
    exact = bf16 if blocks_dev <= 256 else f32
    owner = lax.broadcasted_iota(i32, (shards, count), 0)
    place = lax.broadcasted_iota(i32, (clusters, count), 0).astype(f32)
    before = (
        lax.broadcasted_iota(i32, (count, count), 0) < lax.broadcasted_iota(i32, (count, count), 1)
    ).astype(bf16)
    cols_copy.wait()
    coupling_copy.wait()
    far_cols = jnp.concatenate([cols_ref[s : s + 1, :] for s in range(NEAR, slots)], axis=1)
    local = far_cols - owner * blocks_dev
    hit = (local >= 0) & (local < blocks_dev)
    hits = hit.astype(f32)
    earlier = jnp.dot(hits.astype(bf16), before, preferred_element_type=f32)
    rank = jnp.sum(earlier * hits, axis=0, keepdims=True)
    table = lax.dot_general(
        jnp.where(hit, local, 0).astype(f32).astype(exact),
        (rank == place).astype(f32).astype(exact),
        (((1,), (1,)), ((), ())),
        precision=None if exact == bf16 else lax.Precision.HIGHEST,
        preferred_element_type=f32,
    )
    table_ref[:, 0, :] = table
    level = place_ref[0] // LEVEL
    for dz, ref in enumerate((own_ref, *out_refs)):
        for row in range(LEVEL):
            ref[row] = table_ref[(level ^ dz) * LEVEL + row]
    part = rows[...].astype(f32)
    mass = jnp.sum(jnp.sum(part.reshape(nodes // 8, 8, clusters), axis=0), axis=0, keepdims=True) / nodes_total
    for ref in (own_ref, *out_refs):
        ref[LEVEL] = mass
    half_copy.wait()


def gather_kernel(cap, stage, place_ref, *refs):
    count = (len(refs) - 5) // 2
    heard_refs, sources, out_refs = refs[:count], refs[count : count + 2], refs[count + 2 : 2 * count + 2]
    wanted_ref, wanted_smem, sem = refs[2 * count + 2 :]
    for n, heard in enumerate(heard_refs):
        wanted_ref[n * 8 : n * 8 + LEVEL, :] = heard[:LEVEL, 0, :].astype(i32)
    copy = pltpu.make_async_copy(wanted_ref, wanted_smem, sem)
    copy.start()
    copy.wait()
    spot = place_ref[0] % LEVEL
    for n, out_ref in enumerate(out_refs):
        for sub, src in enumerate(sources):
            row = n * 8 + (spot ^ (2 * stage + sub))
            for j in range(cap):
                out_ref[sub * cap + j] = src[wanted_smem[row, j]]


def split(x):
    high = x.astype(bf16)
    return jnp.concatenate([high, (x - high.astype(f32)).astype(bf16)], axis=1)


def prep_kernel(cap, shards, place_ref, cols_ref, graph_ref, all_tiles_ref, *refs):
    *mass_refs, graph2_ref, pull_ref, where_ref, tiles_ref, count_ref, sem = refs
    tiles_copy = pltpu.make_async_copy(all_tiles_ref, tiles_ref, sem)
    tiles_copy.start()
    slots, blocks_dev = cols_ref.shape
    clusters = graph_ref.shape[0]
    spot, level = place_ref[0] % LEVEL, place_ref[0] // LEVEL
    graph = graph_ref[...].astype(f32)
    colmass = mass_refs[0][...]
    for ref in mass_refs[1:]:
        colmass = colmass + ref[...]
    pull_ref[...] = (
        lax.dot_general(
            jnp.broadcast_to(colmass, (8, clusters)),
            graph * graph,
            (((1,), (1,)), ((), ())),
            precision=lax.Precision.HIGHEST,
            preferred_element_type=f32,
        )
        / clusters
    )
    turned = graph.T.astype(bf16)
    graph2_ref[:clusters, :] = turned
    graph2_ref[clusters:, :] = turned

    @pl.loop(0, shards)
    def _(o):
        count_ref[o] = 0

    for slot_id in range(NEAR, slots):

        @pl.loop(0, blocks_dev)
        def _(b):
            owner = cols_ref[slot_id, b] // blocks_dev
            rank = count_ref[owner]
            count_ref[owner] = rank + 1
            turn = (owner % LEVEL) ^ spot
            row = ((turn // 2) * (shards // LEVEL) + ((owner // LEVEL) ^ level)) * 2 + turn % 2
            where_ref[b * (slots - NEAR) + slot_id - NEAR] = row * cap + rank

    tiles_copy.wait()


def near_kernel(
    group, place_ref, cols_ref, own_ref, chip_ref, level_ref, edge_ref, beyond_ref, tiles_ref,
    graph2_ref, pull_ref, part_ref, window, own_sem, sems,
):
    blocks_dev, tile, clusters = own_ref.shape
    steps = blocks_dev // group
    place = place_ref[0]
    spot = place % LEVEL

    def take(src, i, sem):
        return pltpu.make_async_copy(src, window.at[pl.ds(i * blocks_dev, blocks_dev)], sem)

    take(own_ref, 1, own_sem).start()
    even = spot % 2 == 0
    edge = (spot == 0) | (spot == LEVEL - 1)
    early, late = edge_ref.shape[0], beyond_ref.shape[0]
    for is_even, chip_at, other_at in ((True, 2, 0), (False, 0, 2)):

        @pl.when(even == is_even)
        def _():
            take(chip_ref, chip_at, sems.at[0]).start()

        @pl.when((even == is_even) & jnp.logical_not(edge))
        def _():
            take(level_ref, other_at, sems.at[1]).start()

        @pl.when((even == is_even) & edge)
        def _():
            low = window.at[pl.ds(other_at * blocks_dev, early)]
            high = window.at[pl.ds(other_at * blocks_dev + early, late)]
            pltpu.make_async_copy(edge_ref, low, sems.at[1]).start()
            pltpu.make_async_copy(beyond_ref, high, sems.at[1]).start()

    take(own_ref, 1, own_sem).wait()
    take(chip_ref, 0, sems.at[0]).wait()
    take(chip_ref, 2, sems.at[1]).wait()

    base = (place - 1) * blocks_dev
    scale = 2.0 * eta_step / clusters

    def products(step):
        spreads = []
        for b in range(step * group, (step + 1) * group):
            picked = [window[cols_ref[s, b] - base] for s in range(NEAR)]
            wide = jnp.concatenate([tiles_ref[b, s] for s in range(NEAR)], axis=1)
            spreads.append(split(jnp.dot(wide, jnp.concatenate(picked, axis=0), preferred_element_type=f32)))
        return jnp.concatenate(spreads, axis=0)

    ahead = products(0)
    for step in range(steps):
        spreads = ahead
        if step + 1 < steps:
            ahead = products(step + 1)
        first = step * group
        affinity = jnp.dot(spreads, graph2_ref[...], preferred_element_type=f32)
        own = window[blocks_dev + first : blocks_dev + first + group].reshape(group * tile, clusters)
        part_ref[first * tile : (first + group) * tile, :] = (
            jnp.log(own.astype(f32)) - eta_step * pull_ref[0:1, :] + scale * affinity
        )


def far_kernel(group, nodes_total, where_ref, tiles_ref, part_ref, graph2_ref, *refs):
    *found_refs, logits_ref, mass_ref, blocks_ref, sem = refs
    tile, clusters = blocks_ref.shape[1:]
    blocks_dev, slots = tiles_ref.shape[:2]
    far_slots = slots - NEAR
    steps = blocks_dev // group
    scale = 2.0 * eta_step / clusters
    width = found_refs[0].shape[0]
    for i, found in enumerate(found_refs):
        pltpu.make_async_copy(found, blocks_ref.at[pl.ds(i * width, width)], sem).start()
    pltpu.make_async_copy(blocks_ref, blocks_ref, sem).wait()

    def products(step):
        spreads = []
        for b in range(step * group, (step + 1) * group):
            picked = [blocks_ref[where_ref[b * far_slots + s]] for s in range(far_slots)]
            wide = jnp.concatenate([tiles_ref[b, s] for s in range(NEAR, slots)], axis=1)
            spreads.append(split(jnp.dot(wide, jnp.concatenate(picked, axis=0), preferred_element_type=f32)))
        return jnp.concatenate(spreads, axis=0)

    total = jnp.zeros((8, clusters), f32)
    ahead = products(0)
    for step in range(steps):
        spreads = ahead
        if step + 1 < steps:
            ahead = products(step + 1)
        here = pl.ds(step * group * tile, group * tile)
        affinity = jnp.dot(spreads, graph2_ref[...], preferred_element_type=f32)
        logits = part_ref[here, :] + scale * affinity
        logits_ref[here, :] = logits
        total = total + jnp.sum(jnp.exp(logits).reshape(group * tile // 8, 8, clusters), axis=0)

    mass = jnp.sum(total, axis=0, keepdims=True) / nodes_total
    mass_ref[:, 0, :] = jnp.broadcast_to(mass, (mass_ref.shape[0], clusters))


def last_kernel(parts, logits_ref, mass_ref, target_ref, out_ref, kept, sems):
    newmass = jnp.sum(mass_ref[:, 0, :], axis=0, keepdims=True)
    shift = relax_power * (jnp.log(target_ref[...]) - jnp.log(newmass))
    rows = logits_ref.shape[0]
    step = rows // parts
    copies = []
    for i in range(parts):
        here = pl.ds(i * step, step)
        shifted = logits_ref[here, :] + shift
        kept[here, :] = shifted - jnp.log(jnp.sum(jnp.exp(shifted), axis=1, keepdims=True))
        copies.append(pltpu.make_async_copy(kept.at[here], out_ref.at[here], sems.at[i]))
        copies[-1].start()
    for copy in copies:
        copy.wait()


def local(coupling, tile_vals, tile_cols, cluster_graph, cluster_mass):
    shards = lax.axis_size(NODES)
    my_index = lax.axis_index(NODES)
    blocks_dev, slots = tile_cols.shape
    tile = tile_vals.shape[2]
    rows, clusters = coupling.shape
    far_slots = slots - NEAR
    nodes_total = rows * shards
    far_count = blocks_dev * far_slots
    cap = (far_count + shards - 1) // shards
    blocks = coupling.reshape(blocks_dev, tile, clusters)
    cols = tile_cols.T
    group = 4
    flops = 2 * rows * clusters

    levels = shards // LEVEL
    others = order_of(levels)
    early = blocks_dev - blocks_dev * 7 // 16
    place = my_index.astype(i32).reshape(1)

    def swap(x, bits):
        return lax.ppermute(x, NODES, [(i, i ^ bits) for i in range(shards)])

    over = swap(blocks, 2)
    chip = swap(blocks, 1)
    *asked, mine, held, half = pl.pallas_call(
        functools.partial(requests_kernel, nodes_total),
        out_shape=(
            *[pltpu.VMEM((LEVEL + 1, 1, clusters), f32)] * levels,
            pltpu.VMEM((rows, clusters), bf16),
            pltpu.VMEM((early * tile, clusters), bf16),
        ),
        in_specs=[SMEM, ANY, ANY],
        out_specs=[VMEM] * (levels + 2),
        scratch_shapes=[
            pltpu.VMEM((slots, blocks_dev), i32),
            pltpu.VMEM((shards, 1, clusters), f32),
            pltpu.SemaphoreType.DMA,
            pltpu.SemaphoreType.DMA,
            pltpu.SemaphoreType.DMA,
        ],
        compiler_params=params(8),
        name="requests",
    )(place, in_hbm(cols), in_hbm(coupling))
    heard = [swap(x, dz * LEVEL) for dz, x in ((dz, asked[dz - 1]) for dz in others)]
    edges = [z * LEVEL for z in range(1, levels)]
    edge = lax.ppermute(half, NODES, [(i - 1, i + 2) for i in edges] + [(i, i - 3) for i in edges])

    def gather(stage, heard, sources):
        return pl.pallas_call(
            functools.partial(gather_kernel, cap, stage),
            out_shape=[pltpu.VMEM((2 * cap, tile, clusters), bf16)] * len(heard),
            in_specs=[SMEM] + [VMEM] * (len(heard) + 2),
            out_specs=[VMEM] * len(heard),
            scratch_shapes=[
                pltpu.VMEM((8 * len(heard), clusters), i32),
                pltpu.SMEM((8 * len(heard), clusters), i32),
                pltpu.SemaphoreType.DMA,
            ],
            compiler_params=params(8),
        )(place, *[on_chip(x) for x in heard], *[on_chip(x) for x in sources])

    found = gather(0, heard, (held.reshape(blocks.shape), chip))
    fetched = [swap(x, dz * LEVEL) for dz, x in zip(others, found)]
    over_chip = swap(over, 1)
    beyond = lax.ppermute(
        over[early:], NODES, [(i - 3, i) for i in edges] + [(i + 2, i - 1) for i in edges]
    )
    edge = lax.ppermute(edge, NODES, [(i + 2, i) for i in edges] + [(i - 3, i - 1) for i in edges])
    found = gather(1, (*heard, mine), (over, over_chip))
    there = [swap(x, dz * LEVEL) for dz, x in zip(others, found)]
    home_late = found[-1]
    (home,) = gather(0, (mine,), (held.reshape(blocks.shape), chip))

    mass = mine[LEVEL]
    for x in heard:
        mass = mass + x[LEVEL]
    mass_chip = swap(mass, 1)
    mass = mass + mass_chip
    mass_over = swap(mass, 2)

    graph2, pull, where, tiles = pl.pallas_call(
        functools.partial(prep_kernel, cap, shards),
        out_shape=(
            pltpu.VMEM((2 * clusters, clusters), bf16),
            pltpu.VMEM((8, clusters), f32),
            jax.ShapeDtypeStruct((far_count,), i32),
            pltpu.VMEM(tile_vals.shape, bf16),
        ),
        in_specs=[SMEM, SMEM, VMEM, ANY, VMEM, VMEM],
        out_specs=(VMEM, VMEM, SMEM, VMEM),
        scratch_shapes=[pltpu.SMEM((shards,), i32), pltpu.SemaphoreType.DMA],
        compiler_params=params(4),
        name="prep",
    )(place, cols, cluster_graph, in_hbm(tile_vals), mass, mass_over)

    part = pl.pallas_call(
        functools.partial(near_kernel, group),
        out_shape=pltpu.VMEM((rows, clusters), f32),
        in_specs=[SMEM, SMEM, ANY, ANY, ANY, ANY, ANY, VMEM, VMEM, VMEM],
        out_specs=VMEM,
        scratch_shapes=[
            pltpu.VMEM((3 * blocks_dev, tile, clusters), bf16),
            pltpu.SemaphoreType.DMA,
            pltpu.SemaphoreType.DMA((2,)),
        ],
        compiler_params=params(8),
        cost_estimate=pl.CostEstimate(
            flops=flops * (NEAR * tile + 2 * clusters), bytes_accessed=16 << 20, transcendentals=rows * clusters
        ),
        name="near",
    )(
        place, cols, held.reshape(blocks.shape), chip, over_chip, edge.reshape(early, tile, clusters), beyond,
        on_chip(tiles), on_chip(graph2), on_chip(pull),
    )

    at = [others.index(dz) for dz in range(1, levels)]
    parts = [home, *[fetched[i] for i in at], home_late, *[there[i] for i in at]]
    logits, mass_parts = pl.pallas_call(
        functools.partial(far_kernel, group, nodes_total),
        out_shape=(pltpu.VMEM((rows, clusters), f32), pltpu.VMEM((shards, 1, clusters), f32)),
        in_specs=[SMEM, VMEM, VMEM, VMEM] + [ANY] * len(parts),
        out_specs=(VMEM, VMEM),
        scratch_shapes=[pltpu.VMEM((2 * cap * len(parts), tile, clusters), bf16), pltpu.SemaphoreType.DMA],
        compiler_params=params(8),
        cost_estimate=pl.CostEstimate(
            flops=flops * (far_slots * tile + 2 * clusters), bytes_accessed=8 << 20, transcendentals=rows * clusters
        ),
        name="far",
    )(where, on_chip(tiles), on_chip(part), on_chip(graph2), *parts)

    masses = lax.all_to_all(mass_parts, NODES, split_axis=0, concat_axis=0, tiled=True)

    return pl.pallas_call(
        functools.partial(last_kernel, 8),
        out_shape=jax.ShapeDtypeStruct((rows, clusters), f32),
        in_specs=[VMEM, VMEM, VMEM],
        out_specs=ANY,
        scratch_shapes=[pltpu.VMEM((rows, clusters), f32), pltpu.SemaphoreType.DMA((8,))],
        compiler_params=params(8),
        name="last",
    )(on_chip(logits), on_chip(masses), cluster_mass.reshape(1, clusters))


def solution(mesh):
    return jax.shard_map(
        local,
        mesh=mesh,
        in_specs=(
            P(("groups", "rows", "sub"), None),
            P(("groups", "rows", "sub"), None, None, None),
            P(("groups", "rows", "sub"), None),
            P("groups", None),
            P("groups"),
        ),
        out_specs=P(("groups", "rows", "sub"), None),
        check_vma=False,
    )
```

```python
import functools

import jax
import jax.numpy as jnp
from jax import lax
from jax.experimental import pallas as pl
from jax.experimental.pallas import tpu as pltpu
from jax.sharding import PartitionSpec as P


NEAR = 4
LEVEL = 4
NODES = ("rows", "sub")

eta_step = 2.0
relax_power = 0.5

ANY = pl.BlockSpec(memory_space=pl.ANY)
VMEM = pl.BlockSpec(memory_space=pltpu.VMEM)
SMEM = pl.BlockSpec(memory_space=pltpu.SMEM)

f32, bf16, i32 = jnp.float32, jnp.bfloat16, jnp.int32


def order_of(levels):
    return [*range(levels // 2, levels), *range(1, levels // 2)]


def on_chip(x):
    return pltpu.with_memory_space_constraint(x, pltpu.VMEM)


def in_hbm(x):
    return pltpu.with_memory_space_constraint(x, pltpu.HBM)


def params(mib):
    return pltpu.CompilerParams(vmem_limit_bytes=mib << 20)


def requests_kernel(nodes_total, place_ref, all_cols_ref, coupling_ref, *refs):
    *out_refs, own_ref, rows, half_ref, cols_ref, table_ref, cols_sem, half_sem, sem = refs
    slots, blocks_dev = cols_ref.shape
    cols_copy = pltpu.make_async_copy(all_cols_ref, cols_ref, cols_sem)
    cols_copy.start()
    shards = table_ref.shape[0]
    nodes, clusters = coupling_ref.shape
    coupling_copy = pltpu.make_async_copy(coupling_ref, rows, sem)
    coupling_copy.start()
    half_copy = pltpu.make_async_copy(coupling_ref.at[pl.ds(0, half_ref.shape[0])], half_ref, half_sem)
    half_copy.start()

    count = (slots - NEAR) * blocks_dev
    exact = bf16 if blocks_dev <= 256 else f32
    owner = lax.broadcasted_iota(i32, (shards, count), 0)
    place = lax.broadcasted_iota(i32, (clusters, count), 0).astype(f32)
    before = (
        lax.broadcasted_iota(i32, (count, count), 0) < lax.broadcasted_iota(i32, (count, count), 1)
    ).astype(bf16)
    cols_copy.wait()
    coupling_copy.wait()
    far_cols = jnp.concatenate([cols_ref[s : s + 1, :] for s in range(NEAR, slots)], axis=1)
    local = far_cols - owner * blocks_dev
    hit = (local >= 0) & (local < blocks_dev)
    hits = hit.astype(f32)
    earlier = jnp.dot(hits.astype(bf16), before, preferred_element_type=f32)
    rank = jnp.sum(earlier * hits, axis=0, keepdims=True)
    table = lax.dot_general(
        jnp.where(hit, local, 0).astype(f32).astype(exact),
        (rank == place).astype(f32).astype(exact),
        (((1,), (1,)), ((), ())),
        precision=None if exact == bf16 else lax.Precision.HIGHEST,
        preferred_element_type=f32,
    )
    table_ref[:, 0, :] = table
    level = place_ref[0] // LEVEL
    for dz, ref in enumerate((own_ref, *out_refs)):
        for row in range(LEVEL):
            ref[row] = table_ref[(level ^ dz) * LEVEL + row]
    part = rows[...].astype(f32)
    mass = jnp.sum(jnp.sum(part.reshape(nodes // 8, 8, clusters), axis=0), axis=0, keepdims=True) / nodes_total
    for ref in (own_ref, *out_refs):
        ref[LEVEL] = mass
    half_copy.wait()


def gather_kernel(cap, stage, place_ref, *refs):
    count = (len(refs) - 5) // 2
    heard_refs, sources, out_refs = refs[:count], refs[count : count + 2], refs[count + 2 : 2 * count + 2]
    wanted_ref, wanted_smem, sem = refs[2 * count + 2 :]
    for n, heard in enumerate(heard_refs):
        wanted_ref[n * 8 : n * 8 + LEVEL, :] = heard[:LEVEL, 0, :].astype(i32)
    copy = pltpu.make_async_copy(wanted_ref, wanted_smem, sem)
    copy.start()
    copy.wait()
    spot = place_ref[0] % LEVEL
    for n, out_ref in enumerate(out_refs):
        for sub, src in enumerate(sources):
            row = n * 8 + (spot ^ (2 * stage + sub))
            for j in range(cap):
                out_ref[sub * cap + j] = src[wanted_smem[row, j]]


def split(x):
    high = x.astype(bf16)
    return jnp.concatenate([high, (x - high.astype(f32)).astype(bf16)], axis=1)


def prep_kernel(cap, shards, place_ref, cols_ref, graph_ref, all_tiles_ref, *refs):
    *mass_refs, graph2_ref, pull_ref, where_ref, tiles_ref, count_ref, sem = refs
    tiles_copy = pltpu.make_async_copy(all_tiles_ref, tiles_ref, sem)
    tiles_copy.start()
    slots, blocks_dev = cols_ref.shape
    clusters = graph_ref.shape[0]
    spot, level = place_ref[0] % LEVEL, place_ref[0] // LEVEL
    graph = graph_ref[...].astype(f32)
    colmass = mass_refs[0][...]
    for ref in mass_refs[1:]:
        colmass = colmass + ref[...]
    pull_ref[...] = (
        lax.dot_general(
            jnp.broadcast_to(colmass, (8, clusters)),
            graph * graph,
            (((1,), (1,)), ((), ())),
            precision=lax.Precision.HIGHEST,
            preferred_element_type=f32,
        )
        / clusters
    )
    turned = graph.T.astype(bf16)
    graph2_ref[:clusters, :] = turned
    graph2_ref[clusters:, :] = turned

    @pl.loop(0, shards)
    def _(o):
        count_ref[o] = 0

    for slot_id in range(NEAR, slots):

        @pl.loop(0, blocks_dev)
        def _(b):
            owner = cols_ref[slot_id, b] // blocks_dev
            rank = count_ref[owner]
            count_ref[owner] = rank + 1
            turn = (owner % LEVEL) ^ spot
            row = ((turn // 2) * (shards // LEVEL) + ((owner // LEVEL) ^ level)) * 2 + turn % 2
            where_ref[b * (slots - NEAR) + slot_id - NEAR] = row * cap + rank

    tiles_copy.wait()


def near_kernel(
    group, place_ref, cols_ref, own_ref, chip_ref, level_ref, edge_ref, beyond_ref, tiles_ref,
    graph2_ref, pull_ref, part_ref, window, own_sem, sems,
):
    blocks_dev, tile, clusters = own_ref.shape
    steps = blocks_dev // group
    place = place_ref[0]
    spot = place % LEVEL

    def take(src, i, sem):
        return pltpu.make_async_copy(src, window.at[pl.ds(i * blocks_dev, blocks_dev)], sem)

    take(own_ref, 1, own_sem).start()
    even = spot % 2 == 0
    edge = (spot == 0) | (spot == LEVEL - 1)
    early, late = edge_ref.shape[0], beyond_ref.shape[0]
    for is_even, chip_at, other_at in ((True, 2, 0), (False, 0, 2)):

        @pl.when(even == is_even)
        def _():
            take(chip_ref, chip_at, sems.at[0]).start()

        @pl.when((even == is_even) & jnp.logical_not(edge))
        def _():
            take(level_ref, other_at, sems.at[1]).start()

        @pl.when((even == is_even) & edge)
        def _():
            low = window.at[pl.ds(other_at * blocks_dev, early)]
            high = window.at[pl.ds(other_at * blocks_dev + early, late)]
            pltpu.make_async_copy(edge_ref, low, sems.at[1]).start()
            pltpu.make_async_copy(beyond_ref, high, sems.at[1]).start()

    take(own_ref, 1, own_sem).wait()
    take(chip_ref, 0, sems.at[0]).wait()
    take(chip_ref, 2, sems.at[1]).wait()

    base = (place - 1) * blocks_dev
    scale = 2.0 * eta_step / clusters

    def products(step):
        spreads = []
        for b in range(step * group, (step + 1) * group):
            picked = [window[cols_ref[s, b] - base] for s in range(NEAR)]
            wide = jnp.concatenate([tiles_ref[b, s] for s in range(NEAR)], axis=1)
            spreads.append(split(jnp.dot(wide, jnp.concatenate(picked, axis=0), preferred_element_type=f32)))
        return jnp.concatenate(spreads, axis=0)

    ahead = products(0)
    for step in range(steps):
        spreads = ahead
        if step + 1 < steps:
            ahead = products(step + 1)
        first = step * group
        affinity = jnp.dot(spreads, graph2_ref[...], preferred_element_type=f32)
        own = window[blocks_dev + first : blocks_dev + first + group].reshape(group * tile, clusters)
        part_ref[first * tile : (first + group) * tile, :] = (
            jnp.log(own.astype(f32)) - eta_step * pull_ref[0:1, :] + scale * affinity
        )


def far_kernel(group, nodes_total, where_ref, tiles_ref, part_ref, graph2_ref, *refs):
    *found_refs, logits_ref, mass_ref, blocks_ref, sem = refs
    tile, clusters = blocks_ref.shape[1:]
    blocks_dev, slots = tiles_ref.shape[:2]
    far_slots = slots - NEAR
    steps = blocks_dev // group
    scale = 2.0 * eta_step / clusters
    width = found_refs[0].shape[0]
    for i, found in enumerate(found_refs):
        pltpu.make_async_copy(found, blocks_ref.at[pl.ds(i * width, width)], sem).start()
    pltpu.make_async_copy(blocks_ref, blocks_ref, sem).wait()

    def products(step):
        spreads = []
        for b in range(step * group, (step + 1) * group):
            picked = [blocks_ref[where_ref[b * far_slots + s]] for s in range(far_slots)]
            wide = jnp.concatenate([tiles_ref[b, s] for s in range(NEAR, slots)], axis=1)
            spreads.append(split(jnp.dot(wide, jnp.concatenate(picked, axis=0), preferred_element_type=f32)))
        return jnp.concatenate(spreads, axis=0)

    total = jnp.zeros((8, clusters), f32)
    ahead = products(0)
    for step in range(steps):
        spreads = ahead
        if step + 1 < steps:
            ahead = products(step + 1)
        here = pl.ds(step * group * tile, group * tile)
        affinity = jnp.dot(spreads, graph2_ref[...], preferred_element_type=f32)
        logits = part_ref[here, :] + scale * affinity
        logits_ref[here, :] = logits
        total = total + jnp.sum(jnp.exp(logits).reshape(group * tile // 8, 8, clusters), axis=0)

    mass = jnp.sum(total, axis=0, keepdims=True) / nodes_total
    mass_ref[:, 0, :] = jnp.broadcast_to(mass, (mass_ref.shape[0], clusters))


def last_kernel(parts, logits_ref, mass_ref, target_ref, out_ref, kept, sems):
    newmass = jnp.sum(mass_ref[:, 0, :], axis=0, keepdims=True)
    shift = relax_power * (jnp.log(target_ref[...]) - jnp.log(newmass))
    rows = logits_ref.shape[0]
    step = rows // parts
    copies = []
    for i in range(parts):
        here = pl.ds(i * step, step)
        shifted = logits_ref[here, :] + shift
        kept[here, :] = shifted - jnp.log(jnp.sum(jnp.exp(shifted), axis=1, keepdims=True))
        copies.append(pltpu.make_async_copy(kept.at[here], out_ref.at[here], sems.at[i]))
        copies[-1].start()
    for copy in copies:
        copy.wait()


def local(coupling, tile_vals, tile_cols, cluster_graph, cluster_mass):
    shards = lax.axis_size(NODES)
    my_index = lax.axis_index(NODES)
    blocks_dev, slots = tile_cols.shape
    tile = tile_vals.shape[2]
    rows, clusters = coupling.shape
    far_slots = slots - NEAR
    nodes_total = rows * shards
    far_count = blocks_dev * far_slots
    cap = (far_count + shards - 1) // shards
    blocks = coupling.reshape(blocks_dev, tile, clusters)
    cols = tile_cols.T
    group = 4
    flops = 2 * rows * clusters

    levels = shards // LEVEL
    others = order_of(levels)
    early = blocks_dev - blocks_dev * 3 // 8
    place = my_index.astype(i32).reshape(1)

    def swap(x, bits):
        return lax.ppermute(x, NODES, [(i, i ^ bits) for i in range(shards)])

    over = swap(blocks, 2)
    chip = swap(blocks, 1)
    *asked, mine, held, half = pl.pallas_call(
        functools.partial(requests_kernel, nodes_total),
        out_shape=(
            *[pltpu.VMEM((LEVEL + 1, 1, clusters), f32)] * levels,
            pltpu.VMEM((rows, clusters), bf16),
            pltpu.VMEM((early * tile, clusters), bf16),
        ),
        in_specs=[SMEM, ANY, ANY],
        out_specs=[VMEM] * (levels + 2),
        scratch_shapes=[
            pltpu.VMEM((slots, blocks_dev), i32),
            pltpu.VMEM((shards, 1, clusters), f32),
            pltpu.SemaphoreType.DMA,
            pltpu.SemaphoreType.DMA,
            pltpu.SemaphoreType.DMA,
        ],
        compiler_params=params(8),
        name="requests",
    )(place, in_hbm(cols), in_hbm(coupling))
    heard = [swap(x, dz * LEVEL) for dz, x in ((dz, asked[dz - 1]) for dz in others)]
    edges = [z * LEVEL for z in range(1, levels)]
    edge = lax.ppermute(half, NODES, [(i - 1, i + 2) for i in edges] + [(i, i - 3) for i in edges])

    def gather(stage, heard, sources):
        return pl.pallas_call(
            functools.partial(gather_kernel, cap, stage),
            out_shape=[pltpu.VMEM((2 * cap, tile, clusters), bf16)] * len(heard),
            in_specs=[SMEM] + [VMEM] * (len(heard) + 2),
            out_specs=[VMEM] * len(heard),
            scratch_shapes=[
                pltpu.VMEM((8 * len(heard), clusters), i32),
                pltpu.SMEM((8 * len(heard), clusters), i32),
                pltpu.SemaphoreType.DMA,
            ],
            compiler_params=params(8),
        )(place, *[on_chip(x) for x in heard], *[on_chip(x) for x in sources])

    far_levels = levels - levels // 2
    own_chip = (held.reshape(blocks.shape), chip)
    found = [*gather(0, heard[:far_levels], own_chip)]
    if far_levels < len(others):
        found += gather(0, heard[far_levels:], own_chip)
    fetched = [swap(x, dz * LEVEL) for dz, x in zip(others, found)]
    over_chip = swap(over, 1)
    beyond = lax.ppermute(
        over[early:], NODES, [(i - 3, i) for i in edges] + [(i + 2, i - 1) for i in edges]
    )
    edge = lax.ppermute(edge, NODES, [(i + 2, i) for i in edges] + [(i - 3, i - 1) for i in edges])
    found = gather(1, (*heard, mine), (over, over_chip))
    there = [swap(x, dz * LEVEL) for dz, x in zip(others, found)]
    home_late = found[-1]
    (home,) = gather(0, (mine,), (held.reshape(blocks.shape), chip))

    mass = mine[LEVEL]
    for x in heard:
        mass = mass + x[LEVEL]
    mass_chip = swap(mass, 1)
    mass = mass + mass_chip
    mass_over = swap(mass, 2)

    graph2, pull, where, tiles = pl.pallas_call(
        functools.partial(prep_kernel, cap, shards),
        out_shape=(
            pltpu.VMEM((2 * clusters, clusters), bf16),
            pltpu.VMEM((8, clusters), f32),
            jax.ShapeDtypeStruct((far_count,), i32),
            pltpu.VMEM(tile_vals.shape, bf16),
        ),
        in_specs=[SMEM, SMEM, VMEM, ANY, VMEM, VMEM],
        out_specs=(VMEM, VMEM, SMEM, VMEM),
        scratch_shapes=[pltpu.SMEM((shards,), i32), pltpu.SemaphoreType.DMA],
        compiler_params=params(4),
        name="prep",
    )(place, cols, cluster_graph, in_hbm(tile_vals), mass, mass_over)

    part = pl.pallas_call(
        functools.partial(near_kernel, group),
        out_shape=pltpu.VMEM((rows, clusters), f32),
        in_specs=[SMEM, SMEM, ANY, ANY, ANY, ANY, ANY, VMEM, VMEM, VMEM],
        out_specs=VMEM,
        scratch_shapes=[
            pltpu.VMEM((3 * blocks_dev, tile, clusters), bf16),
            pltpu.SemaphoreType.DMA,
            pltpu.SemaphoreType.DMA((2,)),
        ],
        compiler_params=params(8),
        cost_estimate=pl.CostEstimate(
            flops=flops * (NEAR * tile + 2 * clusters), bytes_accessed=16 << 20, transcendentals=rows * clusters
        ),
        name="near",
    )(
        place, cols, held.reshape(blocks.shape), chip, over_chip, edge.reshape(early, tile, clusters), beyond,
        on_chip(tiles), on_chip(graph2), on_chip(pull),
    )

    at = [others.index(dz) for dz in range(1, levels)]
    parts = [home, *[fetched[i] for i in at], home_late, *[there[i] for i in at]]
    logits, mass_parts = pl.pallas_call(
        functools.partial(far_kernel, group, nodes_total),
        out_shape=(pltpu.VMEM((rows, clusters), f32), pltpu.VMEM((shards, 1, clusters), f32)),
        in_specs=[SMEM, VMEM, VMEM, VMEM] + [ANY] * len(parts),
        out_specs=(VMEM, VMEM),
        scratch_shapes=[pltpu.VMEM((2 * cap * len(parts), tile, clusters), bf16), pltpu.SemaphoreType.DMA],
        compiler_params=params(8),
        cost_estimate=pl.CostEstimate(
            flops=flops * (far_slots * tile + 2 * clusters), bytes_accessed=8 << 20, transcendentals=rows * clusters
        ),
        name="far",
    )(where, on_chip(tiles), on_chip(part), on_chip(graph2), *parts)

    masses = lax.all_to_all(mass_parts, NODES, split_axis=0, concat_axis=0, tiled=True)

    return pl.pallas_call(
        functools.partial(last_kernel, 8),
        out_shape=jax.ShapeDtypeStruct((rows, clusters), f32),
        in_specs=[VMEM, VMEM, VMEM],
        out_specs=ANY,
        scratch_shapes=[pltpu.VMEM((rows, clusters), f32), pltpu.SemaphoreType.DMA((8,))],
        compiler_params=params(8),
        name="last",
    )(on_chip(logits), on_chip(masses), cluster_mass.reshape(1, clusters))


def solution(mesh):
    return jax.shard_map(
        local,
        mesh=mesh,
        in_specs=(
            P(("groups", "rows", "sub"), None),
            P(("groups", "rows", "sub"), None, None, None),
            P(("groups", "rows", "sub"), None),
            P("groups", None),
            P("groups"),
        ),
        out_specs=P(("groups", "rows", "sub"), None),
        check_vma=False,
    )
```
